32 devices in a mesh: dp: 8 (over z, y), seq: 4 (over x, core).
Axes of the slice: x: 2, y: 2, z: 4, core: 2. Of those that a mesh axis runs over, the one named last changes fastest.
Arguments:
- hidden_in: bfloat16 [32, 1024, 768], P('dp', 'seq'), may hold values from -6 to 6
- time_table: bfloat16 [1024, 128], replicated, may hold values from -6 to 6
- time_step: int32 [32], P('dp'), may hold values from 0 to 1023
- token_pos: int32 [32, 1024], P('dp', 'seq'), may hold values from 0 to 3071, as said below
- heads_weight: bfloat16 [768, 2304], P('seq'), may hold values from -0.15625 to 0.15625
- merge_weight: bfloat16 [768, 768], P('seq'), may hold values from -1.75 to 1.75
- lift_weight: bfloat16 [768, 3072], P('seq'), may hold values from -0.21875 to 0.21875
- lift_bias: bfloat16 [3072], P('seq'), may hold values from -3 to 3
- drop_weight: bfloat16 [3072, 768], P('seq'), may hold values from -0.109375 to 0.109375
- drop_bias: bfloat16 [768], P('seq'), may hold values from -3 to 3
- modulate_weight: bfloat16 [4608, 128], P('seq'), may hold values from -0.5 to 0.5
- modulate_bias: bfloat16 [4608], P('seq'), may hold values from -3 to 3
- first_gain: bfloat16 [768], P('seq'), may hold values from 0.099609375 to 1.8984375
- second_gain: bfloat16 [768], P('seq'), may hold values from 0.099609375 to 1.8984375
- out_grad: bfloat16 [32, 1024, 768], P('dp', 'seq'), may hold values from -6 to 6
Outputs:
- block_out: bfloat16 [32, 1024, 768], P('dp', 'seq')
- input_grad: bfloat16 [32, 1024, 768], P('dp', 'seq')
- heads_grad: float32 [768, 2304], P('seq')
- merge_grad: float32 [768, 768], P('seq')
- lift_grad: float32 [768, 3072], P('seq')
- liftbias_grad: float32 [3072], P('seq')
- drop_grad: float32 [3072, 768], P('seq')
- dropbias_grad: float32 [768], P('seq')
- modulate_grad: float32 [4608, 128], P('seq')
- modulatebias_grad: float32 [4608], P('seq')
- firstgain_grad: float32 [768], P('seq')
- secondgain_grad: float32 [768], P('seq')
- table_grad: float32 [1024, 128], P('seq')
The draws below stay inside these ranges and needn't reach their ends.
Inputs may be any that keep to these rules, and one draw needn't show every extreme that they name: `token_pos`: positions count up by one along a row and start again at 0 at each separator token; in every aligned group of 4 rows one row holds no separator; such a row in the first group starts at 2048, such a row in the second group starts at 0.
All inputs are finite; a program needn't handle non-finite values.
Results may differ from the reference program's by a relative error of at most 0.017.
The reference program's roundings to bfloat16 on the way count: a program that leaves them out, or rounds other values in their place, can miss the bound.
Values may be sent and summed in bfloat16 or wider, within the bound.
No kernel may reach another device: no remote copies, remote signals or barrier semaphores. Data moves between devices by JAX's collectives and lax.ppermute only.
A program may use at most 320 MiB of HBM per device.

```python
import math
import jax
import jax.numpy as jnp
from jax import lax

D = 768
HEADS = 12
HD = 64
FF = 3072
CD = 128
NT = 1024
L = 1024
B = 32


def draw_token_pos(key, part):
    key_marks = jax.random.fold_in(key, 11)
    key_start = jax.random.fold_in(key, 12)
    key_whole = jax.random.fold_in(key, 13)
    marks = jax.random.randint(key_marks, (B, L), 0, 64) == 0
    picked = jax.random.randint(key_whole, (), 0, 4)
    row_index = jnp.arange(B, dtype=jnp.int32)
    whole_row = row_index % 4 == picked
    marks = jnp.logical_and(marks, jnp.logical_not(whole_row[:, None]))
    start = jax.random.randint(key_start, (B,), 0, 2048)
    start = jnp.where(row_index == picked, 2048, start)
    start = jnp.where(row_index == picked + 4, 0, start)
    start = start[:, None]
    index = jnp.arange(L, dtype=jnp.int32)[None, :]
    latest = lax.cummax(jnp.where(marks, index, -1), axis=1)
    return jnp.where(latest < 0, start + index, index - latest).astype(jnp.int32)


def with_ends(values, own_key, least, top_value):
    index_at = [jax.random.randint(jax.random.fold_in(own_key, axis), (), 0, length) for axis, length in enumerate(values.shape)]
    longest = values.shape.index(max(values.shape))
    beside = index_at[:longest] + [(index_at[longest] + 1) % values.shape[longest]] + index_at[longest + 1:]
    return values.at[tuple(index_at)].set(least).at[tuple(beside)].set(top_value)


def level_of(own_key, dims, cuts, low, high):
    level = 1.0
    for axis_at, blocks in cuts:
        heights = jax.random.uniform(jax.random.fold_in(jax.random.fold_in(own_key, 6), axis_at), (blocks,), jnp.float32, low / len(cuts), high / len(cuts))
        level = level * jnp.repeat(jnp.exp(heights), dims[axis_at] // blocks).reshape((-1,) + (1,) * (len(dims) - 1 - axis_at))
    return level


def bell_draw(rng, shape, scale, limit, cuts=(), held_as=jnp.bfloat16):
    loudness = level_of(rng, shape, cuts, -0.22, 0.18) if cuts else 1.0
    array = jax.random.normal(rng, shape, jnp.float32) * scale * loudness
    return jnp.minimum(jnp.maximum(array, -limit), limit).astype(held_as)


def setup_inputs(seed: int = 0) -> dict:
    arg_keys = jax.random.split(jax.random.key(seed), 16)
    hidden_in = bell_draw(arg_keys[0], (B, L, D), 1.0, 6.0, ((0, 8), (1, 4)))
    time_table = bell_draw(arg_keys[1], (NT, CD), 1.0, 6.0)
    time_step = with_ends(jax.random.randint(arg_keys[2], (B,), 0, NT), jax.random.fold_in(arg_keys[2], 1), 0, NT - 1).astype(jnp.int32)
    token_pos = draw_token_pos(jax.random.fold_in(arg_keys[15], 71), 0)
    heads_weight = bell_draw(arg_keys[4], (D, 3 * D), (2 * D) ** -0.5, 0.15625, ((0, 4),))
    merge_weight = bell_draw(arg_keys[5], (D, D), (D // 64) ** -0.5, 1.75, ((0, 4),))
    lift_weight = bell_draw(arg_keys[6], (D, FF), D ** -0.5, 0.21875, ((0, 4),))
    lift_bias = bell_draw(arg_keys[7], (FF,), 0.5, 3.0, ((0, 4),))
    drop_weight = bell_draw(arg_keys[8], (FF, D), FF ** -0.5, 0.109375, ((0, 4),))
    drop_bias = bell_draw(arg_keys[9], (D,), 0.5, 3.0, ((0, 4),))
    modulate_weight = bell_draw(arg_keys[10], (6 * D, CD), CD ** -0.5, 0.5, ((0, 4),))
    modulate_bias = bell_draw(arg_keys[11], (6 * D,), 0.5, 3.0, ((0, 4),))
    first_gain = jnp.clip(1.0 + 0.18 * jax.random.normal(arg_keys[12], (D,), jnp.float32), 0.099609375, 1.8984375).astype(jnp.bfloat16)
    second_gain = jnp.clip(1.0 + 0.18 * jax.random.normal(arg_keys[13], (D,), jnp.float32), 0.099609375, 1.8984375).astype(jnp.bfloat16)
    out_grad = bell_draw(arg_keys[14], (B, L, D), 1.0, 6.0, ((0, 8), (1, 4)))
    return dict(hidden_in=hidden_in, time_table=time_table, time_step=time_step, token_pos=token_pos, heads_weight=heads_weight, merge_weight=merge_weight, lift_weight=lift_weight, lift_bias=lift_bias, drop_weight=drop_weight, drop_bias=drop_bias, modulate_weight=modulate_weight, modulate_bias=modulate_bias, first_gain=first_gain, second_gain=second_gain, out_grad=out_grad)


@jax.custom_vjp
def low(v):
    return lax.optimization_barrier(v.astype(jnp.bfloat16)).astype(jnp.float32)

@jax.custom_vjp
def low_back(v):
    return v

def low_keep(v):
    return (low(v), None)

def low_pass(kept, grad):
    return (grad,)

def back_keep(v):
    return (v, None)

def back_low(kept, grad):
    return (low(grad),)
low.defvjp(low_keep, low_pass)
low_back.defvjp(back_keep, back_low)
EPSILON = 1e-05

def precise(form, left, right):
    return jnp.einsum(form, left, right, precision=lax.Precision.HIGHEST)

def layer_norm(values, gain):
    center = values - lax.optimization_barrier(jnp.mean(values, axis=-1, keepdims=True))
    spread = lax.optimization_barrier(jnp.mean(center * center, axis=-1, keepdims=True))
    return center * lax.rsqrt(spread + EPSILON) * gain

def rotate_half(values):
    middle = values.shape[-1] // 2
    return jnp.concatenate([-values[..., middle:], values[..., :middle]], axis=-1)

def rotate(values, cosine, sine):
    return values * cosine + rotate_half(values) * sine

def rotary_tables(positions):
    freqs = 10000.0 ** (-jnp.arange(0, HD, 2, dtype=jnp.float32) / HD)
    angles = positions[..., None] * freqs
    angles = jnp.concatenate([angles, angles], axis=-1)
    return (jnp.cos(angles), jnp.sin(angles))

def block_forward(params, inputs, conds, cosine, sine):
    w_heads, w_merge, w_lift, b_lift, w_drop, b_drop, w_mod, b_mod, gain_one, gain_two = params
    groups = inputs.shape[0]
    modulation = precise('gc,mc->gm', conds, w_mod) + b_mod
    pieces = [piece[:, None, :] for piece in jnp.split(modulation, 6, axis=-1)]
    shift_a, scale_a, gate_a, shift_b, scale_b, gate_b = pieces
    adapted_a = low(layer_norm(inputs, gain_one) * (1.0 + scale_a) + shift_a)
    projected = low_back(precise('gld,de->gle', adapted_a, w_heads))
    query_raw, key_raw, value_raw = jnp.split(projected, 3, axis=-1)
    layout = (groups, L, HEADS, HD)
    query = low(rotate(query_raw.reshape(layout), cosine, sine))
    keys = low(rotate(key_raw.reshape(layout), cosine, sine))
    values = low(value_raw.reshape(layout))
    scores = low_back(precise('glhd,gmhd->ghlm', query, keys) * (1.0 / math.sqrt(HD)))
    probs = low(jax.nn.softmax(scores, axis=-1))
    mixed = precise('ghlm,gmhd->glhd', probs, values).reshape(groups, L, D)
    mixed = low(low_back(mixed))
    branch = low_back(precise('gld,de->gle', mixed, w_merge))
    middle = inputs + gate_a * branch
    adapted_b = low(layer_norm(middle, gain_two) * (1.0 + scale_b) + shift_b)
    upper = low_back(precise('gld,df->glf', adapted_b, w_lift) + b_lift)
    active = low(jax.nn.gelu(upper, approximate=True))
    lowered = low_back(precise('glf,fd->gld', active, w_drop) + b_drop)
    return middle + gate_b * lowered

def reference(hidden_in, time_table, time_step, token_pos, heads_weight, merge_weight, lift_weight, lift_bias, drop_weight, drop_bias, modulate_weight, modulate_bias, first_gain, second_gain, out_grad):
    params = tuple((weight.astype(jnp.float32) for weight in (heads_weight, merge_weight, lift_weight, lift_bias, drop_weight, drop_bias, modulate_weight, modulate_bias, first_gain, second_gain)))
    table = time_table.astype(jnp.float32)
    batch = hidden_in.shape[0]
    group = 4
    count = batch // group
    inputs = hidden_in.astype(jnp.float32).reshape(count, group, L, D)
    upstream = out_grad.astype(jnp.float32).reshape(count, group, L, D)
    steps_all = time_step.reshape(count, group)
    places_all = token_pos.reshape(count, group, L)

    def one_block(totals, block):
        inputs_b, upstream_b, steps_b, places_b = block
        positions = places_b.astype(jnp.float32)
        cosine, sine = rotary_tables(positions)
        cosine = cosine[:, :, None, :]
        sine = sine[:, :, None, :]

        def forward(params_all, table_all, inputs_all):
            conds = table_all[steps_b]
            return block_forward(params_all, inputs_all, conds, cosine, sine)
        output, pullback = jax.vjp(forward, params, table, inputs_b)
        params_grad, table_grad, inputs_grad = pullback(upstream_b)
        totals = jax.tree.map(jnp.add, totals, (params_grad, table_grad))
        return (totals, (output.astype(jnp.bfloat16), inputs_grad.astype(jnp.bfloat16)))
    zeros = jax.tree.map(jnp.zeros_like, (params, table))
    totals, (outputs, input_grads) = lax.scan(one_block, zeros, (inputs, upstream, steps_all, places_all))
    params_grad, table_grad = totals
    block_out = outputs.reshape(batch, L, D)
    input_grad = input_grads.reshape(batch, L, D)
    return (block_out, input_grad, params_grad[0], params_grad[1], params_grad[2], params_grad[3], params_grad[4], params_grad[5], params_grad[6], params_grad[7], params_grad[8], params_grad[9], table_grad)
```

```python
from functools import partial
import math

import jax
import jax.numpy as jnp
from jax import lax
from jax.experimental import pallas as pl
from jax.experimental.pallas import tpu as pltpu
from jax.sharding import PartitionSpec as P

HEADS = 12
EPSILON = 1e-05
LANES = 128
VMEM = 60 * 1024 * 1024
LOW = jnp.bfloat16
FULL = jnp.float32


def matmul(left, right, left_dim=1, right_dim=0):
    dims = (((left_dim,), (right_dim,)), ((), ()))
    return lax.dot_general(left, right, dims, preferred_element_type=FULL)


def call(body, name, grid, in_specs, out_specs, out_shape, scratch, flops, args, moved):
    return pl.pallas_call(
        body,
        name=name,
        grid_spec=pltpu.PrefetchScalarGridSpec(
            num_scalar_prefetch=1,
            grid=grid,
            in_specs=in_specs,
            out_specs=out_specs,
            scratch_shapes=scratch,
        ),
        out_shape=out_shape,
        compiler_params=pltpu.CompilerParams(
            dimension_semantics=("arbitrary",) * len(grid), vmem_limit_bytes=VMEM
        ),
        cost_estimate=pl.CostEstimate(flops=flops, bytes_accessed=moved, transcendentals=0),
    )(*args)


def whole(shape):
    zeros = (0,) * len(shape)
    return pl.BlockSpec(shape, lambda *_: zeros, pipeline_mode=pl.Buffered(1))


def kept(shape):
    zeros = (0,) * len(shape)
    return pl.BlockSpec(shape, lambda *_: zeros)


def assemble(me, target, pieces):
    rows = pieces[0].shape[0]
    for d, piece in enumerate(pieces):
        at = pl.multiple_of((me ^ d) * rows, 16)
        target[pl.ds(at, rows), :] = piece[...]


def split_rows(me, value, keep, send):
    rows = value.shape[0] // 4
    mine_x, mine_c = me >> 1, me & 1
    for j in range(4):
        part = value[j * rows : (j + 1) * rows].astype(LOW)[None]
        at = (j >> 1) ^ mine_x

        @pl.when(mine_c == (j & 1))
        def _(part=part, at=at):
            keep[pl.ds(at, 1)] = part

        @pl.when(mine_c != (j & 1))
        def _(part=part, at=at):
            send[pl.ds(at, 1)] = part


def normalize(values):
    center = values - jnp.mean(values, axis=-1, keepdims=True)
    inverse = lax.rsqrt(jnp.mean(center * center, axis=-1, keepdims=True) + EPSILON)
    return center * inverse, inverse


def unnormalize(weighted, unit, inverse):
    first = jnp.mean(weighted, axis=-1, keepdims=True)
    second = jnp.mean(weighted * unit, axis=-1, keepdims=True)
    return inverse * (weighted - first - unit * second)


def lower_half(head):
    lane = lax.broadcasted_iota(jnp.int32, (1, LANES), 1)
    return (lane & (head - 1)) < head // 2


def column_sum(values):
    return jnp.sum(values, axis=0, keepdims=True)


def project_kernel(head, me_ref, hidden, vectors, p0, p1, p2, p3, cosine, sine, adapted, query, key, value, weight):
    @pl.when(pl.program_id(0) == 0)
    def _():
        assemble(me_ref[0], weight, (p0, p1, p2, p3))

    unit, _ = normalize(hidden[...].astype(FULL))
    low = (unit * vectors[0:1, :] * vectors[1:2, :] + vectors[2:3, :]).astype(LOW)
    adapted[...] = low
    width = low.shape[1]
    cos, sin = cosine[...], sine[...]
    under = lower_half(head)
    signed = jnp.where(under, -sin, sin)
    scale = 1.0 / math.sqrt(head)
    for which, target in enumerate((query, key)):
        part = matmul(low, weight[:, which * width : (which + 1) * width])
        for j in range(width // LANES):
            block = part[:, j * LANES : (j + 1) * LANES]
            turned = jnp.where(
                under,
                pltpu.roll(block, LANES - head // 2, 1),
                pltpu.roll(block, head // 2, 1),
            )
            turned = (block * cos + turned * signed).astype(LOW)
            if which == 0:
                turned = turned * jnp.asarray(scale, LOW)
            target[:, j * LANES : (j + 1) * LANES] = turned
    value[...] = matmul(low, weight[:, 2 * width :]).astype(LOW)


def project(me, hidden, vectors, pieces, cosine, sine, head):
    length, width = hidden.shape
    step = 256
    rows = pl.BlockSpec((step, width), lambda i, _: (i, 0))
    angle = pl.BlockSpec((step, LANES), lambda i, _: (i, 0))
    out = jax.ShapeDtypeStruct((length, width), LOW)
    return call(
        partial(project_kernel, head),
        "project",
        (length // step,),
        [rows, whole(vectors.shape)] + [whole(p.shape) for p in pieces] + [angle, angle],
        [rows] * 4,
        [out] * 4,
        [pltpu.VMEM((width, 3 * width), LOW)],
        2 * length * width * 3 * width,
        (me, hidden, vectors, *pieces, cosine, sine),
        2 * length * width * 8,
    )


def attend_kernel(step, head, me_ref, query, key, value, mixed, logsum):
    lane = lax.broadcasted_iota(jnp.int32, (1, LANES), 1)
    first = lane < head
    keys, values = key[...], value[...]
    zero = jnp.zeros_like(keys)
    split = (jnp.where(first, keys, zero), jnp.where(first, zero, keys))
    for i in range(query.shape[0] // step):
        at = slice(i * step, (i + 1) * step)
        block = query[at, :]
        outs, sums = [], []
        for h in range(2):
            scores = matmul(block, split[h], 1, 1)
            peak = jnp.max(scores, axis=1, keepdims=True)
            expos = jnp.exp(scores - peak)
            total = jnp.sum(expos, axis=1, keepdims=True)
            outs.append(matmul(expos.astype(LOW), values) * (1.0 / total))
            sums.append(peak + jnp.log(total))
        mixed[at, :] = jnp.where(first, outs[0], outs[1]).astype(LOW)
        turned = jnp.where(first, sums[0], sums[1]).T
        logsum[0, 0:1, at] = turned[0:1, :]
        logsum[0, 1:2, at] = turned[head : head + 1, :]


def attend(me, query, key, value, head):
    length, width = query.shape
    pairs = width // LANES
    block = pl.BlockSpec((length, LANES), lambda i, _: (0, i))
    return call(
        partial(attend_kernel, 512, head),
        "attend",
        (pairs,),
        [block] * 3,
        [block, pl.BlockSpec((1, 2, length), lambda i, _: (i, 0, 0))],
        [
            jax.ShapeDtypeStruct((length, width), LOW),
            jax.ShapeDtypeStruct((pairs, 2, length), FULL),
        ],
        [],
        16 * length * length * width,
        (me, query, key, value),
        2 * length * width * 4,
    )


def merge_kernel(me_ref, mixed, hidden, vectors, p0, p1, p2, p3, middle, adapted, weight):
    @pl.when(pl.program_id(0) == 0)
    def _():
        assemble(me_ref[0], weight, (p0, p1, p2, p3))

    branch = matmul(mixed[...], weight[...])
    mid = hidden[...].astype(FULL) + vectors[0:1, :] * branch
    middle[...] = mid
    unit, _ = normalize(mid)
    adapted[...] = (unit * vectors[1:2, :] * vectors[2:3, :] + vectors[3:4, :]).astype(LOW)


def merge(me, mixed, hidden, vectors, pieces):
    length, width = hidden.shape
    step = 256
    rows = pl.BlockSpec((step, width), lambda i, _: (i, 0))
    return call(
        merge_kernel,
        "merge",
        (length // step,),
        [rows, rows, whole(vectors.shape)] + [whole(p.shape) for p in pieces],
        [rows, rows],
        [jax.ShapeDtypeStruct((length, width), FULL), jax.ShapeDtypeStruct((length, width), LOW)],
        [pltpu.VMEM((width, width), LOW)],
        2 * length * width * width,
        (me, mixed, hidden, vectors, *pieces),
        2 * length * width * 6,
    )


ORDER = (1, 3, 0, 2)


def feed_kernel(
    subs, me_ref, adapted, upstream, middle, vectors, lift_bias, l0, l1, l2, l3, d0, d1, d2, d3,
    block_out, adapted_grad, sums, liftbias_grad, lift_keep, lift_send, drop_keep, drop_send,
    lift, drop, turned, lowered_grad, lowered,
):
    i = pl.program_id(0)
    me = me_ref[0]
    gate = vectors[0:1, :]

    @pl.when(i == 0)
    def _():
        turned[...] = adapted[...].T
        lowered_grad[...] = (gate * upstream[...].astype(FULL)).astype(LOW)
        lowered[...] = jnp.zeros_like(lowered)
        adapted_grad[...] = jnp.zeros_like(adapted_grad)

    assemble(me, lift, (l0, l1, l2, l3))
    for at, d in enumerate(ORDER):

        @pl.when(i // subs == at)
        def _(d=d):
            drop[...] = (d0, d1, d2, d3)[d][...]

    weight_up, weight_down = lift[...], drop[...]
    upper = matmul(adapted[...], weight_up) + lift_bias[...]
    square = upper * upper
    root = math.sqrt(2.0 / math.pi)
    bent = jnp.tanh(upper * (root + root * 0.044715 * square))
    half = 0.5 + 0.5 * bent
    slope = half + upper * (0.5 - 0.5 * bent * bent) * (root + 3.0 * root * 0.044715 * square)
    active = (upper * half).astype(LOW)
    lowered[...] += matmul(active, weight_down)
    down = lowered_grad[...]
    upper_grad = (matmul(down, weight_down, 1, 1) * slope).astype(LOW)
    adapted_grad[...] += matmul(upper_grad, weight_up, 1, 1)
    liftbias_grad[...] = column_sum(upper_grad.astype(FULL))
    drop_grad = matmul(active, down, 0, 0).astype(LOW)[None]

    @pl.when(i < 2 * subs)
    def _():
        drop_send[...] = drop_grad

    @pl.when(i >= 2 * subs)
    def _():
        drop_keep[...] = drop_grad

    split_rows(me, matmul(turned[...], upper_grad), lift_keep, lift_send)

    @pl.when(i == 4 * subs - 1)
    def _():
        total = lowered[...] + vectors[1:2, :]
        block_out[...] = (middle[...] + gate * total).astype(LOW)
        sums[0:1, :] = column_sum(upstream[...].astype(FULL) * total)
        sums[1:2, :] = column_sum(lowered_grad[...].astype(FULL))


def feed(me, adapted, upstream, middle, vectors, lift_bias, lifts, drops):
    length, width = adapted.shape
    piece = drops[0].shape[0]
    units = 4 * piece
    step = 384
    subs = piece // step

    def order(i):
        k = i // subs
        return jnp.where(k == 0, 1, jnp.where(k == 1, 3, jnp.where(k == 2, 0, 2)))

    def column(i, me_ref):
        return (me_ref[0] ^ order(i)) * subs + i % subs

    def own(d):
        at = ORDER.index(d)
        return pl.BlockSpec((step, width), lambda i, _: (jnp.clip(i - at * subs, 0, subs - 1), 0))

    strip = pl.BlockSpec((1, step), lambda i, m: (0, column(i, m)))
    lift_spec = pl.BlockSpec((width // 4, step), lambda i, m: (0, column(i, m)))
    quarter = pl.BlockSpec((2, width // 4, step), lambda i, m: (0, 0, column(i, m)))

    def send_at(i, _):
        j = jnp.minimum(i, 2 * subs - 1)
        return (j // subs, j % subs, 0)

    def keep_at(i, _):
        j = jnp.maximum(i - 2 * subs, 0)
        return (j // subs, j % subs, 0)

    low = jax.ShapeDtypeStruct((length, width), LOW)
    return call(
        partial(feed_kernel, subs),
        "feed",
        (4 * subs,),
        [whole(adapted.shape), whole(adapted.shape), whole(adapted.shape), whole(vectors.shape), strip]
        + [lift_spec] * 4
        + [own(d) for d in range(4)],
        [
            kept((length, width)),
            kept((length, width)),
            kept((8, width)),
            strip,
            quarter,
            quarter,
            pl.BlockSpec((1, step, width), keep_at),
            pl.BlockSpec((1, step, width), send_at),
        ],
        [
            low,
            jax.ShapeDtypeStruct((length, width), FULL),
            jax.ShapeDtypeStruct((8, width), FULL),
            jax.ShapeDtypeStruct((1, units), FULL),
            jax.ShapeDtypeStruct((2, width // 4, units), LOW),
            jax.ShapeDtypeStruct((2, width // 4, units), LOW),
            jax.ShapeDtypeStruct((2, piece, width), LOW),
            jax.ShapeDtypeStruct((2, piece, width), LOW),
        ],
        [
            pltpu.VMEM((width, step), LOW),
            pltpu.VMEM((step, width), LOW),
            pltpu.VMEM((width, length), LOW),
            pltpu.VMEM((length, width), LOW),
            pltpu.VMEM((length, width), FULL),
        ],
        12 * length * width * units,
        (me, adapted, upstream, middle, vectors, lift_bias, *lifts, *drops),
        8 * width * units + 24 * length * width,
    )


def unmerge_kernel(
    me_ref, adapted_grad, middle, upstream, mixed, vectors, p0, p1, p2, p3,
    middle_grad, mixed_grad, sums, keep, send, weight, total,
):
    i = pl.program_id(0)

    @pl.when(i == 0)
    def _():
        assemble(me_ref[0], weight, (p0, p1, p2, p3))
        total[...] = jnp.zeros_like(total)
        sums[...] = jnp.zeros_like(sums)

    gate, gain, grow = vectors[0:1, :], vectors[1:2, :], vectors[2:3, :]
    unit, inverse = normalize(middle[...])
    grad = adapted_grad[...]
    sums[0:1, :] += column_sum(grad)
    sums[1:2, :] += column_sum(grad * (unit * gain))
    normed_grad = grad * grow
    sums[2:3, :] += column_sum(normed_grad * unit)
    mid_grad = upstream[...].astype(FULL) + unnormalize(normed_grad * gain, unit, inverse)
    middle_grad[...] = mid_grad
    low = mixed[...]
    sums[3:4, :] += column_sum(mid_grad * matmul(low, weight[...]))
    branch_grad = (gate * mid_grad).astype(LOW)
    total[...] += matmul(low, branch_grad, 0, 0)
    mixed_grad[...] = matmul(branch_grad, weight[...], 1, 1).astype(LOW)

    @pl.when(i == pl.num_programs(0) - 1)
    def _():
        split_rows(me_ref[0], total[...], keep, send)


def unmerge(me, adapted_grad, middle, upstream, mixed, vectors, pieces):
    length, width = mixed.shape
    step = 256
    rows = pl.BlockSpec((step, width), lambda i, _: (i, 0))
    part = (2, width // 4, width)
    return call(
        unmerge_kernel,
        "unmerge",
        (length // step,),
        [rows] * 4 + [whole(vectors.shape)] + [whole(p.shape) for p in pieces],
        [rows, rows, kept((8, width)), kept(part), kept(part)],
        [
            jax.ShapeDtypeStruct((length, width), FULL),
            jax.ShapeDtypeStruct((length, width), LOW),
            jax.ShapeDtypeStruct((8, width), FULL),
            jax.ShapeDtypeStruct(part, LOW),
            jax.ShapeDtypeStruct(part, LOW),
        ],
        [pltpu.VMEM((width, width), LOW), pltpu.VMEM((width, width), FULL)],
        6 * length * width * width,
        (me, adapted_grad, middle, upstream, mixed, vectors, *pieces),
        2 * length * width * 12,
    )


def unattend_kernel(step, head, me_ref, query, key, value, mixed, mixed_grad, logsum, cosine, sine, grads, query_sum, key_sum, value_sum):
    lane = lax.broadcasted_iota(jnp.int32, (1, LANES), 1)
    first = lane < head
    keys, values = key[...], value[...]
    zero = jnp.zeros_like(keys)
    keys_h = (jnp.where(first, keys, zero), jnp.where(first, zero, keys))
    values_h = (jnp.where(first, values, zero), jnp.where(first, zero, values))
    turned = keys.T
    scale = 1.0 / math.sqrt(head)
    for i in range(query.shape[0] // step):
        at = slice(i * step, (i + 1) * step)
        block, grad = query[at, :], mixed_grad[at, :]
        product = (grad.astype(FULL) * mixed[at, :].astype(FULL)).T
        queries, values_new, keys_new = [], [], []
        for h in range(2):
            center = jnp.sum(product[h * head : (h + 1) * head], axis=0, keepdims=True)
            probs = jnp.exp(matmul(keys_h[h], block, 1, 1) - logsum[0, h : h + 1, at])
            probs_grad = matmul(values_h[h], grad, 1, 1)
            scores_grad = (probs * (probs_grad - center)).astype(LOW)
            values_new.append(matmul(probs.astype(LOW), grad))
            keys_new.append(matmul(scores_grad, block))
            queries.append(matmul(turned[h * head : (h + 1) * head], scores_grad))
        query_sum[at, :] = jnp.concatenate(queries, axis=0).T * scale
        key_part = jnp.where(first, keys_new[0], keys_new[1])
        value_part = jnp.where(first, values_new[0], values_new[1])
        if i == 0:
            key_sum[...] = key_part
            value_sum[...] = value_part
        else:
            key_sum[...] += key_part
            value_sum[...] += value_part
    under = lower_half(head)
    cos, sin = cosine[...], sine[...]
    for which, total in enumerate((query_sum, key_sum)):
        rotated = total[...]
        swept = rotated * sin
        back = jnp.where(
            under, pltpu.roll(swept, LANES - head // 2, 1), -pltpu.roll(swept, head // 2, 1)
        )
        grads[which] = (rotated * cos + back).astype(LOW)
    grads[2] = value_sum[...].astype(LOW)


def unattend(me, query, key, value, mixed, mixed_grad, logsum, cosine, sine, head):
    length, width = query.shape
    pairs = width // LANES
    block = pl.BlockSpec((length, LANES), lambda i, _: (0, i))
    return call(
        partial(unattend_kernel, 256, head),
        "unattend",
        (pairs,),
        [block] * 5
        + [pl.BlockSpec((1, 2, length), lambda i, _: (i, 0, 0))]
        + [whole((length, LANES))] * 2,
        [pl.BlockSpec((3, length, LANES), lambda i, _: (0, 0, i))],
        [jax.ShapeDtypeStruct((3, length, width), LOW)],
        [pltpu.VMEM((length, LANES), FULL)] * 3,
        40 * length * length * width,
        (me, query, key, value, mixed, mixed_grad, logsum, cosine, sine),
        2 * length * width * 8,
    )[0]


def weigh_kernel(me_ref, adapted, grads, keep, send, turned):
    @pl.when(pl.program_id(0) == 0)
    def _():
        turned[...] = adapted[...].T

    split_rows(me_ref[0], matmul(turned[...], grads[0]), keep, send)


def weigh(me, adapted, grads):
    length, width = adapted.shape
    step = 384
    subs = width // step
    part = pl.BlockSpec((2, width // 4, step), lambda i, _: (0, 0, i))
    shape = jax.ShapeDtypeStruct((2, width // 4, 3 * width), LOW)
    return call(
        weigh_kernel,
        "weigh",
        (3 * subs,),
        [whole(adapted.shape), pl.BlockSpec((1, length, step), lambda i, _: (i // subs, 0, i % subs))],
        [part, part],
        [shape, shape],
        [pltpu.VMEM((width, length), LOW)],
        6 * length * width * width,
        (me, adapted, grads),
        2 * length * width * 7,
    )


def unproject_kernel(me_ref, grads, hidden, middle_grad, vectors, p0, p1, p2, p3, input_grad, sums, weight):
    i = pl.program_id(0)

    @pl.when(i == 0)
    def _():
        assemble(me_ref[0], weight, (p0, p1, p2, p3))
        sums[...] = jnp.zeros_like(sums)

    gain, grow = vectors[0:1, :], vectors[1:2, :]
    width = hidden.shape[1]
    grad = matmul(grads[0], weight[:, :width], 1, 1)
    grad += matmul(grads[1], weight[:, width : 2 * width], 1, 1)
    grad += matmul(grads[2], weight[:, 2 * width :], 1, 1)
    unit, inverse = normalize(hidden[...].astype(FULL))
    sums[0:1, :] += column_sum(grad)
    sums[1:2, :] += column_sum(grad * (unit * gain))
    normed_grad = grad * grow
    sums[2:3, :] += column_sum(normed_grad * unit)
    input_grad[...] = (middle_grad[...] + unnormalize(normed_grad * gain, unit, inverse)).astype(LOW)


def unproject(me, grads, hidden, middle_grad, vectors, pieces):
    length, width = hidden.shape
    step = 256
    rows = pl.BlockSpec((step, width), lambda i, _: (i, 0))
    return call(
        unproject_kernel,
        "unproject",
        (length // step,),
        [pl.BlockSpec((3, step, width), lambda i, _: (0, i, 0)), rows, rows, whole(vectors.shape)]
        + [whole(p.shape) for p in pieces],
        [rows, kept((8, width))],
        [jax.ShapeDtypeStruct((length, width), LOW), jax.ShapeDtypeStruct((8, width), FULL)],
        [pltpu.VMEM((width, 3 * width), LOW)],
        6 * length * width * width,
        (me, grads, hidden, middle_grad, vectors, *pieces),
        2 * length * width * 10,
    )


def swap(array, axis, distance):
    size = lax.axis_size(axis)
    return lax.ppermute(array, axis, [(i, i ^ distance) for i in range(size)])


def gather_pieces(weight):
    across = swap(weight, "seq", 2)
    return (weight, swap(weight, "seq", 1), across, swap(across, "seq", 1))


def stages(size):
    out = [2] if size > 1 else []
    size //= 2
    while size > 1:
        factor = 4 if size % 4 == 0 else 2
        out.append(factor)
        size //= factor
    return out


def reduce_over_rows(keep, send):
    term = keep.astype(FULL) + swap(send, "seq", 1).astype(FULL)
    term = term[0] + swap(term[1].astype(LOW), "seq", 2).astype(FULL)
    size = lax.axis_size("dp")
    place = lax.axis_index("dp")
    stride = 1
    plan = []
    for factor in stages(size):
        plan.append((factor, stride))
        columns = term.shape[-1]
        parts = term.reshape(factor, -1, columns)
        at = (place // stride) % factor
        if factor == 2:
            mine = lax.dynamic_index_in_dim(parts, at, 0, keepdims=False)
            other = lax.dynamic_index_in_dim(parts, 1 - at, 0, keepdims=False)
            term = mine + swap(other.astype(LOW), "dp", stride).astype(FULL)
        else:
            groups = [
                [base + stride * k for k in range(factor)]
                for base in range(size)
                if (base // stride) % factor == 0
            ]
            parts = lax.all_to_all(
                parts.astype(LOW), "dp", 0, 0, axis_index_groups=groups, tiled=True
            )
            term = jnp.sum(parts.astype(FULL), axis=0)
        stride *= factor
    term = term.astype(LOW)
    for factor, stride in reversed(plan):
        at = (place // stride) % factor
        rows, columns = term.shape
        target = jnp.zeros((factor, rows, columns), LOW)
        for d in range(factor):
            part = swap(term, "dp", d * stride) if d else term
            target = lax.dynamic_update_index_in_dim(target, part, at ^ d, 0)
        term = target.reshape(factor * rows, columns)
    return term.astype(FULL)


def shards(
    hidden_in,
    time_table,
    time_step,
    token_pos,
    heads_weight,
    merge_weight,
    lift_weight,
    lift_bias,
    drop_weight,
    drop_bias,
    modulate_weight,
    modulate_bias,
    first_gain,
    second_gain,
    out_grad,
):
    count = lax.axis_size("seq")
    place = lax.axis_index("seq")
    seqs, span, width = hidden_in.shape
    assert count == 4 and seqs == count
    length = span * count
    head = width // HEADS
    me = place.astype(jnp.int32).reshape(1)

    hidden = lax.all_to_all(hidden_in, "seq", 0, 0, tiled=True).reshape(length, width)
    heads = gather_pieces(heads_weight)
    positions = lax.all_to_all(token_pos, "seq", 0, 0, tiled=True).reshape(length)
    merges = gather_pieces(merge_weight)
    lifts = gather_pieces(lift_weight)
    drops = gather_pieces(drop_weight)
    upstream = lax.all_to_all(out_grad, "seq", 0, 0, tiled=True).reshape(length, width)

    table_rows, depth = time_table.shape
    choose = (time_step[:, None] == jnp.arange(table_rows, dtype=jnp.int32)[None, :]).astype(LOW)
    conds = jnp.dot(choose, time_table, preferred_element_type=FULL)
    modulation = matmul(conds.astype(LOW), modulate_weight, 1, 1) + modulate_bias.astype(FULL)
    columns = modulation.shape[1]
    small = jnp.concatenate(
        [modulation.reshape(-1)]
        + [v.astype(FULL) for v in (lift_bias, drop_bias, first_gain, second_gain)]
    )
    small = lax.all_gather(small, "seq", axis=0)
    chosen = small[:, : seqs * columns].reshape(count, seqs, columns)
    chosen = lax.dynamic_index_in_dim(chosen, place, 1, keepdims=False).reshape(6, width)
    rest = small[:, seqs * columns :]
    sizes = (lift_bias.shape[0], drop_bias.shape[0], first_gain.shape[0], second_gain.shape[0])
    vectors, at = [], 0
    for size in sizes:
        vectors.append(rest[:, at : at + size].reshape(1, -1))
        at += size
    up_bias, down_bias, gain_one, gain_two = vectors
    shift_a, scale_a, gate_a, shift_b, scale_b, gate_b = [chosen[k : k + 1] for k in range(6)]
    grow_a, grow_b = 1.0 + scale_a, 1.0 + scale_b

    def rows(*items):
        blank = jnp.zeros((8 - len(items), width), FULL)
        return jnp.concatenate(items + (blank,), axis=0)

    freqs = 10000.0 ** (-jnp.arange(0, head, 2, dtype=FULL) / head)
    freqs = jnp.tile(freqs, 2 * LANES // head)
    angles = positions.astype(FULL)[:, None] * freqs
    cosine, sine = jnp.cos(angles), jnp.sin(angles)

    adapted_a, query, key, value = project(
        me, hidden, rows(gain_one, grow_a, shift_a), heads, cosine, sine, head
    )
    mixed, logsum = attend(me, query, key, value, head)
    middle, adapted_b = merge(me, mixed, hidden, rows(gate_a, gain_two, grow_b, shift_b), merges)
    block_out, adapted_b_grad, feed_sums, liftbias_grad, lift_keep, lift_send, drop_keep, drop_send = feed(
        me, adapted_b, upstream, middle, rows(gate_b, down_bias), up_bias, lifts, drops
    )
    block_out = lax.all_to_all(block_out.reshape(count, span, width), "seq", 0, 0, tiled=True)
    drop_grad = reduce_over_rows(drop_keep, drop_send)
    lift_grad = reduce_over_rows(lift_keep, lift_send)
    middle_grad, mixed_grad, merge_sums, merge_keep, merge_send = unmerge(
        me, adapted_b_grad, middle, upstream, mixed, rows(gate_a, gain_two, grow_b), merges
    )
    merge_grad = reduce_over_rows(merge_keep, merge_send)
    grads = unattend(me, query, key, value, mixed, mixed_grad, logsum, cosine, sine, head)
    heads_keep, heads_send = weigh(me, adapted_a, grads)
    heads_grad = reduce_over_rows(heads_keep, heads_send)
    input_grad, project_sums = unproject(
        me, grads, hidden, middle_grad, rows(gain_one, grow_a), heads
    )
    input_grad = lax.all_to_all(input_grad.reshape(count, span, width), "seq", 0, 0, tiled=True)

    modulation_grad = jnp.concatenate(
        [project_sums[0:2], merge_sums[3:4], merge_sums[0:2], feed_sums[0:1]], axis=0
    ).reshape(count, columns)
    pack = jnp.concatenate(
        [
            modulation_grad,
            liftbias_grad.reshape(count, -1),
            feed_sums[1].reshape(count, -1),
            project_sums[2].reshape(count, -1),
            merge_sums[2].reshape(count, -1),
        ],
        axis=1,
    )
    pack = lax.all_to_all(pack, "seq", 0, 0, tiled=True)
    pack = jnp.concatenate([pack[:, :columns].reshape(-1), jnp.sum(pack[:, columns:], axis=0)])
    pack = lax.all_gather(pack, "dp", axis=0)
    row_grads = pack[:, : seqs * columns].reshape(-1, columns)
    totals = jnp.sum(pack[:, seqs * columns :], axis=0)
    ends, at = [], 0
    for size in sizes:
        ends.append(totals[at : at + size])
        at += size
    liftbias_out, dropbias_out, firstgain_out, secondgain_out = ends
    steps = lax.all_gather(time_step, "dp", axis=0, tiled=True)
    picks = (steps[:, None] == jnp.arange(table_rows, dtype=jnp.int32)[None, :]).astype(LOW)
    all_conds = jnp.dot(picks, time_table, preferred_element_type=FULL)
    exact = lax.Precision.HIGHEST
    modulate_grad = jnp.einsum("sm,sc->mc", row_grads, all_conds, precision=exact)
    modulatebias_grad = jnp.sum(row_grads, axis=0)
    conds_grad = jnp.einsum(
        "sm,mc->sc", row_grads, modulate_weight.astype(FULL), precision=exact
    )
    conds_grad = lax.psum(conds_grad, "seq")
    share = table_rows // count
    own = (steps[None, :] == (place * share + jnp.arange(share, dtype=jnp.int32))[:, None])
    table_grad = jnp.dot(own.astype(FULL), conds_grad, precision=exact)
    return (
        block_out,
        input_grad,
        heads_grad,
        merge_grad,
        lift_grad,
        liftbias_out,
        drop_grad,
        dropbias_out,
        modulate_grad,
        modulatebias_grad,
        firstgain_out,
        secondgain_out,
        table_grad,
    )


def solution(mesh):
    return jax.shard_map(
        shards,
        mesh=mesh,
        in_specs=(
            P("dp", "seq", None),
            P(),
            P("dp"),
            P("dp", "seq"),
            P("seq", None),
            P("seq", None),
            P("seq", None),
            P("seq"),
            P("seq", None),
            P("seq"),
            P("seq", None),
            P("seq"),
            P("seq"),
            P("seq"),
            P("dp", "seq", None),
        ),
        out_specs=(
            P("dp", "seq", None),
            P("dp", "seq", None),
            P("seq", None),
            P("seq", None),
            P("seq", None),
            P("seq"),
            P("seq", None),
            P("seq"),
            P("seq", None),
            P("seq"),
            P("seq"),
            P("seq"),
            P("seq", None),
        ),
        check_vma=False,
    )
```

```python
from functools import partial
import math

import jax
import jax.numpy as jnp
from jax import lax
from jax.experimental import pallas as pl
from jax.experimental.pallas import tpu as pltpu
from jax.sharding import PartitionSpec as P

HEADS = 12
EPSILON = 1e-05
LANES = 128
VMEM = 60 * 1024 * 1024
LOW = jnp.bfloat16
FULL = jnp.float32


def matmul(left, right, left_dim=1, right_dim=0):
    dims = (((left_dim,), (right_dim,)), ((), ()))
    return lax.dot_general(left, right, dims, preferred_element_type=FULL)


def call(body, name, grid, in_specs, out_specs, out_shape, scratch, flops, args, moved):
    return pl.pallas_call(
        body,
        name=name,
        grid_spec=pltpu.PrefetchScalarGridSpec(
            num_scalar_prefetch=1,
            grid=grid,
            in_specs=in_specs,
            out_specs=out_specs,
            scratch_shapes=scratch,
        ),
        out_shape=out_shape,
        compiler_params=pltpu.CompilerParams(
            dimension_semantics=("arbitrary",) * len(grid), vmem_limit_bytes=VMEM
        ),
        cost_estimate=pl.CostEstimate(flops=1024, bytes_accessed=1024, transcendentals=0),
    )(*args)


def whole(shape):
    zeros = (0,) * len(shape)
    return pl.BlockSpec(shape, lambda *_: zeros, pipeline_mode=pl.Buffered(1))


def kept(shape):
    zeros = (0,) * len(shape)
    return pl.BlockSpec(shape, lambda *_: zeros)


def assemble(at, target, pieces):
    me, b = at[0], at[1]
    own, core, across, handed, core_across, core_handed = pieces
    rows = target.shape[0] // 8
    width = across.shape[-1]
    halves = (
        (me, 0, lambda cut: own[0, cut, :]),
        (me, 1, lambda cut: own[1, cut, :]),
        (me ^ 1, 0, lambda cut: core[0, cut, :]),
        (me ^ 1, 1, lambda cut: core[1, cut, :]),
        (me ^ 2, b, lambda cut: across[cut, :]),
        (me ^ 2, 1 - b, lambda cut: handed[cut, :]),
        (me ^ 3, b, lambda cut: core_across[cut, :]),
        (me ^ 3, 1 - b, lambda cut: core_handed[cut, :]),
    )
    for shard, half, read in halves:
        place = pl.ds(pl.multiple_of((2 * shard + half) * rows, 16), rows)
        for k in range(target.shape[1] // width):
            cut = slice(k * rows, (k + 1) * rows)
            target[place, k * width : (k + 1) * width] = read(cut)


def stack_halves(target, pack):
    rows = target.shape[0] // 8
    for j in range(4):
        for k in range(2):
            low = (2 * j + k) * rows
            target[low : low + rows, :] = pack[4 * k + j]


def merge_spec(pack, width):
    rows = width // 8
    at = pack.shape[1] // rows - 1
    return pl.BlockSpec((8, rows, width), lambda *_: (0, at, 0), pipeline_mode=pl.Buffered(1))


def split_rows(me, value, keep, send):
    rows = value.shape[0] // 4
    mine_x, mine_c = me >> 1, me & 1
    for j in range(4):
        part = value[j * rows : (j + 1) * rows].astype(LOW)[None]
        at = (j >> 1) ^ mine_x

        @pl.when(mine_c == (j & 1))
        def _(part=part, at=at):
            keep[pl.ds(at, 1)] = part

        @pl.when(mine_c != (j & 1))
        def _(part=part, at=at):
            send[pl.ds(at, 1)] = part


def normalize(values):
    center = values - jnp.mean(values, axis=-1, keepdims=True)
    inverse = lax.rsqrt(jnp.mean(center * center, axis=-1, keepdims=True) + EPSILON)
    return center * inverse, inverse


def unnormalize(weighted, unit, inverse):
    first = jnp.mean(weighted, axis=-1, keepdims=True)
    second = jnp.mean(weighted * unit, axis=-1, keepdims=True)
    return inverse * (weighted - first - unit * second)


def lower_half(head):
    lane = lax.broadcasted_iota(jnp.int32, (1, LANES), 1)
    return (lane & (head - 1)) < head // 2


def column_sum(values):
    return jnp.sum(values, axis=0, keepdims=True)


def project_kernel(head, me_ref, hidden, vectors, p0, p1, p2, p3, p4, p5, cosine, sine, adapted, query, key, value, weight):
    @pl.when(pl.program_id(0) == 0)
    def _():
        assemble(me_ref, weight, (p0, p1, p2, p3, p4, p5))

    unit, _ = normalize(hidden[...].astype(FULL))
    low = (unit * vectors[0:1, :] * vectors[1:2, :] + vectors[2:3, :]).astype(LOW)
    adapted[...] = low
    width = low.shape[1]
    cos, sin = cosine[...], sine[...]
    under = lower_half(head)
    signed = jnp.where(under, -sin, sin)
    scale = 1.0 / math.sqrt(head)
    for which, target in enumerate((query, key)):
        part = matmul(low, weight[:, which * width : (which + 1) * width])
        for j in range(width // LANES):
            block = part[:, j * LANES : (j + 1) * LANES]
            turned = jnp.where(
                under,
                pltpu.roll(block, LANES - head // 2, 1),
                pltpu.roll(block, head // 2, 1),
            )
            turned = (block * cos + turned * signed).astype(LOW)
            if which == 0:
                turned = turned * jnp.asarray(scale, LOW)
            target[:, j * LANES : (j + 1) * LANES] = turned
    value[...] = matmul(low, weight[:, 2 * width :]).astype(LOW)


def project(me, hidden, vectors, pieces, cosine, sine, head):
    length, width = hidden.shape
    step = 256
    rows = pl.BlockSpec((step, width), lambda i, _: (i, 0))
    angle = pl.BlockSpec((step, LANES), lambda i, _: (i, 0))
    out = jax.ShapeDtypeStruct((length, width), LOW)
    return call(
        partial(project_kernel, head),
        "project",
        (length // step,),
        [rows, whole(vectors.shape)] + [whole(p.shape) for p in pieces] + [angle, angle],
        [rows] * 4,
        [out] * 4,
        [pltpu.VMEM((width, 3 * width), LOW)],
        2 * length * width * 3 * width,
        (me, hidden, vectors, *pieces, cosine, sine),
        2 * length * width * 8,
    )


def attend_kernel(step, head, me_ref, query, key, value, mixed, logsum):
    lane = lax.broadcasted_iota(jnp.int32, (1, LANES), 1)
    first = lane < head
    keys, values = key[...], value[...]
    zero = jnp.zeros_like(keys)
    split = (jnp.where(first, keys, zero), jnp.where(first, zero, keys))
    for i in range(query.shape[0] // step):
        at = slice(i * step, (i + 1) * step)
        block = query[at, :]
        outs, sums = [], []
        for h in range(2):
            scores = matmul(block, split[h], 1, 1)
            peak = jnp.max(scores, axis=1, keepdims=True)
            expos = jnp.exp(scores - peak)
            total = jnp.sum(expos, axis=1, keepdims=True)
            outs.append(matmul(expos.astype(LOW), values) * (1.0 / total))
            sums.append(peak + jnp.log(total))
        mixed[at, :] = jnp.where(first, outs[0], outs[1]).astype(LOW)
        turned = jnp.where(first, sums[0], sums[1]).T
        logsum[0, 0:1, at] = turned[0:1, :]
        logsum[0, 1:2, at] = turned[head : head + 1, :]


def attend(me, query, key, value, head, start, pairs):
    length = query.shape[0]
    width = pairs * LANES
    block = pl.BlockSpec((length, LANES), lambda i, _: (0, i + start))
    own = pl.BlockSpec((length, LANES), lambda i, _: (0, i))
    return call(
        partial(attend_kernel, 512, head),
        "attend",
        (pairs,),
        [block] * 3,
        [own, pl.BlockSpec((1, 2, length), lambda i, _: (i, 0, 0))],
        [
            jax.ShapeDtypeStruct((length, width), LOW),
            jax.ShapeDtypeStruct((pairs, 2, length), FULL),
        ],
        [],
        16 * length * length * width,
        (me, query, key, value),
        2 * length * width * 4,
    )


def blend(parts, weight):
    total, at = None, 0
    for part in parts:
        size = part.shape[1]
        term = matmul(part[...], weight[at : at + size, :])
        total = term if total is None else total + term
        at += size
    return total


def merge_kernel(me_ref, m0, m1, hidden, vectors, pack, middle, adapted, weight):
    @pl.when(pl.program_id(0) == 0)
    def _():
        stack_halves(weight, pack)

    branch = blend((m0, m1), weight)
    mid = hidden[...].astype(FULL) + vectors[0:1, :] * branch
    middle[...] = mid
    unit, _ = normalize(mid)
    adapted[...] = (unit * vectors[1:2, :] * vectors[2:3, :] + vectors[3:4, :]).astype(LOW)


def merge(me, mixed, hidden, vectors, pack):
    length, width = hidden.shape
    step = 256
    rows = pl.BlockSpec((step, width), lambda i, _: (i, 0))
    some = [pl.BlockSpec((step, m.shape[1]), lambda i, _: (i, 0)) for m in mixed]
    return call(
        merge_kernel,
        "merge",
        (length // step,),
        some + [rows, whole(vectors.shape), merge_spec(pack, width)],
        [rows, rows],
        [jax.ShapeDtypeStruct((length, width), FULL), jax.ShapeDtypeStruct((length, width), LOW)],
        [pltpu.VMEM((width, width), LOW)],
        2 * length * width * width,
        (me, *mixed, hidden, vectors, pack),
        2 * length * width * 6,
    )


def feed_kernel(last, at_ref, adapted, upstream, vectors, lift_bias, pack, *refs):
    if last:
        low_in, grad_in, middle, block_out, adapted_grad, sums, liftbias_grad, grads = refs[:8]
        lift, turned, lowered_grad, lowered, low_got, grad_got, middle_got, sem = refs[8:]
        copies = [
            pltpu.make_async_copy(source, target, sem.at[k])
            for k, (source, target) in enumerate(
                ((low_in, low_got), (grad_in, grad_got), (middle, middle_got))
            )
        ]
        for copy in copies:
            copy.start()
    else:
        lowered, adapted_grad, liftbias_grad, grads = refs[:4]
        lift, turned, lowered_grad = refs[4:]
    gate = vectors[0:1, :]
    rows = lift.shape[0] // 4
    step = lift.shape[1] // 2
    turned[...] = adapted[...].T
    lowered_grad[...] = (gate * upstream[...].astype(FULL)).astype(LOW)
    for i in range(2):
        deep = slice(step + i * rows, step + (i + 1) * rows)
        half_rows, half_step = rows // 2, step // 2
        for j in range(4):
            for k in range(2):
                low = (2 * j + k) * half_rows
                at = half_step + i * half_rows
                lift[low : low + half_rows, :] = pack[4 * k + j, at : at + half_rows, :]
        weight_up = lift[...]
        weight_down = jnp.concatenate(
            [pack[4 * k + j, :half_step, :] for j in (2 * i, 2 * i + 1) for k in range(2)], axis=0
        )
        across = slice(2 * i * step, 2 * (i + 1) * step)
        upper = matmul(adapted[...], weight_up) + lift_bias[:, across]
        square = upper * upper
        root = math.sqrt(2.0 / math.pi)
        bent = jnp.tanh(upper * (root + root * 0.044715 * square))
        half = 0.5 + 0.5 * bent
        slope = half + upper * (0.5 - 0.5 * bent * bent) * (root + 3.0 * root * 0.044715 * square)
        active = (upper * half).astype(LOW)
        low_part = matmul(active, weight_down)
        down = lowered_grad[...]
        upper_grad = (matmul(down, weight_down, 1, 1) * slope).astype(LOW)
        grad_part = matmul(upper_grad, weight_up, 1, 1)
        if i == 0:
            lowered[...] = low_part
            adapted_grad[...] = grad_part
        else:
            lowered[...] += low_part
            adapted_grad[...] += grad_part
        liftbias_grad[:, across] = column_sum(upper_grad.astype(FULL))
        drop_part = matmul(active, down, 0, 0).astype(LOW)
        for k in range(2):
            grads[2 * i + k, :step, :] = drop_part[k * step : (k + 1) * step]
        lift_part = matmul(turned[...], upper_grad).astype(LOW)
        for j in range(4):
            grads[j, deep, :] = lift_part[j * rows : (j + 1) * rows]

    if last:
        for copy in copies:
            copy.wait()
        adapted_grad[...] += grad_got[...]
        total = lowered[...] + low_got[...] + vectors[1:2, :]
        block_out[...] = (middle_got[...] + gate * total).astype(LOW)
        sums[0:1, :] = column_sum(upstream[...].astype(FULL) * total)
        sums[1:2, :] = column_sum(lowered_grad[...].astype(FULL))


def feed(me, adapted, upstream, vectors, lift_bias, pack, which, before=()):
    length, width = adapted.shape
    last = len(before) > 0
    units = lift_bias.shape[1]
    wide = jax.ShapeDtypeStruct((length, width), FULL)
    low = jax.ShapeDtypeStruct((length, width), LOW)
    more = jax.ShapeDtypeStruct((4, units // 2, width), LOW)
    sums = jax.ShapeDtypeStruct((8, width), FULL)
    bias = jax.ShapeDtypeStruct((1, units), FULL)
    outs = [low, wide, sums, bias, more] if last else [wide, wide, bias, more]
    scratch = [
        pltpu.VMEM((width, units // 2), LOW),
        pltpu.VMEM((width, length), LOW),
        pltpu.VMEM((length, width), LOW),
    ]
    if last:
        scratch += [pltpu.VMEM((length, width), FULL)] * 4 + [pltpu.SemaphoreType.DMA((3,))]
    return call(
        partial(feed_kernel, last),
        "feed",
        (1,),
        [whole(a.shape) for a in (adapted, upstream, vectors, lift_bias)]
        + [
            pl.BlockSpec(
                (8, units // 4, width), lambda *_: (0, which, 0), pipeline_mode=pl.Buffered(1)
            )
        ]
        + [pl.BlockSpec(memory_space=pl.ANY) for _ in before],
        [whole(o.shape) for o in outs],
        outs,
        scratch,
        12 * length * width * units,
        (me, adapted, upstream, vectors, lift_bias, pack, *before),
        8 * width * units + 24 * length * width,
    )


def unmerge_kernel(
    me_ref, adapted_grad, middle, upstream, m0, m1, vectors, pack,
    middle_grad, mixed_grad, sums, keep, send, weight, total,
):
    i = pl.program_id(0)

    @pl.when(i == 0)
    def _():
        stack_halves(weight, pack)
        total[...] = jnp.zeros_like(total)
        sums[...] = jnp.zeros_like(sums)

    gate, gain, grow = vectors[0:1, :], vectors[1:2, :], vectors[2:3, :]
    unit, inverse = normalize(middle[...])
    grad = adapted_grad[...]
    sums[0:1, :] += column_sum(grad)
    sums[1:2, :] += column_sum(grad * (unit * gain))
    normed_grad = grad * grow
    sums[2:3, :] += column_sum(normed_grad * unit)
    mid_grad = upstream[...].astype(FULL) + unnormalize(normed_grad * gain, unit, inverse)
    middle_grad[...] = mid_grad
    sums[3:4, :] += column_sum(mid_grad * blend((m0, m1), weight))
    branch_grad = (gate * mid_grad).astype(LOW)
    at = 0
    for part in (m0, m1):
        size = part.shape[1]
        total[at : at + size, :] += matmul(part[...], branch_grad, 0, 0)
        at += size
    mixed_grad[...] = matmul(branch_grad, weight[...], 1, 1).astype(LOW)

    @pl.when(i == pl.num_programs(0) - 1)
    def _():
        split_rows(me_ref[0], total[...], keep, send)


def unmerge(me, adapted_grad, middle, upstream, mixed, vectors, pack):
    length, width = middle.shape
    step = 256
    rows = pl.BlockSpec((step, width), lambda i, _: (i, 0))
    some = [pl.BlockSpec((step, m.shape[1]), lambda i, _: (i, 0)) for m in mixed]
    part = (2, width // 4, width)
    return call(
        unmerge_kernel,
        "unmerge",
        (length // step,),
        [rows] * 3 + some + [whole(vectors.shape), merge_spec(pack, width)],
        [rows, rows, kept((8, width)), kept(part), kept(part)],
        [
            jax.ShapeDtypeStruct((length, width), FULL),
            jax.ShapeDtypeStruct((length, width), LOW),
            jax.ShapeDtypeStruct((8, width), FULL),
            jax.ShapeDtypeStruct(part, LOW),
            jax.ShapeDtypeStruct(part, LOW),
        ],
        [pltpu.VMEM((width, width), LOW), pltpu.VMEM((width, width), FULL)],
        6 * length * width * width,
        (me, adapted_grad, middle, upstream, *mixed, vectors, pack),
        2 * length * width * 12,
    )


def unattend_kernel(step, head, me_ref, query, key, value, mixed, mixed_grad, logsum, cosine, sine, grads, query_sum, key_sum, value_sum):
    lane = lax.broadcasted_iota(jnp.int32, (1, LANES), 1)
    first = lane < head
    keys, values = key[...], value[...]
    zero = jnp.zeros_like(keys)
    keys_h = (jnp.where(first, keys, zero), jnp.where(first, zero, keys))
    values_h = (jnp.where(first, values, zero), jnp.where(first, zero, values))
    turned = keys.T
    scale = 1.0 / math.sqrt(head)
    for i in range(query.shape[0] // step):
        at = slice(i * step, (i + 1) * step)
        block, grad = query[at, :], mixed_grad[at, :]
        product = (grad.astype(FULL) * mixed[at, :].astype(FULL)).T
        queries, values_new, keys_new = [], [], []
        for h in range(2):
            center = jnp.sum(product[h * head : (h + 1) * head], axis=0, keepdims=True)
            probs = jnp.exp(matmul(keys_h[h], block, 1, 1) - logsum[0, h : h + 1, at])
            probs_grad = matmul(values_h[h], grad, 1, 1)
            scores_grad = (probs * (probs_grad - center)).astype(LOW)
            values_new.append(matmul(probs.astype(LOW), grad))
            keys_new.append(matmul(scores_grad, block))
            queries.append(matmul(turned[h * head : (h + 1) * head], scores_grad))
        query_sum[at, :] = jnp.concatenate(queries, axis=0).T * scale
        key_part = jnp.where(first, keys_new[0], keys_new[1])
        value_part = jnp.where(first, values_new[0], values_new[1])
        if i == 0:
            key_sum[...] = key_part
            value_sum[...] = value_part
        else:
            key_sum[...] += key_part
            value_sum[...] += value_part
    under = lower_half(head)
    cos, sin = cosine[...], sine[...]
    for which, total in enumerate((query_sum, key_sum)):
        rotated = total[...]
        swept = rotated * sin
        back = jnp.where(
            under, pltpu.roll(swept, LANES - head // 2, 1), -pltpu.roll(swept, head // 2, 1)
        )
        grads[which] = (rotated * cos + back).astype(LOW)
    grads[2] = value_sum[...].astype(LOW)


def unattend(me, query, key, value, mixed, mixed_grad, logsum, cosine, sine, head, start):
    length, width = mixed.shape
    pairs = width // LANES
    block = pl.BlockSpec((length, LANES), lambda i, _: (0, i + start))
    own = pl.BlockSpec((length, LANES), lambda i, _: (0, i))
    return call(
        partial(unattend_kernel, 256, head),
        "unattend",
        (pairs,),
        [block] * 3
        + [own, block]
        + [pl.BlockSpec((1, 2, length), lambda i, _: (i, 0, 0))]
        + [whole((length, LANES))] * 2,
        [pl.BlockSpec((3, length, LANES), lambda i, _: (0, 0, i))],
        [jax.ShapeDtypeStruct((3, length, width), LOW)],
        [pltpu.VMEM((length, LANES), FULL)] * 3,
        40 * length * length * width,
        (me, query, key, value, mixed, mixed_grad, logsum, cosine, sine),
        2 * length * width * 8,
    )[0]


def weigh_kernel(me_ref, adapted, grads, *refs):
    keep, send, turned = refs[-3:]
    i = pl.program_id(0)

    @pl.when(i == 0)
    def _():
        turned[...] = adapted[...].T

    @pl.when(i < 3)
    def _():
        split_rows(me_ref[0], matmul(turned[...], grads[0]), keep, send)

    if len(refs) > 3:

        @pl.when(i >= 3)
        def _():
            keep[...] = refs[0][...]
            send[...] = refs[1][...]


def weigh(me, adapted, grads, extra=()):
    length, width = adapted.shape
    step = grads.shape[2]
    more = extra[0].shape[2] // step if extra else 0
    part = pl.BlockSpec((2, width // 4, step), lambda i, _: (0, 0, i))
    rider = pl.BlockSpec((2, width // 4, step), lambda i, _: (0, 0, jnp.maximum(i - 3, 0)))
    shape = jax.ShapeDtypeStruct((2, width // 4, (3 + more) * step), LOW)
    return call(
        weigh_kernel,
        "weigh",
        (3 + more,),
        [whole(adapted.shape), pl.BlockSpec((1, length, step), lambda i, _: (jnp.minimum(i, 2), 0, 0))]
        + [rider] * len(extra),
        [part, part],
        [shape, shape],
        [pltpu.VMEM((width, length), LOW)],
        6 * length * width * step,
        (me, adapted, grads, *extra),
        2 * length * width * 7,
    )


def unproject_kernel(me_ref, g0, g1, hidden, middle_grad, vectors, p0, p1, p2, p3, p4, p5, o0, o1, o2, o3, sums, weight):
    i = pl.program_id(0)

    @pl.when(i == 0)
    def _():
        assemble(me_ref, weight, (p0, p1, p2, p3, p4, p5))
        sums[...] = jnp.zeros_like(sums)

    gain, grow = vectors[0:1, :], vectors[1:2, :]
    width = hidden.shape[1]
    grad, at = None, 0
    for part in (g0, g1):
        size = part.shape[2]
        for which in range(3):
            low = which * width + at
            term = matmul(part[which], weight[:, low : low + size], 1, 1)
            grad = term if grad is None else grad + term
        at += size
    unit, inverse = normalize(hidden[...].astype(FULL))
    sums[0:1, :] += column_sum(grad)
    sums[1:2, :] += column_sum(grad * (unit * gain))
    normed_grad = grad * grow
    sums[2:3, :] += column_sum(normed_grad * unit)
    low = (middle_grad[...] + unnormalize(normed_grad * gain, unit, inverse)).astype(LOW)
    for d, target in enumerate((o0, o1, o2, o3)):

        @pl.when(i == me_ref[0] ^ d)
        def _(target=target):
            target[...] = low


def unproject(me, grads, hidden, middle_grad, vectors, pieces):
    length, width = hidden.shape
    step = length // 4
    rows = pl.BlockSpec((step, width), lambda i, _: (i, 0))
    return call(
        unproject_kernel,
        "unproject",
        (length // step,),
        [pl.BlockSpec((3, step, g.shape[2]), lambda i, _: (0, i, 0)) for g in grads]
        + [rows, rows, whole(vectors.shape)]
        + [whole(p.shape) for p in pieces],
        [kept((step, width))] * 4 + [kept((8, width))],
        [jax.ShapeDtypeStruct((step, width), LOW)] * 4 + [jax.ShapeDtypeStruct((8, width), FULL)],
        [pltpu.VMEM((width, 3 * width), LOW)],
        6 * length * width * width,
        (me, *grads, hidden, middle_grad, vectors, *pieces),
        2 * length * width * 10,
    )


def lay_kernel(me_ref, *refs):
    for d, part in enumerate(refs[:-1]):
        refs[-1][pl.ds(me_ref[0] ^ d, 1)] = part[...][None]


def lay(me, parts):
    shape = (len(parts),) + parts[0].shape
    return call(
        lay_kernel, "lay", (1,), [whole(p.shape) for p in parts], [whole(shape)],
        [jax.ShapeDtypeStruct(shape, LOW)], [], 1024, (me, *parts), 1024,
    )[0]


def swap(array, axis, distance):
    size = lax.axis_size(axis)
    return lax.ppermute(array, axis, [(i, i ^ distance) for i in range(size)])


def fence(*trees):
    return lax.optimization_barrier(trees)


def bit(axis, distance):
    return (lax.axis_index(axis) // distance) % 2


def choose(parts, at):
    return lax.dynamic_index_in_dim(parts, at, 0, keepdims=False)


def choose_all(array, place):
    count = array.shape[0]
    return jnp.stack([choose(array, place ^ k) for k in range(count)])


def payload(parts):
    return jnp.concatenate([p.reshape(2, p.shape[0] // 2, p.shape[1]) for p in parts], axis=1)


def blocks_of(weight, width):
    return [weight[:, k : k + width] for k in range(0, weight.shape[1], width)]


def powers(size):
    return [1 << k for k in range(size.bit_length() - 1)]


def gather_small(array, axis, distances):
    array = array[None]
    done = []
    for distance in distances:
        other = swap(array, axis, distance)
        at = bit(axis, distance)
        place = sum(d > distance for d in done)
        lead = [2] * place
        shape = array.shape
        pair = [a.reshape(lead + [1, -1] + list(shape[1:])) for a in (array, other)]
        array = jnp.where(
            at == 0, jnp.concatenate(pair, place), jnp.concatenate(pair[::-1], place)
        ).reshape((2 * shape[0],) + shape[1:])
        done.append(distance)
    return array


def plus(*terms):
    total = terms[0].astype(FULL)
    for term in terms[1:]:
        total = total + term.astype(FULL)
    return total.astype(LOW)


def pair_kernel(at_ref, kept_term, got, mine, other):
    mine[...] = plus(kept_term[0], got[0])
    other[...] = plus(kept_term[1], got[1])


def sum_pair(kept_term, got):
    _, rows, columns = kept_term.shape
    step = rows // 4
    two = pl.BlockSpec((2, step, columns), lambda i, _: (0, i, 0))
    one = pl.BlockSpec((step, columns), lambda i, _: (i, 0))
    out = jax.ShapeDtypeStruct((rows, columns), LOW)
    return call(
        pair_kernel, "pair", (4,), [two, two], [one, one], [out, out], [], 1024,
        (jnp.zeros((1,), jnp.int32), kept_term, got), 1024,
    )


def blend_kernel(at_ref, a, b, c, d, both):
    cut = a.shape[1]
    both[:, :cut] = plus(a[...], b[...])
    both[:, cut:] = plus(c[...], d[...])


def sum_beside(first, second):
    args = (*first, *second)
    rows = args[0].shape[0]
    out = (rows, args[0].shape[1] + args[2].shape[1])
    return call(
        blend_kernel, "beside", (1,), [whole(a.shape) for a in args], [whole(out)],
        [jax.ShapeDtypeStruct(out, LOW)], [], 1024, (jnp.zeros((1,), jnp.int32), *args), 1024,
    )[0]


def deal(term):
    size = lax.axis_size("dp")
    rows, columns = term.shape
    parts = term.reshape(size, rows // size, columns)
    return lax.all_to_all(parts, "dp", 0, 0, tiled=True)


def add_kernel(at_ref, parts, total):
    total[...] = plus(*[parts[k] for k in range(parts.shape[0])])


def add_up(parts):
    shape = parts.shape[1:]
    return call(
        add_kernel, "add", (1,), [whole(parts.shape)], [whole(shape)],
        [jax.ShapeDtypeStruct(shape, LOW)], [], 1024, (jnp.zeros((1,), jnp.int32), parts), 1024,
    )[0]


def place_of(distance):
    return bit("dp", distance).astype(jnp.int32).reshape(1)


def join_kernel(at_ref, first, second, both):
    b = at_ref[0]
    both[pl.ds(b, 1)] = first[...][None]
    both[pl.ds(1 - b, 1)] = second[...][None]


def join(first, second, distance):
    rows, columns = first.shape
    shape = (2, rows, columns)
    return call(
        join_kernel, "join", (1,), [whole(first.shape)] * 2, [whole(shape)],
        [jax.ShapeDtypeStruct(shape, LOW)], [], 1024, (place_of(distance), first, second), 1024,
    )[0].reshape(2 * rows, columns)


def spread(term, got, distances):
    for k, distance in enumerate(distances[:-1]):
        term = join(term, got, distance)
        got = swap(term, "dp", distances[k + 1])
    return term, got


def settle_kernel(plan, size, at_ref, *refs):
    count = len(plan)
    outs = refs[2 * count :]
    depth = size.bit_length() - 1
    b = at_ref[0]
    for p, moves in enumerate(plan):
        rows = 2 * refs[2 * p].shape[0] // size
        for h in range(2):
            value = jnp.where(b == h, refs[2 * p][...], refs[2 * p + 1][...]).astype(FULL)
            for k in range(h, size, 2):
                at = sum(((k >> j) & 1) << (depth - 1 - j) for j in range(1, depth)) * rows
                for top, left, down, wide, out, to_row, to_column in moves:
                    low, high = max(top, k * rows), min(top + down, (k + 1) * rows)
                    if low < high:
                        start = to_row + low - top
                        source = at + low - k * rows
                        outs[out][start : start + high - low, to_column : to_column + wide] = value[
                            source : source + high - low, left : left + wide
                        ]


def settle(pairs, plan, shapes):
    args = [array for pair in pairs for array in pair]
    return call(
        partial(settle_kernel, plan, lax.axis_size("dp")),
        "settle",
        (1,),
        [whole(a.shape) for a in args],
        [whole(shape) for shape in shapes],
        [jax.ShapeDtypeStruct(shape, FULL) for shape in shapes],
        [],
        1024,
        (place_of(1), *args),
        1024,
    )


def shards(
    hidden_in,
    time_table,
    time_step,
    token_pos,
    heads_weight,
    merge_weight,
    lift_weight,
    lift_bias,
    drop_weight,
    drop_bias,
    modulate_weight,
    modulate_bias,
    first_gain,
    second_gain,
    out_grad,
):
    count = lax.axis_size("seq")
    place = lax.axis_index("seq")
    seqs, span, width = hidden_in.shape
    assert count == 4 and seqs == count
    length = span * count
    head = width // HEADS
    bits = powers(lax.axis_size("dp"))
    row_half = bit("dp", 1)
    me = jnp.stack([place, row_half]).astype(jnp.int32)

    units = drop_weight.shape[0]
    step = units // 2
    heads_pack = payload(blocks_of(heads_weight, width))
    heads_across = swap(choose(heads_pack, row_half), "seq", 2)

    parts = []
    for h in range(2):
        columns = [lift_weight[:, j * units + h * step : j * units + (h + 1) * step] for j in range(4)]
        parts.append(drop_weight[h * step : (h + 1) * step])
        parts += [jnp.concatenate(columns[k : k + 2], axis=1) for k in (0, 2)]
    pack = choose(payload(parts + [merge_weight]), row_half)
    def gather_halves(pack):
        size = 2 * count
        total = count * lax.axis_size("dp")
        groups = [list(range(k, k + size)) for k in range(0, total, size)]
        return lax.all_gather(pack, ("dp", "seq"), axis=0, axis_index_groups=groups)

    table_rows, depth = time_table.shape
    chosen_rows = (time_step[:, None] == jnp.arange(table_rows, dtype=jnp.int32)[None, :]).astype(LOW)
    conds = jnp.dot(chosen_rows, time_table, preferred_element_type=FULL)
    modulation = matmul(conds.astype(LOW), modulate_weight, 1, 1) + modulate_bias.astype(FULL)
    columns = modulation.shape[1]
    small = jnp.concatenate(
        [modulation.reshape(-1)]
        + [v.astype(FULL) for v in (lift_bias, drop_bias, first_gain, second_gain)]
        + [token_pos.astype(FULL).reshape(-1)]
    )
    small_across = swap(small, "seq", 2)
    heads_across, small, small_across, hidden_in, pack = fence(
        heads_across, small, small_across, hidden_in, pack
    )
    heads_handed = swap(heads_across, "dp", 1)
    heads_core = swap(heads_pack, "seq", 1), swap(heads_across, "seq", 1)
    hidden = lax.all_to_all(hidden_in, "seq", 0, 0, tiled=True).reshape(length, width)
    packs = gather_halves(pack)
    small = jnp.stack([small, small_across])
    small_core = swap(small, "seq", 1)
    small = jnp.stack([small[0], small_core[0], small[1], small_core[1]])
    small = choose_all(small, place)
    heads = (
        heads_pack,
        heads_core[0],
        heads_across,
        heads_handed,
        heads_core[1],
        swap(heads_handed, "seq", 1),
    )
    chosen = small[:, : seqs * columns].reshape(count, seqs, columns)
    chosen = lax.dynamic_index_in_dim(chosen, place, 1, keepdims=False).reshape(6, width)
    rest = small[:, seqs * columns :]
    sizes = (lift_bias.shape[0], drop_bias.shape[0], first_gain.shape[0], second_gain.shape[0])
    vectors, at = [], 0
    for size in sizes:
        vectors.append(rest[:, at : at + size].reshape(1, -1))
        at += size
    up_bias, down_bias, gain_one, gain_two = vectors
    positions = choose(rest[:, at:].reshape(count, seqs, span).swapaxes(0, 1), place)
    positions = positions.reshape(length)
    shift_a, scale_a, gate_a, shift_b, scale_b, gate_b = [chosen[k : k + 1] for k in range(6)]
    grow_a, grow_b = 1.0 + scale_a, 1.0 + scale_b

    def rows(*items):
        blank = jnp.zeros((8 - len(items), width), FULL)
        return jnp.concatenate(items + (blank,), axis=0)

    freqs = 10000.0 ** (-jnp.arange(0, head, 2, dtype=FULL) / head)
    freqs = jnp.tile(freqs, 2 * LANES // head)
    angles = positions[:, None] * freqs
    cosine, sine = jnp.cos(angles), jnp.sin(angles)

    hidden, heads, cosine, sine, out_grad = fence(hidden, heads, cosine, sine, out_grad)
    adapted_a, query, key, value = project(
        me, hidden, rows(gain_one, grow_a, shift_a), heads, cosine, sine, head
    )
    query, out_grad = fence(query, out_grad)
    upstream = lax.all_to_all(out_grad, "seq", 0, 0, tiled=True).reshape(length, width)
    pairs = width // LANES // 2
    mixed_0, logsum_0 = attend(me, query, key, value, head, 0, pairs)
    merge_vectors, unmerge_vectors = rows(gate_a, gain_two, grow_b, shift_b), rows(gate_a, gain_two, grow_b)
    feed_vectors = rows(gate_b, down_bias)
    bias_0, bias_1 = [up_bias.reshape(4, 2, step)[:, h].reshape(1, 4 * step) for h in range(2)]
    query, merge_vectors, unmerge_vectors, feed_vectors, bias_0, bias_1 = fence(
        query, merge_vectors, unmerge_vectors, feed_vectors, bias_0, bias_1
    )
    query, mixed_0 = fence(query, mixed_0)
    mixed_1, logsum_1 = attend(me, query, key, value, head, pairs, pairs)
    mixed_1, upstream = fence(mixed_1, upstream)
    mixed = (mixed_0, mixed_1)
    middle, adapted_b = merge(me, mixed, hidden, merge_vectors, packs)
    lowered, grad, liftbias_0, grads_0 = feed(
        me, adapted_b, upstream, feed_vectors, bias_0, packs, 0
    )

    def over_seq(grads):
        flat = grads.reshape(-1, grads.shape[-1])
        return lax.psum_scatter(flat, "seq", scatter_dimension=0, tiled=True)

    term_0 = over_seq(grads_0)
    block_out, adapted_b_grad, feed_sums, liftbias_1, grads_1 = feed(
        me, adapted_b, upstream, feed_vectors, bias_1, packs, 1, (lowered, grad, middle)
    )
    term_1 = over_seq(grads_1)
    back = bits[::-1]
    middle_grad, mixed_grad, merge_sums, merge_keep, merge_send = unmerge(
        me, adapted_b_grad, middle, upstream, mixed, unmerge_vectors, packs
    )
    block_out = lax.all_to_all(block_out.reshape(count, span, width), "seq", 0, 0, tiled=True)
    heads_0 = unattend(
        me, query, key, value, mixed_0, mixed_grad, logsum_0, cosine, sine, head, 0
    )
    heads_0, term_0, block_out = fence(heads_0, term_0, block_out)
    parts_0 = deal(term_0)
    keep_2, send_2 = weigh(me, adapted_a, heads_0, (merge_keep, merge_send))
    mixed_grad, send_2 = fence(mixed_grad, send_2)
    got_2 = swap(send_2, "seq", 1)
    heads_1 = unattend(
        me, query, key, value, mixed_1, mixed_grad, logsum_1, cosine, sine, head, pairs
    )
    heads_1, got_2, parts_0 = fence(heads_1, got_2, parts_0)
    heads_1, mine_2, other_2, term_0 = fence(heads_1, *sum_pair(keep_2, got_2), add_up(parts_0))
    got_2 = swap(other_2, "seq", 2)
    got_0 = swap(term_0, "dp", back[0])
    keep_3, send_3 = weigh(me, adapted_a, heads_1)
    heads_1, send_3, got_0, term_1 = fence(heads_1, send_3, got_0, term_1)
    got_3 = swap(send_3, "seq", 1)
    heads_1, term_0 = fence(heads_1, join(term_0, got_0, back[0]))
    got_0 = swap(term_0, "dp", back[1])
    parts_1 = deal(term_1)
    heads_1, got_3 = fence(heads_1, got_3)
    heads_1, mine_3, other_3 = fence(heads_1, *sum_pair(keep_3, got_3))
    got_3 = swap(other_3, "seq", 2)
    *input_parts, project_sums = unproject(
        me, (heads_0, heads_1), hidden, middle_grad, rows(gain_one, grow_a), heads
    )
    liftbias_grad = jnp.stack([liftbias_0.reshape(4, step), liftbias_1.reshape(4, step)], axis=1)
    modulation_grad = jnp.concatenate(
        [project_sums[0:2], merge_sums[3:4], merge_sums[0:2], feed_sums[0:1]], axis=0
    ).reshape(count, columns)
    small = jnp.concatenate(
        [
            modulation_grad,
            liftbias_grad.reshape(count, -1),
            feed_sums[1].reshape(count, -1),
            project_sums[2].reshape(count, -1),
            merge_sums[2].reshape(count, -1),
        ],
        axis=1,
    )
    parts = [choose(small, place ^ d) for d in range(4)]
    parts = [swap(part, "seq", d) if d else part for d, part in enumerate(parts)]
    input_parts, got_0, got_2, got_3, parts_1, parts = fence(
        input_parts, got_0, got_2, got_3, parts_1, parts
    )
    pack = choose_all(jnp.stack(parts), place)
    pack = jnp.concatenate(
        [
            pack[:, :columns].reshape(-1),
            jnp.sum(pack[:, columns:], axis=0),
            conds.reshape(-1),
            time_step.astype(FULL),
        ]
    )[None]

    def doubled(array, other, distance):
        pair = jnp.stack([array, other])
        return jnp.where(bit("dp", distance) == 0, pair, pair[::-1])

    last = len(back) - 1
    term_0 = join(term_0, got_0, back[1])
    term_1 = add_up(parts_1)
    term_2 = sum_beside((mine_2, got_2), (mine_3, got_3))
    input_parts, pack, term_0, term_1, term_2 = fence(input_parts, pack, term_0, term_1, term_2)
    for k in range(2, last):
        term_0 = join(term_0, swap(term_0, "dp", back[k]), back[k])
    got_0 = swap(term_0, "dp", back[-1])
    got_1 = swap(term_1, "dp", back[0])
    parts_2 = deal(term_2)
    other = swap(pack, "dp", back[0])
    input_parts = [swap(part, "seq", d) if d else part for d, part in enumerate(input_parts)]
    input_parts, got_0, got_1, parts_2, other = fence(input_parts, got_0, got_1, parts_2, other)
    term_2 = add_up(parts_2)
    got_2 = None
    for k in range(last):
        term_1 = join(term_1, got_1, back[k])
        if k:
            term_2 = join(term_2, got_2, back[k - 1])
        pack = doubled(pack, other, back[k])
        term_1, term_2, pack = fence(term_1, term_2, pack)
        got_1 = swap(term_1, "dp", back[k + 1])
        got_2 = swap(term_2, "dp", back[k])
        other = swap(pack, "dp", back[k + 1])
        if k == 0:
            input_grad = lay(me, input_parts)
        got_1, got_2, other = fence(got_1, got_2, other)
    pack = doubled(pack, other, back[-1]).reshape(lax.axis_size("dp"), -1)
    term_2 = join(term_2, got_2, back[last - 1])
    pack, term_2 = fence(pack, term_2)
    pair_0, pair_1 = (term_0, got_0), (term_1, got_1)
    pair_2 = (term_2, swap(term_2, "dp", back[-1]))
    deep = width // 4
    drop_grad, lift_grad = settle(
        [pair_0, pair_1],
        [
            [(0, 0, step, width, 0, h * step, 0)]
            + [
                (step + (j >> 1) * deep, (j & 1) * step, deep, step, 1, 0, j * units + h * step)
                for j in range(4)
            ]
            for h in range(2)
        ],
        [drop_weight.shape, lift_weight.shape],
    )
    part = width // 2
    heads_grad, merge_grad = settle(
        [pair_2],
        [
            [(0, 3 * part, deep, width, 1, 0, 0)]
            + [(0, k * part, deep, part, 0, 0, k * width) for k in range(3)]
            + [(0, (5 + k) * part, deep, part, 0, 0, k * width + part) for k in range(3)],
        ],
        [heads_weight.shape, merge_weight.shape],
    )
    row_grads = pack[:, : seqs * columns].reshape(-1, columns)
    at = seqs * columns
    ends = []
    for size in sizes:
        ends.append(jnp.sum(pack[:, at : at + size], axis=0))
        at += size
    liftbias_out, dropbias_out, firstgain_out, secondgain_out = ends
    all_conds = pack[:, at : at + seqs * depth].reshape(-1, depth)
    steps = pack[:, at + seqs * depth :].reshape(-1)
    exact = lax.Precision.HIGHEST
    modulate_grad = jnp.einsum("sm,sc->mc", row_grads, all_conds, precision=exact)
    modulatebias_grad = jnp.sum(row_grads, axis=0)
    conds_grad = jnp.einsum(
        "sm,mc->sc", row_grads, modulate_weight.astype(FULL), precision=exact
    )
    conds_grad = sum([swap(conds_grad, "seq", d) for d in (1, 2, 3)], conds_grad)
    share = table_rows // count
    own = steps[None, :] == (place * share + jnp.arange(share)).astype(FULL)[:, None]
    table_grad = jnp.dot(own.astype(FULL), conds_grad, precision=exact)
    return (
        block_out,
        input_grad,
        heads_grad,
        merge_grad,
        lift_grad,
        liftbias_out,
        drop_grad,
        dropbias_out,
        modulate_grad,
        modulatebias_grad,
        firstgain_out,
        secondgain_out,
        table_grad,
    )


def solution(mesh):
    return jax.shard_map(
        shards,
        mesh=mesh,
        in_specs=(
            P("dp", "seq", None),
            P(),
            P("dp"),
            P("dp", "seq"),
            P("seq", None),
            P("seq", None),
            P("seq", None),
            P("seq"),
            P("seq", None),
            P("seq"),
            P("seq", None),
            P("seq"),
            P("seq"),
            P("seq"),
            P("dp", "seq", None),
        ),
        out_specs=(
            P("dp", "seq", None),
            P("dp", "seq", None),
            P("seq", None),
            P("seq", None),
            P("seq", None),
            P("seq"),
            P("seq", None),
            P("seq"),
            P("seq", None),
            P("seq"),
            P("seq"),
            P("seq"),
            P("seq", None),
        ),
        check_vma=False,
    )
```

```python
from functools import partial
import math

import jax
import jax.numpy as jnp
from jax import lax
from jax.experimental import pallas as pl
from jax.experimental.pallas import tpu as pltpu
from jax.sharding import PartitionSpec as P

HEADS = 12
EPSILON = 1e-05
LANES = 128
VMEM = 60 * 1024 * 1024
LOW = jnp.bfloat16
FULL = jnp.float32


def matmul(left, right, left_dim=1, right_dim=0):
    dims = (((left_dim,), (right_dim,)), ((), ()))
    return lax.dot_general(left, right, dims, preferred_element_type=FULL)


def call(body, name, grid, in_specs, out_specs, out_shape, scratch, flops, args, moved):
    return pl.pallas_call(
        body,
        name=name,
        grid_spec=pltpu.PrefetchScalarGridSpec(
            num_scalar_prefetch=1,
            grid=grid,
            in_specs=in_specs,
            out_specs=out_specs,
            scratch_shapes=scratch,
        ),
        out_shape=out_shape,
        compiler_params=pltpu.CompilerParams(
            dimension_semantics=("arbitrary",) * len(grid), vmem_limit_bytes=VMEM
        ),
        cost_estimate=pl.CostEstimate(flops=flops, bytes_accessed=moved, transcendentals=0)
        if name in ("feed", "two", "add")
        else pl.CostEstimate(flops=1024, bytes_accessed=1024, transcendentals=0),
    )(*args)


def whole(shape):
    zeros = (0,) * len(shape)
    return pl.BlockSpec(shape, lambda *_: zeros, pipeline_mode=pl.Buffered(1))


def kept(shape):
    zeros = (0,) * len(shape)
    return pl.BlockSpec(shape, lambda *_: zeros)


def assemble(at, target, pieces, start, blocks):
    me, b = at[0], at[1]
    own, core, across, handed, core_across, core_handed = pieces
    rows = target.shape[0] // 8
    width = target.shape[1] // blocks
    halves = (
        (me, 0, lambda cut: own[0, cut, :]),
        (me, 1, lambda cut: own[1, cut, :]),
        (me ^ 1, 0, lambda cut: core[0, cut, :]),
        (me ^ 1, 1, lambda cut: core[1, cut, :]),
        (me ^ 2, b, lambda cut: across[cut, :]),
        (me ^ 2, 1 - b, lambda cut: handed[cut, :]),
        (me ^ 3, b, lambda cut: core_across[cut, :]),
        (me ^ 3, 1 - b, lambda cut: core_handed[cut, :]),
    )
    for shard, half, read in halves:
        place = pl.ds(pl.multiple_of((2 * shard + half) * rows, 16), rows)
        for k in range(blocks):
            cut = slice(start + k * rows, start + (k + 1) * rows)
            target[place, k * width : (k + 1) * width] = read(cut)


def portion(pieces, start, size):
    at = start // size
    return [
        pl.BlockSpec(
            p.shape[:-2] + (size, p.shape[-1]),
            partial(lambda n, *_: (0,) * n + (at, 0), len(p.shape) - 2),
            pipeline_mode=pl.Buffered(1),
        )
        for p in pieces
    ]


def split_rows(me, value, keep, send):
    rows = value.shape[0] // 4
    mine_x, mine_c = me >> 1, me & 1
    for j in range(4):
        part = value[j * rows : (j + 1) * rows].astype(LOW)[None]
        at = (j >> 1) ^ mine_x

        @pl.when(mine_c == (j & 1))
        def _(part=part, at=at):
            keep[pl.ds(at, 1)] = part

        @pl.when(mine_c != (j & 1))
        def _(part=part, at=at):
            send[pl.ds(at, 1)] = part


def normalize(values):
    center = values - jnp.mean(values, axis=-1, keepdims=True)
    inverse = lax.rsqrt(jnp.mean(center * center, axis=-1, keepdims=True) + EPSILON)
    return center * inverse, inverse


def unnormalize(weighted, unit, inverse):
    first = jnp.mean(weighted, axis=-1, keepdims=True)
    second = jnp.mean(weighted * unit, axis=-1, keepdims=True)
    return inverse * (weighted - first - unit * second)


def lower_half(head):
    lane = lax.broadcasted_iota(jnp.int32, (1, LANES), 1)
    return (lane & (head - 1)) < head // 2


def column_sum(values):
    return jnp.sum(values, axis=0, keepdims=True)


def project_kernel(head, me_ref, hidden, vectors, p0, p1, p2, p3, p4, p5, cosine, sine, adapted, query, key, value, weight):
    @pl.when(pl.program_id(0) == 0)
    def _():
        assemble(me_ref, weight, (p0, p1, p2, p3, p4, p5), 0, 3)

    unit, _ = normalize(hidden[...].astype(FULL))
    low = (unit * vectors[0:1, :] * vectors[1:2, :] + vectors[2:3, :]).astype(LOW)
    adapted[...] = low
    width = low.shape[1]
    cos, sin = cosine[...], sine[...]
    under = lower_half(head)
    signed = jnp.where(under, -sin, sin)
    scale = 1.0 / math.sqrt(head)
    for which, target in enumerate((query, key)):
        part = matmul(low, weight[:, which * width : (which + 1) * width])
        for j in range(width // LANES):
            block = part[:, j * LANES : (j + 1) * LANES]
            turned = jnp.where(
                under,
                pltpu.roll(block, LANES - head // 2, 1),
                pltpu.roll(block, head // 2, 1),
            )
            turned = (block * cos + turned * signed).astype(LOW)
            if which == 0:
                turned = turned * jnp.asarray(scale, LOW)
            target[:, j * LANES : (j + 1) * LANES] = turned
    value[...] = matmul(low, weight[:, 2 * width :]).astype(LOW)


def project(me, hidden, vectors, pieces, cosine, sine, head):
    length, width = hidden.shape
    step = 256
    rows = pl.BlockSpec((step, width), lambda i, _: (i, 0))
    angle = pl.BlockSpec((step, LANES), lambda i, _: (i, 0))
    out = jax.ShapeDtypeStruct((length, width), LOW)
    return call(
        partial(project_kernel, head),
        "project",
        (length // step,),
        [rows, whole(vectors.shape)] + portion(pieces, 0, 3 * width // 8) + [angle, angle],
        [rows] * 4,
        [out] * 4,
        [pltpu.VMEM((width, 3 * width), LOW)],
        2 * length * width * 3 * width,
        (me, hidden, vectors, *pieces, cosine, sine),
        2 * length * width * 8,
    )


def attend_kernel(step, head, me_ref, query, key, value, mixed, logsum):
    lane = lax.broadcasted_iota(jnp.int32, (1, LANES), 1)
    first = lane < head
    keys, values = key[...], value[...]
    zero = jnp.zeros_like(keys)
    split = (jnp.where(first, keys, zero), jnp.where(first, zero, keys))
    for i in range(query.shape[0] // step):
        at = slice(i * step, (i + 1) * step)
        block = query[at, :]
        outs, sums = [], []
        for h in range(2):
            scores = matmul(block, split[h], 1, 1)
            peak = jnp.max(scores, axis=1, keepdims=True)
            expos = jnp.exp(scores - peak)
            total = jnp.sum(expos, axis=1, keepdims=True)
            outs.append(matmul(expos.astype(LOW), values) * (1.0 / total))
            sums.append(peak + jnp.log(total))
        mixed[at, :] = jnp.where(first, outs[0], outs[1]).astype(LOW)
        turned = jnp.where(first, sums[0], sums[1]).T
        logsum[0, 0:1, at] = turned[0:1, :]
        logsum[0, 1:2, at] = turned[head : head + 1, :]


def attend(me, query, key, value, head):
    length, width = query.shape
    pairs = width // LANES
    block = pl.BlockSpec((length, LANES), lambda i, _: (0, i))
    return call(
        partial(attend_kernel, 512, head),
        "attend",
        (pairs,),
        [block] * 3,
        [block, pl.BlockSpec((1, 2, length), lambda i, _: (i, 0, 0))],
        [
            jax.ShapeDtypeStruct((length, width), LOW),
            jax.ShapeDtypeStruct((pairs, 2, length), FULL),
        ],
        [],
        16 * length * length * width,
        (me, query, key, value),
        2 * length * width * 4,
    )


def merge_kernel(me_ref, mixed, hidden, vectors, p0, p1, p2, p3, p4, p5, middle, adapted, weight):
    @pl.when(pl.program_id(0) == 0)
    def _():
        assemble(me_ref, weight, (p0, p1, p2, p3, p4, p5), 0, 1)

    branch = matmul(mixed[...], weight[...])
    mid = hidden[...].astype(FULL) + vectors[0:1, :] * branch
    middle[...] = mid
    unit, _ = normalize(mid)
    adapted[...] = (unit * vectors[1:2, :] * vectors[2:3, :] + vectors[3:4, :]).astype(LOW)


def merge(me, mixed, hidden, vectors, pieces):
    length, width = hidden.shape
    step = 256
    rows = pl.BlockSpec((step, width), lambda i, _: (i, 0))
    return call(
        merge_kernel,
        "merge",
        (length // step,),
        [rows, rows, whole(vectors.shape)] + portion(pieces, 3 * width // 8, width // 8),
        [rows, rows],
        [jax.ShapeDtypeStruct((length, width), FULL), jax.ShapeDtypeStruct((length, width), LOW)],
        [pltpu.VMEM((width, width), LOW)],
        2 * length * width * width,
        (me, mixed, hidden, vectors, *pieces),
        2 * length * width * 6,
    )


def feed_kernel(last, at_ref, adapted, upstream, vectors, lift_bias, p0, p1, p2, p3, *refs):
    if last:
        low_in, grad_in, middle, o0, o1, o2, o3, adapted_grad, sums, liftbias_grad, keep, send = refs[:12]
        grads, pack, lift, turned, lowered_grad, out_sem, lowered, low_got, grad_got, middle_got, sem = refs[12:]
        copies = [
            pltpu.make_async_copy(source, target, sem.at[k])
            for k, (source, target) in enumerate(
                ((low_in, low_got), (grad_in, grad_got), (middle, middle_got))
            )
        ]
        for copy in copies:
            copy.start()
    else:
        lowered, adapted_grad, liftbias_grad, keep, send = refs[:5]
        grads, pack, lift, turned, lowered_grad, out_sem = refs[5:]
    for d, piece in enumerate((p0, p1, p2, p3)):
        pack[pl.ds(at_ref[0] ^ d, 1)] = piece[...][None]
    me = at_ref[0]
    gate = vectors[0:1, :]
    rows = lift.shape[0] // 4
    step = lift.shape[1] // 2

    def leave(j, half):
        at = slice(0, step) if half == 0 else slice(step + (half - 1) * rows, step + half * rows)
        where = (j >> 1) ^ (me >> 1)
        for target, odd in ((keep, 0), (send, 1)):

            @pl.when(((me ^ j) & 1) == odd)
            def _(target=target):
                pltpu.make_async_copy(
                    grads.at[j, at, :], target.at[where, at, :], out_sem.at[j, half]
                ).start()

    def left(j, half):
        at = slice(0, step) if half == 0 else slice(step + (half - 1) * rows, step + half * rows)
        pltpu.make_async_copy(
            grads.at[j, at, :], keep.at[0, at, :], out_sem.at[j, half]
        ).wait()

    turned[...] = adapted[...].T
    lowered_grad[...] = (gate * upstream[...].astype(FULL)).astype(LOW)
    for i in range(2):
        deep = slice(step + i * rows, step + (i + 1) * rows)
        for j in range(4):
            lift[j * rows : (j + 1) * rows, :] = pack[j, deep, :]
        weight_up = lift[...]
        weight_down = jnp.concatenate([pack[2 * i, :step, :], pack[2 * i + 1, :step, :]], axis=0)
        across = slice(2 * i * step, 2 * (i + 1) * step)
        upper = matmul(adapted[...], weight_up) + lift_bias[:, across]
        square = upper * upper
        root = math.sqrt(2.0 / math.pi)
        bent = jnp.tanh(upper * (root + root * 0.044715 * square))
        half = 0.5 + 0.5 * bent
        slope = half + upper * (0.5 - 0.5 * bent * bent) * (root + 3.0 * root * 0.044715 * square)
        active = (upper * half).astype(LOW)
        low_part = matmul(active, weight_down)
        down = lowered_grad[...]
        upper_grad = (matmul(down, weight_down, 1, 1) * slope).astype(LOW)
        grad_part = matmul(upper_grad, weight_up, 1, 1)
        if i == 0:
            lowered[...] = low_part
            adapted_grad[...] = grad_part
        else:
            lowered[...] += low_part
            adapted_grad[...] += grad_part
        liftbias_grad[:, across] = column_sum(upper_grad.astype(FULL))
        drop_part = matmul(active, down, 0, 0).astype(LOW)
        for k in range(2):
            grads[2 * i + k, :step, :] = drop_part[k * step : (k + 1) * step]
            leave(2 * i + k, 0)
        lift_part = matmul(turned[...], upper_grad).astype(LOW)
        for j in range(4):
            grads[j, deep, :] = lift_part[j * rows : (j + 1) * rows]
            leave(j, 1 + i)

    if last:
        for copy in copies:
            copy.wait()
        adapted_grad[...] += grad_got[...]
        total = lowered[...] + low_got[...] + vectors[1:2, :]
        low_got[...] = middle_got[...] + gate * total
        span = o0.shape[0]
        for d, target in enumerate((o0, o1, o2, o3)):
            target[...] = low_got[pl.ds(pl.multiple_of((me ^ d) * span, 16), span), :].astype(LOW)
        sums[0:1, :] = column_sum(upstream[...].astype(FULL) * total)
        sums[1:2, :] = column_sum(lowered_grad[...].astype(FULL))
    for j in range(4):
        for half in range(3):
            left(j, half)


def feed(me, adapted, upstream, vectors, lift_bias, pieces, before=()):
    length, width = adapted.shape
    last = len(before) > 0
    units = lift_bias.shape[1]
    wide = jax.ShapeDtypeStruct((length, width), FULL)
    low = jax.ShapeDtypeStruct((length // 4, width), LOW)
    more = jax.ShapeDtypeStruct((2, units // 2, width), LOW)
    sums = jax.ShapeDtypeStruct((8, width), FULL)
    bias = jax.ShapeDtypeStruct((1, units), FULL)
    outs = [low] * 4 + [wide, sums, bias, more, more] if last else [wide, wide, bias, more, more]
    scratch = [
        pltpu.VMEM((4, units // 2, width), LOW),
        pltpu.VMEM((4, units // 2, width), LOW),
        pltpu.VMEM((width, units // 2), LOW),
        pltpu.VMEM((width, length), LOW),
        pltpu.VMEM((length, width), LOW),
        pltpu.SemaphoreType.DMA((4, 3)),
    ]
    if last:
        scratch += [pltpu.VMEM((length, width), FULL)] * 4 + [pltpu.SemaphoreType.DMA((3,))]
    return call(
        partial(feed_kernel, last),
        "feed",
        (1,),
        [whole(a.shape) for a in (adapted, upstream, vectors, lift_bias, *pieces)]
        + [pl.BlockSpec(memory_space=pl.ANY) for _ in before],
        [whole(o.shape) for o in outs[:-2]] + [pl.BlockSpec(memory_space=pl.ANY)] * 2,
        outs,
        scratch,
        12 * length * width * units,
        (me, adapted, upstream, vectors, lift_bias, *pieces, *before),
        8 * width * units + 24 * length * width,
    )


def unmerge_kernel(
    me_ref, adapted_grad, middle, upstream, mixed, vectors, p0, p1, p2, p3, p4, p5,
    middle_grad, mixed_grad, sums, keep, send, weight, total,
):
    i = pl.program_id(0)

    @pl.when(i == 0)
    def _():
        assemble(me_ref, weight, (p0, p1, p2, p3, p4, p5), 0, 1)
        total[...] = jnp.zeros_like(total)
        sums[...] = jnp.zeros_like(sums)

    gate, gain, grow = vectors[0:1, :], vectors[1:2, :], vectors[2:3, :]
    unit, inverse = normalize(middle[...])
    grad = adapted_grad[...]
    sums[0:1, :] += column_sum(grad)
    sums[1:2, :] += column_sum(grad * (unit * gain))
    normed_grad = grad * grow
    sums[2:3, :] += column_sum(normed_grad * unit)
    mid_grad = upstream[...].astype(FULL) + unnormalize(normed_grad * gain, unit, inverse)
    middle_grad[...] = mid_grad
    low = mixed[...]
    sums[3:4, :] += column_sum(mid_grad * matmul(low, weight[...]))
    branch_grad = (gate * mid_grad).astype(LOW)
    total[...] += matmul(low, branch_grad, 0, 0)
    mixed_grad[...] = matmul(branch_grad, weight[...], 1, 1).astype(LOW)

    @pl.when(i == pl.num_programs(0) - 1)
    def _():
        split_rows(me_ref[0], total[...], keep, send)


def unmerge(me, adapted_grad, middle, upstream, mixed, vectors, pieces):
    length, width = middle.shape
    step = 256
    rows = pl.BlockSpec((step, width), lambda i, _: (i, 0))
    part = (2, width // 4, width)
    return call(
        unmerge_kernel,
        "unmerge",
        (length // step,),
        [rows] * 4 + [whole(vectors.shape)] + portion(pieces, 3 * width // 8, width // 8),
        [rows, rows, kept((8, width)), kept(part), kept(part)],
        [
            jax.ShapeDtypeStruct((length, width), FULL),
            jax.ShapeDtypeStruct((length, width), LOW),
            jax.ShapeDtypeStruct((8, width), FULL),
            jax.ShapeDtypeStruct(part, LOW),
            jax.ShapeDtypeStruct(part, LOW),
        ],
        [pltpu.VMEM((width, width), LOW), pltpu.VMEM((width, width), FULL)],
        6 * length * width * width,
        (me, adapted_grad, middle, upstream, mixed, vectors, *pieces),
        2 * length * width * 12,
    )


def unattend_kernel(step, head, me_ref, query, key, value, mixed, mixed_grad, logsum, cosine, sine, grads, query_sum, key_sum, value_sum):
    lane = lax.broadcasted_iota(jnp.int32, (1, LANES), 1)
    first = lane < head
    keys, values = key[...], value[...]
    zero = jnp.zeros_like(keys)
    keys_h = (jnp.where(first, keys, zero), jnp.where(first, zero, keys))
    values_h = (jnp.where(first, values, zero), jnp.where(first, zero, values))
    turned = keys.T
    scale = 1.0 / math.sqrt(head)
    for i in range(query.shape[0] // step):
        at = slice(i * step, (i + 1) * step)
        block, grad = query[at, :], mixed_grad[at, :]
        product = (grad.astype(FULL) * mixed[at, :].astype(FULL)).T
        queries, values_new, keys_new = [], [], []
        for h in range(2):
            center = jnp.sum(product[h * head : (h + 1) * head], axis=0, keepdims=True)
            probs = jnp.exp(matmul(keys_h[h], block, 1, 1) - logsum[0, h : h + 1, at])
            probs_grad = matmul(values_h[h], grad, 1, 1)
            scores_grad = (probs * (probs_grad - center)).astype(LOW)
            values_new.append(matmul(probs.astype(LOW), grad))
            keys_new.append(matmul(scores_grad, block))
            queries.append(matmul(turned[h * head : (h + 1) * head], scores_grad))
        query_sum[at, :] = jnp.concatenate(queries, axis=0).T * scale
        key_part = jnp.where(first, keys_new[0], keys_new[1])
        value_part = jnp.where(first, values_new[0], values_new[1])
        if i == 0:
            key_sum[...] = key_part
            value_sum[...] = value_part
        else:
            key_sum[...] += key_part
            value_sum[...] += value_part
    under = lower_half(head)
    cos, sin = cosine[...], sine[...]
    for which, total in enumerate((query_sum, key_sum)):
        rotated = total[...]
        swept = rotated * sin
        back = jnp.where(
            under, pltpu.roll(swept, LANES - head // 2, 1), -pltpu.roll(swept, head // 2, 1)
        )
        grads[which] = (rotated * cos + back).astype(LOW)
    grads[2] = value_sum[...].astype(LOW)


def unattend(me, query, key, value, mixed, mixed_grad, logsum, cosine, sine, head, start, pairs):
    length = mixed.shape[0]
    width = pairs * LANES
    block = pl.BlockSpec((length, LANES), lambda i, _: (0, i + start))
    own = pl.BlockSpec((length, LANES), lambda i, _: (0, i))
    return call(
        partial(unattend_kernel, 256, head),
        "unattend",
        (pairs,),
        [block] * 5
        + [pl.BlockSpec((1, 2, length), lambda i, _: (i + start, 0, 0))]
        + [whole((length, LANES))] * 2,
        [pl.BlockSpec((3, length, LANES), lambda i, _: (0, 0, i))],
        [jax.ShapeDtypeStruct((3, length, width), LOW)],
        [pltpu.VMEM((length, LANES), FULL)] * 3,
        40 * length * length * width,
        (me, query, key, value, mixed, mixed_grad, logsum, cosine, sine),
        2 * length * width * 8,
    )[0]


def weigh_kernel(me_ref, adapted, grads, *refs):
    keep, send, turned = refs[-3:]
    i = pl.program_id(0)

    @pl.when(i == 0)
    def _():
        turned[...] = adapted[...].T

    @pl.when(i < 3)
    def _():
        split_rows(me_ref[0], matmul(turned[...], grads[0]), keep, send)

    if len(refs) > 3:

        @pl.when(i >= 3)
        def _():
            keep[...] = refs[0][...]
            send[...] = refs[1][...]


def weigh(me, adapted, grads, extra=()):
    length, width = adapted.shape
    step = grads.shape[2]
    more = extra[0].shape[2] // step if extra else 0
    part = pl.BlockSpec((2, width // 4, step), lambda i, _: (0, 0, i))
    rider = pl.BlockSpec((2, width // 4, step), lambda i, _: (0, 0, jnp.maximum(i - 3, 0)))
    shape = jax.ShapeDtypeStruct((2, width // 4, (3 + more) * step), LOW)
    return call(
        weigh_kernel,
        "weigh",
        (3 + more,),
        [whole(adapted.shape), pl.BlockSpec((1, length, step), lambda i, _: (jnp.minimum(i, 2), 0, 0))]
        + [rider] * len(extra),
        [part, part],
        [shape, shape],
        [pltpu.VMEM((width, length), LOW)],
        6 * length * width * step,
        (me, adapted, grads, *extra),
        2 * length * width * 7,
    )


def unproject_kernel(me_ref, g0, g1, hidden, middle_grad, vectors, p0, p1, p2, p3, p4, p5, o0, o1, o2, o3, sums, weight):
    i = pl.program_id(0)

    @pl.when(i == 0)
    def _():
        assemble(me_ref, weight, (p0, p1, p2, p3, p4, p5), 0, 3)
        sums[...] = jnp.zeros_like(sums)

    gain, grow = vectors[0:1, :], vectors[1:2, :]
    width = hidden.shape[1]
    grad, at = None, 0
    for part in (g0, g1):
        size = part.shape[2]
        for which in range(3):
            low = which * width + at
            term = matmul(part[which], weight[:, low : low + size], 1, 1)
            grad = term if grad is None else grad + term
        at += size
    unit, inverse = normalize(hidden[...].astype(FULL))
    sums[0:1, :] += column_sum(grad)
    sums[1:2, :] += column_sum(grad * (unit * gain))
    normed_grad = grad * grow
    sums[2:3, :] += column_sum(normed_grad * unit)
    low = (middle_grad[...] + unnormalize(normed_grad * gain, unit, inverse)).astype(LOW)
    for d, target in enumerate((o0, o1, o2, o3)):

        @pl.when(i == me_ref[0] ^ d)
        def _(target=target):
            target[...] = low


def unproject(me, grads, hidden, middle_grad, vectors, pieces):
    length, width = hidden.shape
    step = length // 4
    rows = pl.BlockSpec((step, width), lambda i, _: (i, 0))
    return call(
        unproject_kernel,
        "unproject",
        (length // step,),
        [pl.BlockSpec((3, step, g.shape[2]), lambda i, _: (0, i, 0)) for g in grads]
        + [rows, rows, whole(vectors.shape)]
        + portion(pieces, 0, 3 * width // 8),
        [kept((step, width))] * 4 + [kept((8, width))],
        [jax.ShapeDtypeStruct((step, width), LOW)] * 4 + [jax.ShapeDtypeStruct((8, width), FULL)],
        [pltpu.VMEM((width, 3 * width), LOW)],
        6 * length * width * width,
        (me, *grads, hidden, middle_grad, vectors, *pieces),
        2 * length * width * 10,
    )


def lay_kernel(me_ref, *refs):
    for d, part in enumerate(refs[:-1]):
        refs[-1][pl.ds(me_ref[0] ^ d, 1)] = part[...][None]


def lay(me, parts):
    shape = (len(parts),) + parts[0].shape
    return call(
        lay_kernel, "lay", (1,), [whole(p.shape) for p in parts], [whole(shape)],
        [jax.ShapeDtypeStruct(shape, LOW)], [], 1024, (me, *parts), 1024,
    )[0]


def finish_kernel(
    seqs, columns, depth, me_ref, parts, others, heads, merges, modulate, modulate_bias, up, down, one, two, table
):
    half, rows = parts.shape[0], parts.shape[1] - 8
    size = 2 * half
    wide = parts.shape[2] // 2
    width = merges.shape[1]
    part = width // 2
    for p in range(size):
        at = slice(p * rows, (p + 1) * rows)
        value = jnp.where(
            me_ref[1] == p // half, parts[p % half, 8:, :], others[p % half, 8:, :]
        ).astype(FULL)
        for k in range(3):
            heads[at, k * width : k * width + part] = value[:, k * part : (k + 1) * part]
            heads[at, k * width + part : (k + 1) * width] = value[:, (5 + k) * part : (6 + k) * part]
        merges[at, :] = value[:, 3 * part : 5 * part]
    small = jnp.concatenate(
        [
            source[p, :8, :wide].astype(FULL) + source[p, :8, wide:].astype(FULL)
            for source in (parts, others)
            for p in range(half)
        ],
        axis=0,
    )
    row = lax.broadcasted_iota(jnp.int32, (8 * size, 1), 0) & 7
    mine = row < seqs
    zero = jnp.zeros((), FULL)
    grads = jnp.where(mine, small[:, :columns], zero)
    conds = jnp.where(mine, small[:, columns : columns + depth], zero)
    conds_grad = jnp.where(mine, small[:, columns + depth : columns + 2 * depth], zero)
    steps = small[:, columns + 2 * depth : columns + 2 * depth + 1].astype(jnp.int32)

    def exact(left, right):
        dims = (((0,), (0,)), ((), ()))
        return lax.dot_general(
            left, right, dims, precision=lax.Precision.HIGHEST, preferred_element_type=FULL
        )

    modulate[...] = exact(grads, conds)
    modulate_bias[...] = column_sum(grads)[0]
    ends = column_sum(jnp.where(row == seqs, small, zero))
    at = 0
    for target in (up, down, one, two):
        size = target.shape[0]
        target[...] = ends[0, at : at + size]
        at += size
    share = table.shape[0]
    own = me_ref[0] * share + lax.broadcasted_iota(jnp.int32, (1, share), 1)
    table[...] = exact(jnp.where(mine & (steps == own), 1.0, 0.0), conds_grad)


def finish(me, parts, others, width, columns, depth, sizes, share):
    shapes = [(width // 4, 3 * width), (width // 4, width), (columns, depth), (columns,)]
    shapes += [(size,) for size in sizes] + [(share, depth)]
    return call(
        partial(finish_kernel, 4, columns, depth), "finish", (1,), [whole(parts.shape)] * 2,
        [whole(s) for s in shapes], [jax.ShapeDtypeStruct(s, FULL) for s in shapes], [], 1024,
        (me, parts, others), 1024,
    )


def swap(array, axis, distance):
    size = lax.axis_size(axis)
    return lax.ppermute(array, axis, [(i, i ^ distance) for i in range(size)])


def fence(*trees):
    return lax.optimization_barrier(trees)


def bit(axis, distance):
    return (lax.axis_index(axis) // distance) % 2


def choose(parts, at):
    return lax.dynamic_index_in_dim(parts, at, 0, keepdims=False)


def choose_all(array, place):
    count = array.shape[0]
    return jnp.stack([choose(array, place ^ k) for k in range(count)])


def payload(parts):
    return jnp.concatenate([p.reshape(2, p.shape[0] // 2, p.shape[1]) for p in parts], axis=1)


def blocks_of(weight, width):
    return [weight[:, k : k + width] for k in range(0, weight.shape[1], width)]


def powers(size):
    return [1 << k for k in range(size.bit_length() - 1)]


def plus(*terms):
    total = terms[0].astype(FULL)
    for term in terms[1:]:
        total = total + term.astype(FULL)
    return total.astype(LOW)


def pair_kernel(at_ref, kept_term, got, mine, other):
    mine[...] = plus(kept_term[0], got[0])
    other[...] = plus(kept_term[1], got[1])


def sum_pair(kept_term, got):
    _, rows, columns = kept_term.shape
    step = rows // 4
    two = pl.BlockSpec((2, step, columns), lambda i, _: (0, i, 0))
    one = pl.BlockSpec((step, columns), lambda i, _: (i, 0))
    out = jax.ShapeDtypeStruct((rows, columns), LOW)
    return call(
        pair_kernel, "pair", (4,), [two, two], [one, one], [out, out], [], 1024,
        (jnp.zeros((1,), jnp.int32), kept_term, got), 1024,
    )


def two_kernel(at_ref, first, second, total):
    total[...] = plus(first[...], second[...])


def sum_two(first, second):
    rows, columns = first.shape
    steps = 2 if rows % 32 == 0 else 1
    spec = pl.BlockSpec((rows // steps, columns), lambda i, _: (i, 0))
    return call(
        two_kernel, "two", (steps,), [spec] * 2, [spec],
        [jax.ShapeDtypeStruct((rows, columns), LOW)], [], 1 << 33,
        (jnp.zeros((1,), jnp.int32), first, second), 1 << 24,
    )[0]


def beside_kernel(at_ref, a, b, c, d, mine, other):
    cut = a.shape[2]
    for target, at in ((mine, at_ref[0]), (other, 1 - at_ref[0])):
        at = pl.ds(at, 1)
        target[:, :cut] = plus(a[at], b[at])[0]
        target[:, cut:] = plus(c[at], d[at])[0]


def split_beside(first, second):
    args = [a.reshape(2, -1, a.shape[1]) for a in (*first, *second)]
    rows = args[0].shape[1]
    out = (rows, args[0].shape[2] + args[2].shape[2])
    return call(
        beside_kernel, "beside", (1,), [whole(a.shape) for a in args], [whole(out)] * 2,
        [jax.ShapeDtypeStruct(out, LOW)] * 2, [], 1024, (place_of(1), *args), 1024,
    )


def terms_kernel(at_ref, small, parts, total):
    value = plus(*[parts[k] for k in range(parts.shape[0])])
    for k in range(total.shape[0]):
        total[k, :8, :] = small[...]
        total[k, 8:, :] = value


def gather_terms(small, parts):
    shape = (parts.shape[0], 8 + parts.shape[1], small.shape[1])
    return call(
        terms_kernel, "terms", (1,), [whole(small.shape), whole(parts.shape)], [whole(shape)],
        [jax.ShapeDtypeStruct(shape, LOW)], [], 1024, (jnp.zeros((1,), jnp.int32), small, parts), 1024,
    )[0]


def exchange(parts):
    size = lax.axis_size("dp")
    groups = None
    if parts.shape[0] < size:
        groups = [list(range(b, size, 2)) for b in range(2)]
    return lax.all_to_all(parts, "dp", 0, 0, axis_index_groups=groups, tiled=True)


def deal(term, size=None):
    size = size or lax.axis_size("dp")
    rows, columns = term.shape
    return exchange(term.reshape(size, rows // size, columns))


def add_kernel(at_ref, parts, total):
    total[...] = plus(*[parts[k] for k in range(parts.shape[0])])


def add_up(parts):
    shape = parts.shape[1:]
    return call(
        add_kernel, "add", (1,), [whole(parts.shape)], [whole(shape)],
        [jax.ShapeDtypeStruct(shape, LOW)], [], 1 << 33, (jnp.zeros((1,), jnp.int32), parts), 1 << 24,
    )[0]


def place_of(distance):
    return bit("dp", distance).astype(jnp.int32).reshape(1)


def join_kernel(at_ref, first, second, both):
    b = at_ref[0]
    both[pl.ds(b, 1)] = first[...][None]
    both[pl.ds(1 - b, 1)] = second[...][None]


def join(first, second, distance):
    rows, columns = first.shape
    shape = (2, rows, columns)
    return call(
        join_kernel, "join", (1,), [whole(first.shape)] * 2, [whole(shape)],
        [jax.ShapeDtypeStruct(shape, LOW)], [], 1024, (place_of(distance), first, second), 1024,
    )[0].reshape(2 * rows, columns)


def settle_kernel(plan, size, at_ref, *refs):
    count = len(plan)
    outs = refs[2 * count :]
    depth = size.bit_length() - 1
    b = at_ref[0]
    for p, moves in enumerate(plan):
        rows = 2 * refs[2 * p].shape[0] // size
        for h in range(2):
            value = jnp.where(b == h, refs[2 * p][...], refs[2 * p + 1][...]).astype(FULL)
            for k in range(h, size, 2):
                at = sum(((k >> j) & 1) << (depth - 1 - j) for j in range(1, depth)) * rows
                for top, left, down, wide, out, to_row, to_column in moves:
                    low, high = max(top, k * rows), min(top + down, (k + 1) * rows)
                    if low < high:
                        start = to_row + low - top
                        source = at + low - k * rows
                        outs[out][start : start + high - low, to_column : to_column + wide] = value[
                            source : source + high - low, left : left + wide
                        ]


def settle(pairs, plan, shapes):
    args = [array for pair in pairs for array in pair]
    return call(
        partial(settle_kernel, plan, lax.axis_size("dp")),
        "settle",
        (1,),
        [whole(a.shape) for a in args],
        [whole(shape) for shape in shapes],
        [jax.ShapeDtypeStruct(shape, FULL) for shape in shapes],
        [],
        1024,
        (place_of(1), *args),
        1024,
    )


def shards(
    hidden_in,
    time_table,
    time_step,
    token_pos,
    heads_weight,
    merge_weight,
    lift_weight,
    lift_bias,
    drop_weight,
    drop_bias,
    modulate_weight,
    modulate_bias,
    first_gain,
    second_gain,
    out_grad,
):
    count = lax.axis_size("seq")
    place = lax.axis_index("seq")
    seqs, span, width = hidden_in.shape
    assert count == 4 and seqs == count
    length = span * count
    head = width // HEADS
    bits = powers(lax.axis_size("dp"))
    row_half = bit("dp", 1)
    me = jnp.stack([place, row_half]).astype(jnp.int32)

    units = drop_weight.shape[0]
    step = units // 2
    heads_pack = payload(blocks_of(heads_weight, width) + [merge_weight])
    heads_half = choose(heads_pack, row_half)
    heads_half, time_step = fence(heads_half, time_step)
    heads_across = swap(heads_half, "seq", 2)

    def feed_pack(h):
        columns = [lift_weight[:, j * units + h * step : j * units + (h + 1) * step] for j in range(4)]
        blocks = [jnp.concatenate(columns[k : k + 2], axis=1) for k in (0, 2)]
        return jnp.concatenate([drop_weight[h * step : (h + 1) * step]] + blocks, axis=0)

    table_rows, depth = time_table.shape
    chosen_rows = (time_step[:, None] == jnp.arange(table_rows, dtype=jnp.int32)[None, :]).astype(LOW)
    conds = jnp.dot(chosen_rows, time_table, preferred_element_type=FULL)
    modulation = matmul(conds.astype(LOW), modulate_weight, 1, 1) + modulate_bias.astype(FULL)
    columns = modulation.shape[1]
    vectors = [v.astype(FULL) for v in (lift_bias, drop_bias, first_gain, second_gain)]
    above = jnp.concatenate([modulation, token_pos.astype(FULL)], axis=1)
    below = jnp.concatenate(vectors)[None]
    below = jnp.pad(below, ((0, 0), (0, above.shape[1] - below.shape[1])))
    small = jnp.concatenate([above, below], axis=0)
    small_across = swap(small, "seq", 2)
    hidden_in, small = fence(hidden_in, small)
    heads_across, small, lift_weight, drop_weight = fence(
        heads_across, small, lift_weight, drop_weight
    )
    heads_handed = swap(heads_across, "dp", 1)
    heads_core = swap(heads_pack, "seq", 1), swap(heads_across, "seq", 1)
    hidden = lax.all_to_all(hidden_in, "seq", 0, 0, tiled=True).reshape(length, width)
    small = jnp.stack([small, small_across])
    small_core = swap(small, "seq", 1)
    small = jnp.stack([small[0], small_core[0], small[1], small_core[1]])
    small = choose_all(small, place)
    heads = (
        heads_pack,
        heads_core[0],
        heads_across,
        heads_handed,
        heads_core[1],
        swap(heads_handed, "seq", 1),
    )
    mine = lax.dynamic_index_in_dim(small, place, 1, keepdims=False)
    chosen = mine[:, :columns].reshape(6, width)
    positions = mine[:, columns:].reshape(length)
    rest = small[:, seqs]
    sizes = (lift_bias.shape[0], drop_bias.shape[0], first_gain.shape[0], second_gain.shape[0])
    vectors, at = [], 0
    for size in sizes:
        vectors.append(rest[:, at : at + size].reshape(1, -1))
        at += size
    up_bias, down_bias, gain_one, gain_two = vectors
    shift_a, scale_a, gate_a, shift_b, scale_b, gate_b = [chosen[k : k + 1] for k in range(6)]
    grow_a, grow_b = 1.0 + scale_a, 1.0 + scale_b

    def rows(*items):
        blank = jnp.zeros((8 - len(items), width), FULL)
        return jnp.concatenate(items + (blank,), axis=0)

    freqs = 10000.0 ** (-jnp.arange(0, head, 2, dtype=FULL) / head)
    freqs = jnp.tile(freqs, 2 * LANES // head)
    angles = positions[:, None] * freqs
    cosine, sine = jnp.cos(angles), jnp.sin(angles)

    pack_0, pack_1 = feed_pack(0), feed_pack(1)
    hidden, heads, cosine, sine, pack_0, pack_1, out_grad = fence(
        hidden, heads, cosine, sine, pack_0, pack_1, out_grad
    )
    across_0 = swap(pack_0, "seq", 2)
    core_0, core_1 = swap(pack_0, "seq", 1), swap(pack_1, "seq", 1)
    adapted_a, query, key, value = project(
        me, hidden, rows(gain_one, grow_a, shift_a), heads, cosine, sine, head
    )
    merge_vectors, unmerge_vectors = rows(gate_a, gain_two, grow_b, shift_b), rows(gate_a, gain_two, grow_b)
    feed_vectors = rows(gate_b, down_bias)
    bias_0, bias_1 = [up_bias.reshape(4, 2, step)[:, h].reshape(1, 4 * step) for h in range(2)]
    query, merge_vectors, unmerge_vectors, feed_vectors, bias_0, bias_1 = fence(
        query, merge_vectors, unmerge_vectors, feed_vectors, bias_0, bias_1
    )
    query, out_grad = fence(query, out_grad)
    upstream = lax.all_to_all(out_grad, "seq", 0, 0, tiled=True).reshape(length, width)
    mixed, logsum = attend(me, query, key, value, head)
    mixed, logsum, across_0 = fence(mixed, logsum, across_0)
    other_0 = swap(across_0, "seq", 1)
    middle, adapted_b = merge(me, mixed, hidden, merge_vectors, heads)
    middle, adapted_b, core_0, other_0, upstream = fence(
        middle, adapted_b, core_0, other_0, upstream
    )
    pairs = width // LANES // 2
    adapted_b, upstream, pack_1, core_1 = fence(adapted_b, upstream, pack_1, core_1)
    across_1 = swap(pack_1, "seq", 2)
    lowered, grad, liftbias_0, keep_0, send_0 = feed(
        me, adapted_b, upstream, feed_vectors, bias_0, (pack_0, core_0, across_0, other_0)
    )
    lowered, grad, liftbias_0, keep_0, send_0, across_1 = fence(
        lowered, grad, liftbias_0, keep_0, send_0, across_1
    )
    other_1 = swap(across_1, "seq", 1)
    got_0 = swap(send_0, "seq", 1)
    *out_parts, adapted_b_grad, feed_sums, liftbias_1, keep_1, send_1 = feed(
        me, adapted_b, upstream, feed_vectors, bias_1, (pack_1, core_1, across_1, other_1),
        (lowered, grad, middle),
    )
    back = bits[::-1]
    last = len(back) - 1
    out_parts, adapted_b_grad, feed_sums, liftbias_1, keep_1, send_1, got_0 = fence(
        out_parts, adapted_b_grad, feed_sums, liftbias_1, keep_1, send_1, got_0
    )
    got_1 = swap(send_1, "seq", 1)
    adapted_b_grad, (mine_0, other_0) = fence(adapted_b_grad, sum_pair(keep_0, got_0))
    got_0 = swap(other_0, "seq", 2)
    middle_grad, mixed_grad, merge_sums, merge_keep, merge_send = unmerge(
        me, adapted_b_grad, middle, upstream, mixed, unmerge_vectors, heads
    )
    middle_grad, mixed_grad, merge_sums, merge_keep, merge_send, got_1 = fence(
        middle_grad, mixed_grad, merge_sums, merge_keep, merge_send, got_1
    )
    mixed_grad, (mine_1, other_1) = fence(mixed_grad, sum_pair(keep_1, got_1))
    got_1 = swap(other_1, "seq", 2)
    heads_0 = unattend(
        me, query, key, value, mixed, mixed_grad, logsum, cosine, sine, head, 0, pairs
    )
    heads_0, got_0 = fence(heads_0, got_0)
    heads_0, term_0 = fence(heads_0, sum_two(mine_0, got_0))
    parts_0 = deal(term_0)
    keep_2, send_2 = weigh(me, adapted_a, heads_0, (merge_keep, merge_send))
    mixed_grad, keep_2, send_2 = fence(mixed_grad, keep_2, send_2)
    got_2 = swap(send_2, "seq", 1)
    heads_1 = unattend(
        me, query, key, value, mixed, mixed_grad, logsum, cosine, sine, head, pairs, pairs
    )
    heads_1, got_1 = fence(heads_1, got_1)
    heads_1, term_1, parts_0 = fence(heads_1, sum_two(mine_1, got_1), parts_0)
    parts_1 = deal(term_1)
    heads_1, got_2 = fence(heads_1, got_2)
    heads_1, (mine_2, other_2) = fence(heads_1, sum_pair(keep_2, got_2))
    got_2 = swap(other_2, "seq", 2)
    keep_3, send_3 = weigh(me, adapted_a, heads_1)
    keep_3, send_3, parts_0 = fence(keep_3, send_3, parts_0)
    got_3 = swap(send_3, "seq", 1)
    term_0, got_3 = fence(add_up(parts_0), got_3)
    heads_1, term_0, (mine_3, other_3) = fence(heads_1, term_0, sum_pair(keep_3, got_3))
    got_3 = swap(other_3, "seq", 2)
    got_0 = swap(term_0, "dp", back[0])
    *input_parts, project_sums = unproject(
        me, (heads_0, heads_1), hidden, middle_grad, rows(gain_one, grow_a), heads
    )
    input_parts, project_sums, got_2, got_3, parts_1 = fence(
        input_parts, project_sums, got_2, got_3, parts_1
    )
    (mine_a, other_a), input_parts, project_sums, parts_1, got_0 = fence(
        split_beside((mine_2, got_2), (mine_3, got_3)), input_parts, project_sums, parts_1, got_0
    )
    got_a = swap(other_a, "dp", 1)
    liftbias_grad = jnp.stack([liftbias_0.reshape(4, step), liftbias_1.reshape(4, step)], axis=1)
    modulation_grad = jnp.concatenate(
        [project_sums[0:2], merge_sums[3:4], merge_sums[0:2], feed_sums[0:1]], axis=0
    ).reshape(count, columns)
    small = jnp.concatenate(
        [
            modulation_grad,
            liftbias_grad.reshape(count, -1),
            feed_sums[1].reshape(count, -1),
            project_sums[2].reshape(count, -1),
            merge_sums[2].reshape(count, -1),
        ],
        axis=1,
    )
    parts = [choose(small, place ^ d) for d in range(4)]
    term_1, term_0, parts = fence(add_up(parts_1), join(term_0, got_0, back[0]), parts)
    got_1 = swap(term_1, "dp", back[0])
    got_0 = swap(term_0, "dp", back[1])
    parts = [swap(part, "seq", d) if d else part for d, part in enumerate(parts)]
    input_parts, parts = fence(input_parts, parts)
    input_parts = [swap(part, "seq", d) if d else part for d, part in enumerate(input_parts)]
    mine_a, got_a, parts_1 = fence(mine_a, got_a, parts_1)
    mine_a, got_a, got_1, got_0, parts = fence(mine_a, got_a, got_1, got_0, parts)
    term_a, got_0, got_1, parts, out_parts = fence(
        sum_two(mine_a, got_a), got_0, got_1, parts, out_parts
    )
    parts_a = deal(term_a, lax.axis_size("dp") // 2)
    term_0, term_1 = join(term_0, got_0, back[1]), join(term_1, got_1, back[0])
    for k in range(2, last):
        term_0 = join(term_0, swap(term_0, "dp", back[k]), back[k])
    got_0 = swap(term_0, "dp", back[-1])
    got_1 = swap(term_1, "dp", back[1])
    small = choose_all(jnp.stack(parts), place)
    exact = lax.Precision.HIGHEST
    conds_grad = jnp.einsum(
        "sm,mc->sc", small[:, :columns], modulate_weight.astype(FULL), precision=exact
    )
    conds_grad = sum([swap(conds_grad, "seq", d) for d in (1, 2, 3)], conds_grad)
    spare = term_a.shape[1] // 2 - columns - 2 * depth
    above = jnp.concatenate(
        [
            small[:, :columns],
            conds,
            conds_grad,
            jnp.broadcast_to(time_step.astype(FULL)[:, None], (seqs, spare)),
        ],
        axis=1,
    )
    below = jnp.sum(small[:, columns:], axis=0)[None]
    below = jnp.pad(below, ((0, 7 - seqs), (0, above.shape[1] - below.shape[1])))
    small = jnp.concatenate([above, below], axis=0)
    upper = lax.reduce_precision(small, 8, 7)
    small = jnp.concatenate([upper, small - upper], axis=1).astype(LOW)
    small, input_parts = fence(small, input_parts)
    input_grad = lay(me, input_parts)
    small, parts_a = fence(small, parts_a)
    small, parts_a, got_1, got_0, out_parts, input_grad = fence(
        small, parts_a, got_1, got_0, out_parts, input_grad
    )
    term_a, got_1, input_grad, out_parts = fence(
        gather_terms(small, parts_a), got_1, input_grad, out_parts
    )
    parts_a = exchange(term_a)
    term_1 = join(term_1, got_1, back[1])
    for k in range(2, last):
        term_1 = join(term_1, swap(term_1, "dp", back[k]), back[k])
    got_1 = swap(term_1, "dp", back[-1])
    out_parts = [swap(part, "seq", d) if d else part for d, part in enumerate(out_parts)]
    parts_a, got_1 = fence(parts_a, got_1)
    parts_a, got_1, out_parts, input_grad = fence(parts_a, got_1, out_parts, input_grad)
    got_a = swap(parts_a, "dp", 1)
    block_out = lay(me, out_parts)
    pair_0, pair_1 = (term_0, got_0), (term_1, got_1)
    deep = width // 4
    drop_grad, lift_grad = settle(
        [pair_0, pair_1],
        [
            [(0, 0, step, width, 0, h * step, 0)]
            + [
                (step + (j >> 1) * deep, (j & 1) * step, deep, step, 1, 0, j * units + h * step)
                for j in range(4)
            ]
            for h in range(2)
        ],
        [drop_weight.shape, lift_weight.shape],
    )
    block_out, input_grad, drop_grad, lift_grad, parts_a, got_a = fence(
        block_out, input_grad, drop_grad, lift_grad, parts_a, got_a
    )
    share = table_rows // count
    (
        heads_grad, merge_grad, modulate_grad, modulatebias_grad,
        liftbias_out, dropbias_out, firstgain_out, secondgain_out, table_grad,
    ) = finish(me, parts_a, got_a, width, columns, depth, sizes, share)
    return (
        block_out,
        input_grad,
        heads_grad,
        merge_grad,
        lift_grad,
        liftbias_out,
        drop_grad,
        dropbias_out,
        modulate_grad,
        modulatebias_grad,
        firstgain_out,
        secondgain_out,
        table_grad,
    )


def solution(mesh):
    return jax.shard_map(
        shards,
        mesh=mesh,
        in_specs=(
            P("dp", "seq", None),
            P(),
            P("dp"),
            P("dp", "seq"),
            P("seq", None),
            P("seq", None),
            P("seq", None),
            P("seq"),
            P("seq", None),
            P("seq"),
            P("seq", None),
            P("seq"),
            P("seq"),
            P("seq"),
            P("dp", "seq", None),
        ),
        out_specs=(
            P("dp", "seq", None),
            P("dp", "seq", None),
            P("seq", None),
            P("seq", None),
            P("seq", None),
            P("seq"),
            P("seq", None),
            P("seq"),
            P("seq", None),
            P("seq"),
            P("seq"),
            P("seq"),
            P("seq", None),
        ),
        check_vma=False,
    )
```

```python
from functools import partial
import math

import jax
import jax.numpy as jnp
from jax import lax
from jax.experimental import pallas as pl
from jax.experimental.pallas import tpu as pltpu
from jax.sharding import PartitionSpec as P

HEADS = 12
EPSILON = 1e-05
LANES = 128
VMEM = 60 * 1024 * 1024
LOW = jnp.bfloat16
FULL = jnp.float32


def matmul(left, right, left_dim=1, right_dim=0):
    dims = (((left_dim,), (right_dim,)), ((), ()))
    return lax.dot_general(left, right, dims, preferred_element_type=FULL)


def call(body, name, grid, in_specs, out_specs, out_shape, scratch, flops, args, moved):
    return pl.pallas_call(
        body,
        name=name,
        grid_spec=pltpu.PrefetchScalarGridSpec(
            num_scalar_prefetch=1,
            grid=grid,
            in_specs=in_specs,
            out_specs=out_specs,
            scratch_shapes=scratch,
        ),
        out_shape=out_shape,
        compiler_params=pltpu.CompilerParams(
            dimension_semantics=("arbitrary",) * len(grid), vmem_limit_bytes=VMEM
        ),
        cost_estimate=pl.CostEstimate(flops=flops, bytes_accessed=moved, transcendentals=0)
        if name in ("feed", "two", "add")
        else pl.CostEstimate(flops=1024, bytes_accessed=1024, transcendentals=0),
    )(*args)


def whole(shape):
    zeros = (0,) * len(shape)
    return pl.BlockSpec(shape, lambda *_: zeros, pipeline_mode=pl.Buffered(1))


def kept(shape):
    zeros = (0,) * len(shape)
    return pl.BlockSpec(shape, lambda *_: zeros)


def assemble(at, target, pieces, start, blocks):
    me, b = at[0], at[1]
    own, core, across, handed, core_across, core_handed = pieces
    rows = target.shape[0] // 8
    width = target.shape[1] // blocks
    halves = (
        (me, 0, lambda cut: own[0, cut, :]),
        (me, 1, lambda cut: own[1, cut, :]),
        (me ^ 1, 0, lambda cut: core[0, cut, :]),
        (me ^ 1, 1, lambda cut: core[1, cut, :]),
        (me ^ 2, b, lambda cut: across[cut, :]),
        (me ^ 2, 1 - b, lambda cut: handed[cut, :]),
        (me ^ 3, b, lambda cut: core_across[cut, :]),
        (me ^ 3, 1 - b, lambda cut: core_handed[cut, :]),
    )
    for shard, half, read in halves:
        place = pl.ds(pl.multiple_of((2 * shard + half) * rows, 16), rows)
        for k in range(blocks):
            cut = slice(start + k * rows, start + (k + 1) * rows)
            target[place, k * width : (k + 1) * width] = read(cut)


def portion(pieces, start, size):
    at = start // size
    return [
        pl.BlockSpec(
            p.shape[:-2] + (size, p.shape[-1]),
            partial(lambda n, *_: (0,) * n + (at, 0), len(p.shape) - 2),
            pipeline_mode=pl.Buffered(1),
        )
        for p in pieces
    ]


def split_rows(me, value, keep, send):
    rows = value.shape[0] // 4
    mine_x, mine_c = me >> 1, me & 1
    for j in range(4):
        part = value[j * rows : (j + 1) * rows].astype(LOW)[None]
        at = (j >> 1) ^ mine_x

        @pl.when(mine_c == (j & 1))
        def _(part=part, at=at):
            keep[pl.ds(at, 1)] = part

        @pl.when(mine_c != (j & 1))
        def _(part=part, at=at):
            send[pl.ds(at, 1)] = part


def normalize(values):
    center = values - jnp.mean(values, axis=-1, keepdims=True)
    inverse = lax.rsqrt(jnp.mean(center * center, axis=-1, keepdims=True) + EPSILON)
    return center * inverse, inverse


def unnormalize(weighted, unit, inverse):
    first = jnp.mean(weighted, axis=-1, keepdims=True)
    second = jnp.mean(weighted * unit, axis=-1, keepdims=True)
    return inverse * (weighted - first - unit * second)


def lower_half(head):
    lane = lax.broadcasted_iota(jnp.int32, (1, LANES), 1)
    return (lane & (head - 1)) < head // 2


def column_sum(values):
    return jnp.sum(values, axis=0, keepdims=True)


def project_kernel(head, me_ref, hidden, vectors, p0, p1, p2, p3, p4, p5, cosine, sine, turned, query, key, value, weight):
    @pl.when(pl.program_id(0) == 0)
    def _():
        assemble(me_ref, weight, (p0, p1, p2, p3, p4, p5), 0, 3)

    unit, _ = normalize(hidden[...].astype(FULL))
    low = (unit * vectors[0:1, :] * vectors[1:2, :] + vectors[2:3, :]).astype(LOW)
    turned[...] = low.T
    width = low.shape[1]
    cos, sin = cosine[...], sine[...]
    under = lower_half(head)
    signed = jnp.where(under, -sin, sin)
    scale = 1.0 / math.sqrt(head)
    for which, target in enumerate((query, key)):
        part = matmul(low, weight[:, which * width : (which + 1) * width])
        for j in range(width // LANES):
            block = part[:, j * LANES : (j + 1) * LANES]
            turned = jnp.where(
                under,
                pltpu.roll(block, LANES - head // 2, 1),
                pltpu.roll(block, head // 2, 1),
            )
            turned = (block * cos + turned * signed).astype(LOW)
            if which == 0:
                turned = turned * jnp.asarray(scale, LOW)
            target[:, j * LANES : (j + 1) * LANES] = turned
    value[...] = matmul(low, weight[:, 2 * width :]).astype(LOW)


def project(me, hidden, vectors, pieces, cosine, sine, head):
    length, width = hidden.shape
    step = 512
    rows = pl.BlockSpec((step, width), lambda i, _: (i, 0))
    angle = pl.BlockSpec((step, LANES), lambda i, _: (i, 0))
    out = jax.ShapeDtypeStruct((length, width), LOW)
    return call(
        partial(project_kernel, head),
        "project",
        (length // step,),
        [rows, whole(vectors.shape)] + portion(pieces, 0, 3 * width // 8) + [angle, angle],
        [pl.BlockSpec((width, step), lambda i, _: (0, i))] + [rows] * 3,
        [jax.ShapeDtypeStruct((width, length), LOW)] + [out] * 3,
        [pltpu.VMEM((width, 3 * width), LOW)],
        2 * length * width * 3 * width,
        (me, hidden, vectors, *pieces, cosine, sine),
        2 * length * width * 8,
    )


def attend_kernel(step, head, me_ref, query, key, value, mixed, logsum):
    lane = lax.broadcasted_iota(jnp.int32, (1, LANES), 1)
    first = lane < head
    keys, values = key[...], value[...]
    zero = jnp.zeros_like(keys)
    split = (jnp.where(first, keys, zero), jnp.where(first, zero, keys))
    for i in range(query.shape[0] // step):
        at = slice(i * step, (i + 1) * step)
        block = query[at, :]
        outs, sums = [], []
        for h in range(2):
            scores = matmul(block, split[h], 1, 1)
            peak = jnp.max(scores, axis=1, keepdims=True)
            expos = jnp.exp(scores - peak)
            total = jnp.sum(expos, axis=1, keepdims=True)
            outs.append(matmul(expos.astype(LOW), values) * (1.0 / total))
            sums.append(peak + jnp.log(total))
        mixed[at, :] = jnp.where(first, outs[0], outs[1]).astype(LOW)
        turned = jnp.where(first, sums[0], sums[1]).T
        logsum[0, 0:1, at] = turned[0:1, :]
        logsum[0, 1:2, at] = turned[head : head + 1, :]


def attend(me, query, key, value, head):
    length, width = query.shape
    pairs = width // LANES
    block = pl.BlockSpec((length, LANES), lambda i, _: (0, i))
    return call(
        partial(attend_kernel, 512, head),
        "attend",
        (pairs,),
        [block] * 3,
        [block, pl.BlockSpec((1, 2, length), lambda i, _: (i, 0, 0))],
        [
            jax.ShapeDtypeStruct((length, width), LOW),
            jax.ShapeDtypeStruct((pairs, 2, length), FULL),
        ],
        [],
        16 * length * length * width,
        (me, query, key, value),
        2 * length * width * 4,
    )


def merge_kernel(me_ref, mixed, hidden, vectors, p0, p1, p2, p3, p4, p5, middle, adapted, weight):
    @pl.when(pl.program_id(0) == 0)
    def _():
        assemble(me_ref, weight, (p0, p1, p2, p3, p4, p5), 0, 1)

    branch = matmul(mixed[...], weight[...])
    mid = hidden[...].astype(FULL) + vectors[0:1, :] * branch
    middle[...] = mid
    unit, _ = normalize(mid)
    adapted[...] = (unit * vectors[1:2, :] * vectors[2:3, :] + vectors[3:4, :]).astype(LOW)


def merge(me, mixed, hidden, vectors, pieces):
    length, width = hidden.shape
    step = 512
    rows = pl.BlockSpec((step, width), lambda i, _: (i, 0))
    return call(
        merge_kernel,
        "merge",
        (length // step,),
        [rows, rows, whole(vectors.shape)] + portion(pieces, 3 * width // 8, width // 8),
        [rows, rows],
        [jax.ShapeDtypeStruct((length, width), FULL), jax.ShapeDtypeStruct((length, width), LOW)],
        [pltpu.VMEM((width, width), LOW)],
        2 * length * width * width,
        (me, mixed, hidden, vectors, *pieces),
        2 * length * width * 6,
    )


def feed_kernel(last, at_ref, adapted, upstream, vectors, lift_bias, p0, p1, p2, p3, *refs):
    if last:
        low_in, grad_in, middle, o0, o1, o2, o3, adapted_grad, sums, liftbias_grad, keep, send = refs[:12]
        grads, pack, lift, turned, lowered_grad, out_sem, lowered, low_got, grad_got, middle_got, sem = refs[12:]
        copies = [
            pltpu.make_async_copy(source, target, sem.at[k])
            for k, (source, target) in enumerate(
                ((low_in, low_got), (grad_in, grad_got), (middle, middle_got))
            )
        ]
        for copy in copies:
            copy.start()
    else:
        lowered, adapted_grad, liftbias_grad, keep, send = refs[:5]
        grads, pack, lift, turned, lowered_grad, out_sem = refs[5:]
    for d, piece in enumerate((p0, p1, p2, p3)):
        pack[pl.ds(at_ref[0] ^ d, 1)] = piece[...][None]
    me = at_ref[0]
    gate = vectors[0:1, :]
    rows = lift.shape[0] // 4
    step = lift.shape[1] // 2

    def leave(j, half):
        at = slice(0, step) if half == 0 else slice(step + (half - 1) * rows, step + half * rows)
        where = (j >> 1) ^ (me >> 1)
        for target, odd in ((keep, 0), (send, 1)):

            @pl.when(((me ^ j) & 1) == odd)
            def _(target=target):
                pltpu.make_async_copy(
                    grads.at[j, at, :], target.at[where, at, :], out_sem.at[j, half]
                ).start()

    def left(j, half):
        at = slice(0, step) if half == 0 else slice(step + (half - 1) * rows, step + half * rows)
        pltpu.make_async_copy(
            grads.at[j, at, :], keep.at[0, at, :], out_sem.at[j, half]
        ).wait()

    turned[...] = adapted[...].T
    lowered_grad[...] = (gate * upstream[...].astype(FULL)).astype(LOW)
    for i in range(2):
        deep = slice(step + i * rows, step + (i + 1) * rows)
        for j in range(4):
            lift[j * rows : (j + 1) * rows, :] = pack[j, deep, :]
        weight_up = lift[...]
        weight_down = jnp.concatenate([pack[2 * i, :step, :], pack[2 * i + 1, :step, :]], axis=0)
        across = slice(2 * i * step, 2 * (i + 1) * step)
        upper = matmul(adapted[...], weight_up) + lift_bias[:, across]
        square = upper * upper
        root = math.sqrt(2.0 / math.pi)
        bent = jnp.tanh(upper * (root + root * 0.044715 * square))
        half = 0.5 + 0.5 * bent
        slope = half + upper * (0.5 - 0.5 * bent * bent) * (root + 3.0 * root * 0.044715 * square)
        active = (upper * half).astype(LOW)
        low_part = matmul(active, weight_down)
        down = lowered_grad[...]
        upper_grad = (matmul(down, weight_down, 1, 1) * slope).astype(LOW)
        grad_part = matmul(upper_grad, weight_up, 1, 1)
        if i == 0:
            lowered[...] = low_part
            adapted_grad[...] = grad_part
        else:
            lowered[...] += low_part
            adapted_grad[...] += grad_part
        liftbias_grad[:, across] = column_sum(upper_grad.astype(FULL))
        drop_part = matmul(active, down, 0, 0).astype(LOW)
        for k in range(2):
            grads[2 * i + k, :step, :] = drop_part[k * step : (k + 1) * step]
            leave(2 * i + k, 0)
        lift_part = matmul(turned[...], upper_grad).astype(LOW)
        for j in range(4):
            grads[j, deep, :] = lift_part[j * rows : (j + 1) * rows]
            leave(j, 1 + i)

    if last:
        for copy in copies:
            copy.wait()
        adapted_grad[...] += grad_got[...]
        total = lowered[...] + low_got[...] + vectors[1:2, :]
        low_got[...] = middle_got[...] + gate * total
        span = o0.shape[0]
        for d, target in enumerate((o0, o1, o2, o3)):
            target[...] = low_got[pl.ds(pl.multiple_of((me ^ d) * span, 16), span), :].astype(LOW)
        sums[0:1, :] = column_sum(upstream[...].astype(FULL) * total)
        sums[1:2, :] = column_sum(lowered_grad[...].astype(FULL))
    for j in range(4):
        for half in range(3):
            left(j, half)


def feed(me, adapted, upstream, vectors, lift_bias, pieces, before=()):
    length, width = adapted.shape
    last = len(before) > 0
    units = lift_bias.shape[1]
    wide = jax.ShapeDtypeStruct((length, width), FULL)
    low = jax.ShapeDtypeStruct((length // 4, width), LOW)
    more = jax.ShapeDtypeStruct((2, units // 2, width), LOW)
    sums = jax.ShapeDtypeStruct((8, width), FULL)
    bias = jax.ShapeDtypeStruct((1, units), FULL)
    outs = [low] * 4 + [wide, sums, bias, more, more] if last else [wide, wide, bias, more, more]
    scratch = [
        pltpu.VMEM((4, units // 2, width), LOW),
        pltpu.VMEM((4, units // 2, width), LOW),
        pltpu.VMEM((width, units // 2), LOW),
        pltpu.VMEM((width, length), LOW),
        pltpu.VMEM((length, width), LOW),
        pltpu.SemaphoreType.DMA((4, 3)),
    ]
    if last:
        scratch += [pltpu.VMEM((length, width), FULL)] * 4 + [pltpu.SemaphoreType.DMA((3,))]
    return call(
        partial(feed_kernel, last),
        "feed",
        (1,),
        [whole(a.shape) for a in (adapted, upstream, vectors, lift_bias, *pieces)]
        + [pl.BlockSpec(memory_space=pl.ANY) for _ in before],
        [whole(o.shape) for o in outs[:-2]] + [pl.BlockSpec(memory_space=pl.ANY)] * 2,
        outs,
        scratch,
        12 * length * width * units,
        (me, adapted, upstream, vectors, lift_bias, *pieces, *before),
        8 * width * units + 24 * length * width,
    )


def unmerge_kernel(
    me_ref, adapted_grad, middle, upstream, mixed, vectors, p0, p1, p2, p3, p4, p5,
    middle_grad, mixed_grad, sums, keep, send, weight, total,
):
    i = pl.program_id(0)

    @pl.when(i == 0)
    def _():
        assemble(me_ref, weight, (p0, p1, p2, p3, p4, p5), 0, 1)
        total[...] = jnp.zeros_like(total)
        sums[...] = jnp.zeros_like(sums)

    gate, gain, grow = vectors[0:1, :], vectors[1:2, :], vectors[2:3, :]
    unit, inverse = normalize(middle[...])
    grad = adapted_grad[...]
    sums[0:1, :] += column_sum(grad)
    sums[1:2, :] += column_sum(grad * (unit * gain))
    normed_grad = grad * grow
    sums[2:3, :] += column_sum(normed_grad * unit)
    mid_grad = upstream[...].astype(FULL) + unnormalize(normed_grad * gain, unit, inverse)
    middle_grad[...] = mid_grad
    low = mixed[...]
    sums[3:4, :] += column_sum(mid_grad * matmul(low, weight[...]))
    branch_grad = (gate * mid_grad).astype(LOW)
    total[...] += matmul(low, branch_grad, 0, 0)
    mixed_grad[...] = matmul(branch_grad, weight[...], 1, 1).astype(LOW)

    @pl.when(i == pl.num_programs(0) - 1)
    def _():
        split_rows(me_ref[0], total[...], keep, send)


def unmerge(me, adapted_grad, middle, upstream, mixed, vectors, pieces):
    length, width = middle.shape
    step = 512
    rows = pl.BlockSpec((step, width), lambda i, _: (i, 0))
    part = (2, width // 4, width)
    return call(
        unmerge_kernel,
        "unmerge",
        (length // step,),
        [rows] * 4 + [whole(vectors.shape)] + portion(pieces, 3 * width // 8, width // 8),
        [rows, rows, kept((8, width)), kept(part), kept(part)],
        [
            jax.ShapeDtypeStruct((length, width), FULL),
            jax.ShapeDtypeStruct((length, width), LOW),
            jax.ShapeDtypeStruct((8, width), FULL),
            jax.ShapeDtypeStruct(part, LOW),
            jax.ShapeDtypeStruct(part, LOW),
        ],
        [pltpu.VMEM((width, width), LOW), pltpu.VMEM((width, width), FULL)],
        6 * length * width * width,
        (me, adapted_grad, middle, upstream, mixed, vectors, *pieces),
        2 * length * width * 12,
    )


def unattend_kernel(step, head, sums, me_ref, query, key, value, mixed, mixed_grad, logsum, cosine, sine, *refs):
    if sums:
        grads, mine, other = refs[2:5]
        mine[...] = plus(refs[0][0], refs[1][0])
        other[...] = plus(refs[0][1], refs[1][1])
    else:
        grads = refs[0]
    query_sum, key_sum, value_sum = refs[-3:]
    lane = lax.broadcasted_iota(jnp.int32, (1, LANES), 1)
    first = lane < head
    keys, values = key[...], value[...]
    zero = jnp.zeros_like(keys)
    keys_h = (jnp.where(first, keys, zero), jnp.where(first, zero, keys))
    values_h = (jnp.where(first, values, zero), jnp.where(first, zero, values))
    turned = keys.T
    scale = 1.0 / math.sqrt(head)
    for i in range(query.shape[0] // step):
        at = slice(i * step, (i + 1) * step)
        block, grad = query[at, :], mixed_grad[at, :]
        product = (grad.astype(FULL) * mixed[at, :].astype(FULL)).T
        queries, values_new, keys_new = [], [], []
        for h in range(2):
            center = jnp.sum(product[h * head : (h + 1) * head], axis=0, keepdims=True)
            probs = jnp.exp(matmul(keys_h[h], block, 1, 1) - logsum[0, h : h + 1, at])
            probs_grad = matmul(values_h[h], grad, 1, 1)
            scores_grad = (probs * (probs_grad - center)).astype(LOW)
            values_new.append(matmul(probs.astype(LOW), grad))
            keys_new.append(matmul(scores_grad, block))
            queries.append(matmul(turned[h * head : (h + 1) * head], scores_grad))
        query_sum[at, :] = jnp.concatenate(queries, axis=0).T * scale
        key_part = jnp.where(first, keys_new[0], keys_new[1])
        value_part = jnp.where(first, values_new[0], values_new[1])
        if i == 0:
            key_sum[...] = key_part
            value_sum[...] = value_part
        else:
            key_sum[...] += key_part
            value_sum[...] += value_part
    under = lower_half(head)
    cos, sin = cosine[...], sine[...]
    for which, total in enumerate((query_sum, key_sum)):
        rotated = total[...]
        swept = rotated * sin
        back = jnp.where(
            under, pltpu.roll(swept, LANES - head // 2, 1), -pltpu.roll(swept, head // 2, 1)
        )
        grads[which] = (rotated * cos + back).astype(LOW)
    grads[2] = value_sum[...].astype(LOW)


def unattend(
    me, query, key, value, mixed, mixed_grad, logsum, cosine, sine, head, start, pairs, sums=()
):
    length = mixed.shape[0]
    width = pairs * LANES
    more, outs, specs = [], [], []
    if sums:
        _, rows, columns = sums[0].shape
        part = rows // pairs
        more = [pl.BlockSpec((2, part, columns), lambda i, _: (0, i, 0))] * 2
        outs = [jax.ShapeDtypeStruct((rows, columns), LOW)] * 2
        specs = [pl.BlockSpec((part, columns), lambda i, _: (i, 0))] * 2
    block = pl.BlockSpec((length, LANES), lambda i, _: (0, i + start))
    own = pl.BlockSpec((length, LANES), lambda i, _: (0, i))
    return call(
        partial(unattend_kernel, 256, head, len(sums)),
        "unattend",
        (pairs,),
        [block] * 5
        + [pl.BlockSpec((1, 2, length), lambda i, _: (i + start, 0, 0))]
        + [whole((length, LANES))] * 2
        + more,
        [pl.BlockSpec((3, length, LANES), lambda i, _: (0, 0, i))] + specs,
        [jax.ShapeDtypeStruct((3, length, width), LOW)] + outs,
        [pltpu.VMEM((length, LANES), FULL)] * 3,
        40 * length * length * width,
        (me, query, key, value, mixed, mixed_grad, logsum, cosine, sine, *sums),
        2 * length * width * 8,
    )


def weigh_kernel(riders, sums, me_ref, turned, grads, *refs):
    ins, outs = refs[: riders + sums], refs[riders + sums :]
    keep, send = outs[:2]
    outs = outs[2:]
    if sums:
        mine, other = outs[:2]
        outs = outs[2:]
    found, sem = outs[:2]
    outs = outs[2:]
    me = me_ref[0]
    rows, wide = found.shape[1:]
    step = grads.shape[2]
    moves = []
    if riders:
        for k, (source, target) in enumerate(((ins[0], keep), (ins[1], send))):
            at = target.at[:, :, wide : wide + source.shape[2]]
            moves.append(pltpu.make_async_copy(source, at, sem.at[4 + k, 0]))
    if sums:
        for k in range(2):
            moves.append(pltpu.make_async_copy(ins[riders + k], outs[k], sem.at[4 + k, 1]))
    for move in moves:
        move.start()
    for which in range(3):
        cut = slice(which * step, (which + 1) * step)
        value = matmul(turned[...], grads[which]).astype(LOW)
        for j in range(4):
            found[j, :, cut] = value[j * rows : (j + 1) * rows]
            where = (j >> 1) ^ (me >> 1)
            for target, odd in ((keep, 0), (send, 1)):

                @pl.when(((me ^ j) & 1) == odd)
                def _(target=target, j=j, cut=cut, which=which, where=where):
                    pltpu.make_async_copy(
                        found.at[j, :, cut], target.at[where, :, cut], sem.at[j, which]
                    ).start()

    for move in moves:
        move.wait()
    if sums:
        mine[...] = plus(outs[0][0], outs[1][0])
        other[...] = plus(outs[0][1], outs[1][1])
    for j in range(4):
        for which in range(3):
            cut = slice(which * step, (which + 1) * step)
            pltpu.make_async_copy(
                found.at[j, :, cut], keep.at[0, :, cut], sem.at[j, which]
            ).wait()


def weigh(me, turned, grads, riders=(), sums=()):
    width, length = turned.shape
    step = grads.shape[2]
    more = riders[0].shape[2] if riders else 0
    shape = jax.ShapeDtypeStruct((2, width // 4, 3 * step + more), LOW)
    outs, scratch = [shape, shape], []
    away = pl.BlockSpec(memory_space=pl.ANY)
    specs = [away, away]
    if sums:
        out = jax.ShapeDtypeStruct(sums[0].shape[1:], LOW)
        outs += [out, out]
        specs += [whole(out.shape)] * 2
        scratch = [pltpu.VMEM(sums[0].shape, LOW)] * 2
    return call(
        partial(weigh_kernel, len(riders), len(sums)),
        "weigh",
        (1,),
        [whole(a.shape) for a in (turned, grads, *riders)] + [away] * len(sums),
        specs,
        outs,
        [pltpu.VMEM((4, width // 4, 3 * step), LOW), pltpu.SemaphoreType.DMA((6, 3))] + scratch,
        6 * length * width * step,
        (me, turned, grads, *riders, *sums),
        2 * length * width * 7,
    )


def unproject_kernel(me_ref, g0, g1, hidden, middle_grad, vectors, p0, p1, p2, p3, p4, p5, o0, o1, o2, o3, sums, weight):
    i = pl.program_id(0)

    @pl.when(i == 0)
    def _():
        assemble(me_ref, weight, (p0, p1, p2, p3, p4, p5), 0, 3)
        sums[...] = jnp.zeros_like(sums)

    gain, grow = vectors[0:1, :], vectors[1:2, :]
    width = hidden.shape[1]
    grad, at = None, 0
    for part in (g0, g1):
        size = part.shape[2]
        for which in range(3):
            low = which * width + at
            term = matmul(part[which], weight[:, low : low + size], 1, 1)
            grad = term if grad is None else grad + term
        at += size
    unit, inverse = normalize(hidden[...].astype(FULL))
    sums[0:1, :] += column_sum(grad)
    sums[1:2, :] += column_sum(grad * (unit * gain))
    normed_grad = grad * grow
    sums[2:3, :] += column_sum(normed_grad * unit)
    low = (middle_grad[...] + unnormalize(normed_grad * gain, unit, inverse)).astype(LOW)
    for d, target in enumerate((o0, o1, o2, o3)):

        @pl.when(i == me_ref[0] ^ d)
        def _(target=target):
            target[...] = low


def unproject(me, grads, hidden, middle_grad, vectors, pieces):
    length, width = hidden.shape
    step = length // 4
    rows = pl.BlockSpec((step, width), lambda i, _: (i, 0))
    return call(
        unproject_kernel,
        "unproject",
        (length // step,),
        [pl.BlockSpec((3, step, g.shape[2]), lambda i, _: (0, i, 0)) for g in grads]
        + [rows, rows, whole(vectors.shape)]
        + portion(pieces, 0, 3 * width // 8),
        [kept((step, width))] * 4 + [kept((8, width))],
        [jax.ShapeDtypeStruct((step, width), LOW)] * 4 + [jax.ShapeDtypeStruct((8, width), FULL)],
        [pltpu.VMEM((width, 3 * width), LOW)],
        6 * length * width * width,
        (me, *grads, hidden, middle_grad, vectors, *pieces),
        2 * length * width * 10,
    )


def lay_kernel(me_ref, *refs):
    for d, part in enumerate(refs[:-1]):
        refs[-1][pl.ds(me_ref[0] ^ d, 1)] = part[...][None]


def lay(me, parts):
    shape = (len(parts),) + parts[0].shape
    return call(
        lay_kernel, "lay", (1,), [whole(p.shape) for p in parts], [whole(shape)],
        [jax.ShapeDtypeStruct(shape, LOW)], [], 1024, (me, *parts), 1024,
    )[0]


def finish_kernel(
    seqs, columns, depth, me_ref, parts, others, heads, merges, modulate, modulate_bias, up, down, one, two, table
):
    half, rows = parts.shape[0], parts.shape[1] - 8
    size = 2 * half
    wide = parts.shape[2] // 2
    width = merges.shape[1]
    part = width // 2
    for p in range(size):
        at = slice(p * rows, (p + 1) * rows)
        value = jnp.where(
            me_ref[1] == p // half, parts[p % half, 8:, :], others[p % half, 8:, :]
        ).astype(FULL)
        for k in range(3):
            heads[at, k * width : k * width + part] = value[:, k * part : (k + 1) * part]
            heads[at, k * width + part : (k + 1) * width] = value[:, (5 + k) * part : (6 + k) * part]
        merges[at, :] = value[:, 3 * part : 5 * part]
    small = jnp.concatenate(
        [
            source[p, :8, :wide].astype(FULL) + source[p, :8, wide:].astype(FULL)
            for source in (parts, others)
            for p in range(half)
        ],
        axis=0,
    )
    row = lax.broadcasted_iota(jnp.int32, (8 * size, 1), 0) & 7
    mine = row < seqs
    zero = jnp.zeros((), FULL)
    grads = jnp.where(mine, small[:, :columns], zero)
    conds = jnp.where(mine, small[:, columns : columns + depth], zero)
    conds_grad = jnp.where(mine, small[:, columns + depth : columns + 2 * depth], zero)
    steps = small[:, columns + 2 * depth : columns + 2 * depth + 1].astype(jnp.int32)

    def exact(left, right):
        dims = (((0,), (0,)), ((), ()))
        return lax.dot_general(
            left, right, dims, precision=lax.Precision.HIGHEST, preferred_element_type=FULL
        )

    modulate[...] = exact(grads, conds)
    modulate_bias[...] = column_sum(grads)[0]
    ends = column_sum(jnp.where(row == seqs, small, zero))
    at = 0
    for target in (up, down, one, two):
        size = target.shape[0]
        target[...] = ends[0, at : at + size]
        at += size
    share = table.shape[0]
    own = me_ref[0] * share + lax.broadcasted_iota(jnp.int32, (1, share), 1)
    table[...] = exact(jnp.where(mine & (steps == own), 1.0, 0.0), conds_grad)


def finish(me, parts, others, width, columns, depth, sizes, share):
    shapes = [(width // 4, 3 * width), (width // 4, width), (columns, depth), (columns,)]
    shapes += [(size,) for size in sizes] + [(share, depth)]
    return call(
        partial(finish_kernel, 4, columns, depth), "finish", (1,), [whole(parts.shape)] * 2,
        [whole(s) for s in shapes], [jax.ShapeDtypeStruct(s, FULL) for s in shapes], [], 1024,
        (me, parts, others), 1024,
    )


def swap(array, axis, distance):
    size = lax.axis_size(axis)
    return lax.ppermute(array, axis, [(i, i ^ distance) for i in range(size)])


def fence(*trees):
    return lax.optimization_barrier(trees)


def bit(axis, distance):
    return (lax.axis_index(axis) // distance) % 2


def choose(parts, at):
    return lax.dynamic_index_in_dim(parts, at, 0, keepdims=False)


def choose_all(array, place):
    count = array.shape[0]
    return jnp.stack([choose(array, place ^ k) for k in range(count)])


def payload(parts):
    return jnp.concatenate([p.reshape(2, p.shape[0] // 2, p.shape[1]) for p in parts], axis=1)


def blocks_of(weight, width):
    return [weight[:, k : k + width] for k in range(0, weight.shape[1], width)]


def powers(size):
    return [1 << k for k in range(size.bit_length() - 1)]


def plus(*terms):
    total = terms[0].astype(FULL)
    for term in terms[1:]:
        total = total + term.astype(FULL)
    return total.astype(LOW)


def other_kernel(at_ref, kept_term, got, other):
    other[...] = plus(kept_term[0], got[0])


def sum_other(kept_term, got):
    _, rows, columns = kept_term.shape
    steps = 4 if rows % 256 == 0 else 2
    part = rows // steps
    two = pl.BlockSpec((1, part, columns), lambda i, _: (1, i, 0))
    return call(
        other_kernel, "other", (steps,), [two, two], [pl.BlockSpec((part, columns), lambda i, _: (i, 0))],
        [jax.ShapeDtypeStruct((rows, columns), LOW)], [], 1024,
        (jnp.zeros((1,), jnp.int32), kept_term, got), 1024,
    )[0]


def three_kernel(at_ref, kept_term, got, last, total):
    total[...] = plus(kept_term[0], got[0], last[...])


def sum_three(kept_term, got, last):
    _, rows, columns = kept_term.shape
    part = rows // 2
    two = pl.BlockSpec((1, part, columns), lambda i, _: (0, i, 0))
    one = pl.BlockSpec((part, columns), lambda i, _: (i, 0))
    return call(
        three_kernel, "two", (2,), [two, two, one], [one],
        [jax.ShapeDtypeStruct((rows, columns), LOW)], [], 1 << 33,
        (jnp.zeros((1,), jnp.int32), kept_term, got, last), 1 << 24,
    )[0]


def two_kernel(at_ref, first, second, total):
    total[...] = plus(first[...], second[...])


def sum_two(first, second):
    rows, columns = first.shape
    steps = 2 if rows % 32 == 0 else 1
    spec = pl.BlockSpec((rows // steps, columns), lambda i, _: (i, 0))
    return call(
        two_kernel, "two", (steps,), [spec] * 2, [spec],
        [jax.ShapeDtypeStruct((rows, columns), LOW)], [], 1 << 33,
        (jnp.zeros((1,), jnp.int32), first, second), 1 << 24,
    )[0]


def beside_kernel(at_ref, a, b, c, d, e, mine, other):
    cut = a.shape[2]
    for target, at in ((mine, at_ref[0]), (other, 1 - at_ref[0])):
        at = pl.ds(at, 1)
        target[:, :cut] = plus(a[at], b[at])[0]
        target[:, cut:] = plus(c[0, at], d[0, at], e[at])[0]


def split_beside(first, second):
    args = [a.reshape(a.shape[:-2] + (2, -1, a.shape[-1])) for a in (*first, *second)]
    rows = args[0].shape[1]
    out = (rows, args[0].shape[2] + args[4].shape[2])
    pair = pl.BlockSpec((1,) + args[2].shape[1:], lambda *_: (0, 0, 0, 0), pipeline_mode=pl.Buffered(1))
    return call(
        beside_kernel, "beside", (1,),
        [whole(args[0].shape), whole(args[1].shape), pair, pair, whole(args[4].shape)], [whole(out)] * 2,
        [jax.ShapeDtypeStruct(out, LOW)] * 2, [], 1024, (place_of(1), *args), 1024,
    )


def terms_kernel(at_ref, small, parts, total):
    value = plus(*[parts[k] for k in range(parts.shape[0])])
    for k in range(total.shape[0]):
        total[k, :8, :] = small[...]
        total[k, 8:, :] = value


def gather_terms(small, parts):
    shape = (parts.shape[0], 8 + parts.shape[1], small.shape[1])
    return call(
        terms_kernel, "terms", (1,), [whole(small.shape), whole(parts.shape)], [whole(shape)],
        [jax.ShapeDtypeStruct(shape, LOW)], [], 1024, (jnp.zeros((1,), jnp.int32), small, parts), 1024,
    )[0]


def exchange(parts):
    size = lax.axis_size("dp")
    groups = None
    if parts.shape[0] < size:
        groups = [list(range(b, size, 2)) for b in range(2)]
    return lax.all_to_all(parts, "dp", 0, 0, axis_index_groups=groups, tiled=True)


def deal(term, size=None):
    size = size or lax.axis_size("dp")
    rows, columns = term.shape
    return exchange(term.reshape(size, rows // size, columns))


def add_kernel(at_ref, parts, total):
    total[...] = plus(*[parts[k] for k in range(parts.shape[0])])


def add_up(parts):
    shape = parts.shape[1:]
    return call(
        add_kernel, "add", (1,), [whole(parts.shape)], [whole(shape)],
        [jax.ShapeDtypeStruct(shape, LOW)], [], 1 << 33, (jnp.zeros((1,), jnp.int32), parts), 1 << 24,
    )[0]


def place_of(distance):
    return bit("dp", distance).astype(jnp.int32).reshape(1)


def join_kernel(at_ref, first, second, both):
    b = at_ref[0]
    both[pl.ds(b, 1)] = first[...][None]
    both[pl.ds(1 - b, 1)] = second[...][None]


def join(first, second, distance):
    rows, columns = first.shape
    shape = (2, rows, columns)
    return call(
        join_kernel, "join", (1,), [whole(first.shape)] * 2, [whole(shape)],
        [jax.ShapeDtypeStruct(shape, LOW)], [], 1024, (place_of(distance), first, second), 1024,
    )[0].reshape(2 * rows, columns)


def settle_kernel(plan, size, at_ref, *refs):
    count = len(plan)
    outs = refs[2 * count :]
    depth = size.bit_length() - 1
    b = at_ref[0]
    for p, moves in enumerate(plan):
        rows = 2 * refs[2 * p].shape[0] // size
        for h in range(2):
            value = jnp.where(b == h, refs[2 * p][...], refs[2 * p + 1][...]).astype(FULL)
            for k in range(h, size, 2):
                at = sum(((k >> j) & 1) << (depth - 1 - j) for j in range(1, depth)) * rows
                for top, left, down, wide, out, to_row, to_column in moves:
                    low, high = max(top, k * rows), min(top + down, (k + 1) * rows)
                    if low < high:
                        start = to_row + low - top
                        source = at + low - k * rows
                        outs[out][start : start + high - low, to_column : to_column + wide] = value[
                            source : source + high - low, left : left + wide
                        ]


def settle(pairs, plan, shapes):
    args = [array for pair in pairs for array in pair]
    return call(
        partial(settle_kernel, plan, lax.axis_size("dp")),
        "settle",
        (1,),
        [whole(a.shape) for a in args],
        [whole(shape) for shape in shapes],
        [jax.ShapeDtypeStruct(shape, FULL) for shape in shapes],
        [],
        1024,
        (place_of(1), *args),
        1024,
    )


def shards(
    hidden_in,
    time_table,
    time_step,
    token_pos,
    heads_weight,
    merge_weight,
    lift_weight,
    lift_bias,
    drop_weight,
    drop_bias,
    modulate_weight,
    modulate_bias,
    first_gain,
    second_gain,
    out_grad,
):
    count = lax.axis_size("seq")
    place = lax.axis_index("seq")
    seqs, span, width = hidden_in.shape
    assert count == 4 and seqs == count
    length = span * count
    head = width // HEADS
    bits = powers(lax.axis_size("dp"))
    row_half = bit("dp", 1)
    me = jnp.stack([place, row_half]).astype(jnp.int32)

    units = drop_weight.shape[0]
    step = units // 2
    heads_pack = payload(blocks_of(heads_weight, width) + [merge_weight])
    heads_half = choose(heads_pack, row_half)
    heads_half, time_step = fence(heads_half, time_step)
    heads_across = swap(heads_half, "seq", 2)

    def feed_pack(h):
        columns = [lift_weight[:, j * units + h * step : j * units + (h + 1) * step] for j in range(4)]
        blocks = [jnp.concatenate(columns[k : k + 2], axis=1) for k in (0, 2)]
        return jnp.concatenate([drop_weight[h * step : (h + 1) * step]] + blocks, axis=0)

    table_rows, depth = time_table.shape
    chosen_rows = (time_step[:, None] == jnp.arange(table_rows, dtype=jnp.int32)[None, :]).astype(LOW)
    conds = jnp.dot(chosen_rows, time_table, preferred_element_type=FULL)
    modulation = matmul(conds.astype(LOW), modulate_weight, 1, 1) + modulate_bias.astype(FULL)
    columns = modulation.shape[1]
    vectors = [v.astype(FULL) for v in (lift_bias, drop_bias, first_gain, second_gain)]
    above = jnp.concatenate([modulation, token_pos.astype(FULL)], axis=1)
    below = jnp.concatenate(vectors)[None]
    below = jnp.pad(below, ((0, 0), (0, above.shape[1] - below.shape[1])))
    small = jnp.concatenate([above, below], axis=0)
    small_across = swap(small, "seq", 2)
    hidden_in, small = fence(hidden_in, small)
    heads_across, small, lift_weight, drop_weight = fence(
        heads_across, small, lift_weight, drop_weight
    )
    heads_handed = swap(heads_across, "dp", 1)
    heads_core = swap(heads_pack, "seq", 1), swap(heads_across, "seq", 1)
    hidden = lax.all_to_all(hidden_in, "seq", 0, 0, tiled=True).reshape(length, width)
    small = jnp.stack([small, small_across])
    small_core = swap(small, "seq", 1)
    small = jnp.stack([small[0], small_core[0], small[1], small_core[1]])
    small = choose_all(small, place)
    mine = lax.dynamic_index_in_dim(small, place, 1, keepdims=False)
    chosen = mine[:, :columns].reshape(6, width)
    positions = mine[:, columns:].reshape(length)
    rest = small[:, seqs]
    sizes = (lift_bias.shape[0], drop_bias.shape[0], first_gain.shape[0], second_gain.shape[0])
    vectors, at = [], 0
    for size in sizes:
        vectors.append(rest[:, at : at + size].reshape(1, -1))
        at += size
    up_bias, down_bias, gain_one, gain_two = vectors
    shift_a, scale_a, gate_a, shift_b, scale_b, gate_b = [chosen[k : k + 1] for k in range(6)]
    grow_a, grow_b = 1.0 + scale_a, 1.0 + scale_b

    def rows(*items):
        blank = jnp.zeros((8 - len(items), width), FULL)
        return jnp.concatenate(items + (blank,), axis=0)

    freqs = 10000.0 ** (-jnp.arange(0, head, 2, dtype=FULL) / head)
    freqs = jnp.tile(freqs, 2 * LANES // head)
    angles = positions[:, None] * freqs
    cosine, sine = jnp.cos(angles), jnp.sin(angles)

    pack_0, pack_1 = feed_pack(0), feed_pack(1)
    project_vectors = rows(gain_one, grow_a, shift_a)
    heads_handed, project_vectors, cosine, sine, pack_0, pack_1, me = fence(
        heads_handed, project_vectors, cosine, sine, pack_0, pack_1, me
    )
    heads = (
        heads_pack,
        heads_core[0],
        heads_across,
        heads_handed,
        heads_core[1],
        swap(heads_handed, "seq", 1),
    )
    hidden, heads, cosine, sine, pack_0, pack_1, out_grad = fence(
        hidden, heads, cosine, sine, pack_0, pack_1, out_grad
    )
    across_0 = swap(pack_0, "seq", 2)
    core_0, core_1 = swap(pack_0, "seq", 1), swap(pack_1, "seq", 1)
    adapted_a, query, key, value = project(
        me, hidden, project_vectors, heads, cosine, sine, head
    )
    merge_vectors, unmerge_vectors = rows(gate_a, gain_two, grow_b, shift_b), rows(gate_a, gain_two, grow_b)
    feed_vectors = rows(gate_b, down_bias)
    bias_0, bias_1 = [up_bias.reshape(4, 2, step)[:, h].reshape(1, 4 * step) for h in range(2)]
    query, merge_vectors, unmerge_vectors, feed_vectors, bias_0, bias_1 = fence(
        query, merge_vectors, unmerge_vectors, feed_vectors, bias_0, bias_1
    )
    query, out_grad = fence(query, out_grad)
    upstream = lax.all_to_all(out_grad, "seq", 0, 0, tiled=True).reshape(length, width)
    mixed, logsum = attend(me, query, key, value, head)
    mixed, logsum, across_0 = fence(mixed, logsum, across_0)
    mixed, pack_1 = fence(mixed, pack_1)
    other_0 = swap(across_0, "seq", 1)
    across_1 = swap(pack_1, "seq", 2)
    middle, adapted_b = merge(me, mixed, hidden, merge_vectors, heads)
    middle, adapted_b, core_0, other_0, upstream = fence(
        middle, adapted_b, core_0, other_0, upstream
    )
    pairs = width // LANES // 2
    adapted_b, upstream, core_1 = fence(adapted_b, upstream, core_1)
    lowered, grad, liftbias_0, keep_0, send_0 = feed(
        me, adapted_b, upstream, feed_vectors, bias_0, (pack_0, core_0, across_0, other_0)
    )
    lowered, grad, liftbias_0, keep_0, send_0, across_1 = fence(
        lowered, grad, liftbias_0, keep_0, send_0, across_1
    )
    other_1 = swap(across_1, "seq", 1)
    got_0 = swap(send_0, "seq", 1)
    *out_parts, adapted_b_grad, feed_sums, liftbias_1, keep_1, send_1 = feed(
        me, adapted_b, upstream, feed_vectors, bias_1, (pack_1, core_1, across_1, other_1),
        (lowered, grad, middle),
    )
    back = bits[::-1]
    last = len(back) - 1
    out_parts, adapted_b_grad, feed_sums, liftbias_1, keep_1, send_1, got_0 = fence(
        out_parts, adapted_b_grad, feed_sums, liftbias_1, keep_1, send_1, got_0
    )
    got_1 = swap(send_1, "seq", 1)
    core_0 = got_0
    adapted_b_grad, other_0 = fence(adapted_b_grad, sum_other(keep_0, core_0))
    got_0 = swap(other_0, "seq", 2)
    middle_grad, mixed_grad, merge_sums, merge_keep, merge_send = unmerge(
        me, adapted_b_grad, middle, upstream, mixed, unmerge_vectors, heads
    )
    middle_grad, mixed_grad, merge_sums, merge_keep, merge_send, got_1 = fence(
        middle_grad, mixed_grad, merge_sums, merge_keep, merge_send, got_1
    )
    heads_0, mine_1, other_1 = unattend(
        me, query, key, value, mixed, mixed_grad, logsum, cosine, sine, head, 0, pairs, (keep_1, got_1)
    )
    heads_0, mine_1, other_1, got_0 = fence(heads_0, mine_1, other_1, got_0)
    got_1 = swap(other_1, "seq", 2)
    heads_0, term_0 = fence(heads_0, sum_three(keep_0, core_0, got_0))
    parts_0 = deal(term_0)
    keep_2, send_2 = weigh(me, adapted_a, heads_0, (merge_keep, merge_send))
    mixed_grad, keep_2, send_2 = fence(mixed_grad, keep_2, send_2)
    got_2 = swap(send_2, "seq", 1)
    (heads_1,) = unattend(
        me, query, key, value, mixed, mixed_grad, logsum, cosine, sine, head, pairs, pairs
    )
    heads_1, got_1 = fence(heads_1, got_1)
    heads_1, term_1, parts_0 = fence(heads_1, sum_two(mine_1, got_1), parts_0)
    parts_1 = deal(term_1)
    heads_1, got_2 = fence(heads_1, got_2)
    keep_3, send_3, mine_2, other_2 = weigh(me, adapted_a, heads_1, (), (keep_2, got_2))
    keep_3, send_3, mine_2, other_2, parts_0 = fence(keep_3, send_3, mine_2, other_2, parts_0)
    got_3 = swap(send_3, "seq", 1)
    got_2 = swap(other_2, "seq", 2)
    term_0, core_3 = fence(add_up(parts_0), got_3)
    heads_1, term_0, other_3 = fence(heads_1, term_0, sum_other(keep_3, core_3))
    got_3 = swap(other_3, "seq", 2)
    got_0 = swap(term_0, "dp", back[0])
    *input_parts, project_sums = unproject(
        me, (heads_0, heads_1), hidden, middle_grad, rows(gain_one, grow_a), heads
    )
    input_parts, project_sums, got_0 = fence(input_parts, project_sums, got_0)
    input_parts, project_sums, term_0 = fence(
        input_parts, project_sums, join(term_0, got_0, back[0])
    )
    got_0 = swap(term_0, "dp", back[1])
    input_parts, project_sums, got_2, got_3, parts_1 = fence(
        input_parts, project_sums, got_2, got_3, parts_1
    )
    (mine_a, other_a), input_parts, project_sums, parts_1 = fence(
        split_beside((mine_2, got_2), (keep_3, core_3, got_3)), input_parts, project_sums, parts_1
    )
    got_a = swap(other_a, "dp", 1)
    liftbias_grad = jnp.stack([liftbias_0.reshape(4, step), liftbias_1.reshape(4, step)], axis=1)
    modulation_grad = jnp.concatenate(
        [project_sums[0:2], merge_sums[3:4], merge_sums[0:2], feed_sums[0:1]], axis=0
    ).reshape(count, columns)
    small = jnp.concatenate(
        [
            modulation_grad,
            liftbias_grad.reshape(count, -1),
            feed_sums[1].reshape(count, -1),
            project_sums[2].reshape(count, -1),
            merge_sums[2].reshape(count, -1),
        ],
        axis=1,
    )
    parts = [choose(small, place ^ d) for d in range(4)]
    term_1, parts = fence(add_up(parts_1), parts)
    got_1 = swap(term_1, "dp", back[0])
    parts = [swap(part, "seq", d) if d else part for d, part in enumerate(parts)]
    term_0, input_parts, parts = fence(join(term_0, got_0, back[1]), input_parts, parts)
    for k in range(2, last):
        term_0 = join(term_0, swap(term_0, "dp", back[k]), back[k])
    got_0 = swap(term_0, "dp", back[-1])
    input_parts = [swap(part, "seq", d) if d else part for d, part in enumerate(input_parts)]
    mine_a, got_a = fence(mine_a, got_a)
    mine_a, got_a, got_1, parts, term_0 = fence(mine_a, got_a, got_1, parts, term_0)
    term_a, got_1, parts, out_parts = fence(sum_two(mine_a, got_a), got_1, parts, out_parts)
    parts_a = deal(term_a, lax.axis_size("dp") // 2)
    term_1 = join(term_1, got_1, back[0])
    got_1 = swap(term_1, "dp", back[1])
    out_parts = [swap(part, "seq", d) if d else part for d, part in enumerate(out_parts)]
    small = choose_all(jnp.stack(parts), place)
    exact = lax.Precision.HIGHEST
    conds_grad = jnp.einsum(
        "sm,mc->sc", small[:, :columns], modulate_weight.astype(FULL), precision=exact
    )
    conds_grad = sum([swap(conds_grad, "seq", d) for d in (1, 2, 3)], conds_grad)
    spare = term_a.shape[1] // 2 - columns - 2 * depth
    above = jnp.concatenate(
        [
            small[:, :columns],
            conds,
            conds_grad,
            jnp.broadcast_to(time_step.astype(FULL)[:, None], (seqs, spare)),
        ],
        axis=1,
    )
    below = jnp.sum(small[:, columns:], axis=0)[None]
    below = jnp.pad(below, ((0, 7 - seqs), (0, above.shape[1] - below.shape[1])))
    small = jnp.concatenate([above, below], axis=0)
    upper = lax.reduce_precision(small, 8, 7)
    small = jnp.concatenate([upper, small - upper], axis=1).astype(LOW)
    small, parts_a = fence(small, parts_a)
    small, parts_a, got_1, input_parts = fence(small, parts_a, got_1, input_parts)
    term_a, got_1, input_parts = fence(gather_terms(small, parts_a), got_1, input_parts)
    parts_a = exchange(term_a)
    term_1 = join(term_1, got_1, back[1])
    for k in range(2, last):
        term_1 = join(term_1, swap(term_1, "dp", back[k]), back[k])
    got_1 = swap(term_1, "dp", back[-1])
    input_grad = lay(me, input_parts)
    parts_a, got_0 = fence(parts_a, got_0)
    parts_a, got_0, got_1, out_parts, input_grad = fence(
        parts_a, got_0, got_1, out_parts, input_grad
    )
    got_a = swap(parts_a, "dp", 1)
    block_out = lay(me, out_parts)
    pair_0, pair_1 = (term_0, got_0), (term_1, got_1)
    deep = width // 4
    drop_grad, lift_grad = settle(
        [pair_0, pair_1],
        [
            [(0, 0, step, width, 0, h * step, 0)]
            + [
                (step + (j >> 1) * deep, (j & 1) * step, deep, step, 1, 0, j * units + h * step)
                for j in range(4)
            ]
            for h in range(2)
        ],
        [drop_weight.shape, lift_weight.shape],
    )
    block_out, input_grad, drop_grad, lift_grad, parts_a, got_a = fence(
        block_out, input_grad, drop_grad, lift_grad, parts_a, got_a
    )
    share = table_rows // count
    (
        heads_grad, merge_grad, modulate_grad, modulatebias_grad,
        liftbias_out, dropbias_out, firstgain_out, secondgain_out, table_grad,
    ) = finish(me, parts_a, got_a, width, columns, depth, sizes, share)
    return (
        block_out,
        input_grad,
        heads_grad,
        merge_grad,
        lift_grad,
        liftbias_out,
        drop_grad,
        dropbias_out,
        modulate_grad,
        modulatebias_grad,
        firstgain_out,
        secondgain_out,
        table_grad,
    )


def solution(mesh):
    return jax.shard_map(
        shards,
        mesh=mesh,
        in_specs=(
            P("dp", "seq", None),
            P(),
            P("dp"),
            P("dp", "seq"),
            P("seq", None),
            P("seq", None),
            P("seq", None),
            P("seq"),
            P("seq", None),
            P("seq"),
            P("seq", None),
            P("seq"),
            P("seq"),
            P("seq"),
            P("dp", "seq", None),
        ),
        out_specs=(
            P("dp", "seq", None),
            P("dp", "seq", None),
            P("seq", None),
            P("seq", None),
            P("seq", None),
            P("seq"),
            P("seq", None),
            P("seq"),
            P("seq", None),
            P("seq"),
            P("seq"),
            P("seq"),
            P("seq", None),
        ),
        check_vma=False,
    )
```

```python
from functools import partial
import math

import jax
import jax.numpy as jnp
from jax import lax
from jax.experimental import pallas as pl
from jax.experimental.pallas import tpu as pltpu
from jax.sharding import PartitionSpec as P

HEADS = 12
EPSILON = 1e-05
LANES = 128
VMEM = 60 * 1024 * 1024
LOW = jnp.bfloat16
FULL = jnp.float32


def matmul(left, right, left_dim=1, right_dim=0):
    dims = (((left_dim,), (right_dim,)), ((), ()))
    return lax.dot_general(left, right, dims, preferred_element_type=FULL)


def call(body, name, grid, in_specs, out_specs, out_shape, scratch, flops, args, moved):
    return pl.pallas_call(
        body,
        name=name,
        grid_spec=pltpu.PrefetchScalarGridSpec(
            num_scalar_prefetch=1,
            grid=grid,
            in_specs=in_specs,
            out_specs=out_specs,
            scratch_shapes=scratch,
        ),
        out_shape=out_shape,
        compiler_params=pltpu.CompilerParams(
            dimension_semantics=("arbitrary",) * len(grid), vmem_limit_bytes=VMEM
        ),
        cost_estimate=pl.CostEstimate(flops=flops, bytes_accessed=moved, transcendentals=0)
        if name in ("feed", "two", "add")
        else pl.CostEstimate(flops=1024, bytes_accessed=1024, transcendentals=0),
    )(*args)


def whole(shape):
    zeros = (0,) * len(shape)
    return pl.BlockSpec(shape, lambda *_: zeros, pipeline_mode=pl.Buffered(1))


def kept(shape):
    zeros = (0,) * len(shape)
    return pl.BlockSpec(shape, lambda *_: zeros)


def assemble(at, target, pieces, start, blocks):
    me, b = at[0], at[1]
    own, core, across, handed, core_across, core_handed = pieces
    rows = target.shape[0] // 8
    width = target.shape[1] // blocks
    halves = (
        (me, 0, lambda cut: own[0, cut, :]),
        (me, 1, lambda cut: own[1, cut, :]),
        (me ^ 1, 0, lambda cut: core[0, cut, :]),
        (me ^ 1, 1, lambda cut: core[1, cut, :]),
        (me ^ 2, b, lambda cut: across[cut, :]),
        (me ^ 2, 1 - b, lambda cut: handed[cut, :]),
        (me ^ 3, b, lambda cut: core_across[cut, :]),
        (me ^ 3, 1 - b, lambda cut: core_handed[cut, :]),
    )
    for shard, half, read in halves:
        place = pl.ds(pl.multiple_of((2 * shard + half) * rows, 16), rows)
        for k in range(blocks):
            cut = slice(start + k * rows, start + (k + 1) * rows)
            target[place, k * width : (k + 1) * width] = read(cut)


def portion(pieces, start, size):
    at = start // size
    return [
        pl.BlockSpec(
            p.shape[:-2] + (size, p.shape[-1]),
            partial(lambda n, *_: (0,) * n + (at, 0), len(p.shape) - 2),
            pipeline_mode=pl.Buffered(1),
        )
        for p in pieces
    ]


def split_rows(me, value, keep, send):
    rows = value.shape[0] // 4
    mine_x, mine_c = me >> 1, me & 1
    for j in range(4):
        part = value[j * rows : (j + 1) * rows].astype(LOW)[None]
        at = (j >> 1) ^ mine_x

        @pl.when(mine_c == (j & 1))
        def _(part=part, at=at):
            keep[pl.ds(at, 1)] = part

        @pl.when(mine_c != (j & 1))
        def _(part=part, at=at):
            send[pl.ds(at, 1)] = part


def normalize(values):
    center = values - jnp.mean(values, axis=-1, keepdims=True)
    inverse = lax.rsqrt(jnp.mean(center * center, axis=-1, keepdims=True) + EPSILON)
    return center * inverse, inverse


def unnormalize(weighted, unit, inverse):
    first = jnp.mean(weighted, axis=-1, keepdims=True)
    second = jnp.mean(weighted * unit, axis=-1, keepdims=True)
    return inverse * (weighted - first - unit * second)


def lower_half(head):
    lane = lax.broadcasted_iota(jnp.int32, (1, LANES), 1)
    return (lane & (head - 1)) < head // 2


def column_sum(values):
    return jnp.sum(values, axis=0, keepdims=True)


def project_kernel(head, me_ref, hidden, vectors, p0, p1, p2, p3, p4, p5, cosine, sine, turned, query, key, value, weight):
    @pl.when(pl.program_id(0) == 0)
    def _():
        assemble(me_ref, weight, (p0, p1, p2, p3, p4, p5), 0, 3)

    unit, _ = normalize(hidden[...].astype(FULL))
    low = (unit * vectors[0:1, :] * vectors[1:2, :] + vectors[2:3, :]).astype(LOW)
    turned[...] = low.T
    width = low.shape[1]
    cos, sin = cosine[...], sine[...]
    under = lower_half(head)
    signed = jnp.where(under, -sin, sin)
    scale = 1.0 / math.sqrt(head)
    for which, target in enumerate((query, key)):
        part = matmul(low, weight[:, which * width : (which + 1) * width])
        for j in range(width // LANES):
            block = part[:, j * LANES : (j + 1) * LANES]
            turned = jnp.where(
                under,
                pltpu.roll(block, LANES - head // 2, 1),
                pltpu.roll(block, head // 2, 1),
            )
            turned = (block * cos + turned * signed).astype(LOW)
            if which == 0:
                turned = turned * jnp.asarray(scale, LOW)
            target[:, j * LANES : (j + 1) * LANES] = turned
    value[...] = matmul(low, weight[:, 2 * width :]).astype(LOW)


def project(me, hidden, vectors, pieces, cosine, sine, head):
    length, width = hidden.shape
    step = 512
    rows = pl.BlockSpec((step, width), lambda i, _: (i, 0))
    angle = pl.BlockSpec((step, LANES), lambda i, _: (i, 0))
    out = jax.ShapeDtypeStruct((length, width), LOW)
    return call(
        partial(project_kernel, head),
        "project",
        (length // step,),
        [rows, whole(vectors.shape)] + portion(pieces, 0, 3 * width // 8) + [angle, angle],
        [pl.BlockSpec((width, step), lambda i, _: (0, i))] + [rows] * 3,
        [jax.ShapeDtypeStruct((width, length), LOW)] + [out] * 3,
        [pltpu.VMEM((width, 3 * width), LOW)],
        2 * length * width * 3 * width,
        (me, hidden, vectors, *pieces, cosine, sine),
        2 * length * width * 8,
    )


def attend_kernel(step, head, me_ref, query, key, value, mixed, logsum):
    lane = lax.broadcasted_iota(jnp.int32, (1, LANES), 1)
    first = lane < head
    keys, values = key[...], value[...]
    zero = jnp.zeros_like(keys)
    split = (jnp.where(first, keys, zero), jnp.where(first, zero, keys))
    for i in range(query.shape[0] // step):
        at = slice(i * step, (i + 1) * step)
        block = query[at, :]
        outs, sums = [], []
        for h in range(2):
            scores = matmul(block, split[h], 1, 1)
            peak = jnp.max(scores, axis=1, keepdims=True)
            expos = jnp.exp(scores - peak)
            total = jnp.sum(expos, axis=1, keepdims=True)
            outs.append(matmul(expos.astype(LOW), values) * (1.0 / total))
            sums.append(peak + jnp.log(total))
        mixed[at, :] = jnp.where(first, outs[0], outs[1]).astype(LOW)
        turned = jnp.where(first, sums[0], sums[1]).T
        logsum[0, 0:1, at] = turned[0:1, :]
        logsum[0, 1:2, at] = turned[head : head + 1, :]


def attend(me, query, key, value, head):
    length, width = query.shape
    pairs = width // LANES
    block = pl.BlockSpec((length, LANES), lambda i, _: (0, i))
    return call(
        partial(attend_kernel, 512, head),
        "attend",
        (pairs,),
        [block] * 3,
        [block, pl.BlockSpec((1, 2, length), lambda i, _: (i, 0, 0))],
        [
            jax.ShapeDtypeStruct((length, width), LOW),
            jax.ShapeDtypeStruct((pairs, 2, length), FULL),
        ],
        [],
        16 * length * length * width,
        (me, query, key, value),
        2 * length * width * 4,
    )


def merge_kernel(me_ref, mixed, hidden, vectors, p0, p1, p2, p3, p4, p5, middle, adapted, weight):
    @pl.when(pl.program_id(0) == 0)
    def _():
        assemble(me_ref, weight, (p0, p1, p2, p3, p4, p5), 0, 1)

    branch = matmul(mixed[...], weight[...])
    mid = hidden[...].astype(FULL) + vectors[0:1, :] * branch
    middle[...] = mid
    unit, _ = normalize(mid)
    adapted[...] = (unit * vectors[1:2, :] * vectors[2:3, :] + vectors[3:4, :]).astype(LOW)


def merge(me, mixed, hidden, vectors, pieces):
    length, width = hidden.shape
    step = 512
    rows = pl.BlockSpec((step, width), lambda i, _: (i, 0))
    return call(
        merge_kernel,
        "merge",
        (length // step,),
        [rows, rows, whole(vectors.shape)] + portion(pieces, 3 * width // 8, width // 8),
        [rows, rows],
        [jax.ShapeDtypeStruct((length, width), FULL), jax.ShapeDtypeStruct((length, width), LOW)],
        [pltpu.VMEM((width, width), LOW)],
        2 * length * width * width,
        (me, mixed, hidden, vectors, *pieces),
        2 * length * width * 6,
    )


def feed_kernel(last, at_ref, adapted, upstream, vectors, lift_bias, p0, p1, p2, p3, *refs):
    if last:
        low_in, grad_in, middle, o0, o1, o2, o3, adapted_grad, sums, liftbias_grad, keep, send = refs[:12]
        grads, pack, lift, turned, lowered_grad, out_sem, lowered, low_got, grad_got, middle_got, sem = refs[12:]
        copies = [
            pltpu.make_async_copy(source, target, sem.at[k])
            for k, (source, target) in enumerate(
                ((low_in, low_got), (grad_in, grad_got), (middle, middle_got))
            )
        ]
        for copy in copies:
            copy.start()
    else:
        lowered, adapted_grad, liftbias_grad, keep, send = refs[:5]
        grads, pack, lift, turned, lowered_grad, out_sem = refs[5:]
    for d, piece in enumerate((p0, p1, p2, p3)):
        pack[pl.ds(at_ref[0] ^ d, 1)] = piece[...][None]
    me = at_ref[0]
    gate = vectors[0:1, :]
    rows = lift.shape[0] // 4
    step = lift.shape[1] // 2

    def leave(j, half):
        at = slice(0, step) if half == 0 else slice(step + (half - 1) * rows, step + half * rows)
        where = (j >> 1) ^ (me >> 1)
        for target, odd in ((keep, 0), (send, 1)):

            @pl.when(((me ^ j) & 1) == odd)
            def _(target=target):
                pltpu.make_async_copy(
                    grads.at[j, at, :], target.at[where, at, :], out_sem.at[j, half]
                ).start()

    def left(j, half):
        at = slice(0, step) if half == 0 else slice(step + (half - 1) * rows, step + half * rows)
        pltpu.make_async_copy(
            grads.at[j, at, :], keep.at[0, at, :], out_sem.at[j, half]
        ).wait()

    turned[...] = adapted[...].T
    lowered_grad[...] = (gate * upstream[...].astype(FULL)).astype(LOW)
    for i in range(2):
        deep = slice(step + i * rows, step + (i + 1) * rows)
        for j in range(4):
            lift[j * rows : (j + 1) * rows, :] = pack[j, deep, :]
        weight_up = lift[...]
        weight_down = jnp.concatenate([pack[2 * i, :step, :], pack[2 * i + 1, :step, :]], axis=0)
        across = slice(2 * i * step, 2 * (i + 1) * step)
        upper = matmul(adapted[...], weight_up) + lift_bias[:, across]
        square = upper * upper
        root = math.sqrt(2.0 / math.pi)
        bent = jnp.tanh(upper * (root + root * 0.044715 * square))
        half = 0.5 + 0.5 * bent
        slope = half + upper * (0.5 - 0.5 * bent * bent) * (root + 3.0 * root * 0.044715 * square)
        active = (upper * half).astype(LOW)
        low_part = matmul(active, weight_down)
        down = lowered_grad[...]
        upper_grad = (matmul(down, weight_down, 1, 1) * slope).astype(LOW)
        grad_part = matmul(upper_grad, weight_up, 1, 1)
        if i == 0:
            lowered[...] = low_part
            adapted_grad[...] = grad_part
        else:
            lowered[...] += low_part
            adapted_grad[...] += grad_part
        liftbias_grad[:, across] = column_sum(upper_grad.astype(FULL))
        drop_part = matmul(active, down, 0, 0).astype(LOW)
        for k in range(2):
            grads[2 * i + k, :step, :] = drop_part[k * step : (k + 1) * step]
            leave(2 * i + k, 0)
        lift_part = matmul(turned[...], upper_grad).astype(LOW)
        for j in range(4):
            grads[j, deep, :] = lift_part[j * rows : (j + 1) * rows]
            leave(j, 1 + i)

    if last:
        for copy in copies:
            copy.wait()
        adapted_grad[...] += grad_got[...]
        total = lowered[...] + low_got[...] + vectors[1:2, :]
        low_got[...] = middle_got[...] + gate * total
        span = o0.shape[0]
        for d, target in enumerate((o0, o1, o2, o3)):
            target[...] = low_got[pl.ds(pl.multiple_of((me ^ d) * span, 16), span), :].astype(LOW)
        sums[0:1, :] = column_sum(upstream[...].astype(FULL) * total)
        sums[1:2, :] = column_sum(lowered_grad[...].astype(FULL))
    for j in range(4):
        for half in range(3):
            left(j, half)


def feed(me, adapted, upstream, vectors, lift_bias, pieces, before=()):
    length, width = adapted.shape
    last = len(before) > 0
    units = lift_bias.shape[1]
    wide = jax.ShapeDtypeStruct((length, width), FULL)
    low = jax.ShapeDtypeStruct((length // 4, width), LOW)
    more = jax.ShapeDtypeStruct((2, units // 2, width), LOW)
    sums = jax.ShapeDtypeStruct((8, width), FULL)
    bias = jax.ShapeDtypeStruct((1, units), FULL)
    outs = [low] * 4 + [wide, sums, bias, more, more] if last else [wide, wide, bias, more, more]
    scratch = [
        pltpu.VMEM((4, units // 2, width), LOW),
        pltpu.VMEM((4, units // 2, width), LOW),
        pltpu.VMEM((width, units // 2), LOW),
        pltpu.VMEM((width, length), LOW),
        pltpu.VMEM((length, width), LOW),
        pltpu.SemaphoreType.DMA((4, 3)),
    ]
    if last:
        scratch += [pltpu.VMEM((length, width), FULL)] * 4 + [pltpu.SemaphoreType.DMA((3,))]
    return call(
        partial(feed_kernel, last),
        "feed",
        (1,),
        [whole(a.shape) for a in (adapted, upstream, vectors, lift_bias, *pieces)]
        + [pl.BlockSpec(memory_space=pl.ANY) for _ in before],
        [whole(o.shape) for o in outs[:-2]] + [pl.BlockSpec(memory_space=pl.ANY)] * 2,
        outs,
        scratch,
        12 * length * width * units,
        (me, adapted, upstream, vectors, lift_bias, *pieces, *before),
        8 * width * units + 24 * length * width,
    )


def unmerge_kernel(
    me_ref, adapted_grad, middle, upstream, mixed, vectors, p0, p1, p2, p3, p4, p5,
    middle_grad, mixed_grad, sums, keep, send, weight, total,
):
    i = pl.program_id(0)

    @pl.when(i == 0)
    def _():
        assemble(me_ref, weight, (p0, p1, p2, p3, p4, p5), 0, 1)
        total[...] = jnp.zeros_like(total)
        sums[...] = jnp.zeros_like(sums)

    gate, gain, grow = vectors[0:1, :], vectors[1:2, :], vectors[2:3, :]
    unit, inverse = normalize(middle[...])
    grad = adapted_grad[...]
    sums[0:1, :] += column_sum(grad)
    sums[1:2, :] += column_sum(grad * (unit * gain))
    normed_grad = grad * grow
    sums[2:3, :] += column_sum(normed_grad * unit)
    mid_grad = upstream[...].astype(FULL) + unnormalize(normed_grad * gain, unit, inverse)
    middle_grad[...] = mid_grad
    low = mixed[...]
    sums[3:4, :] += column_sum(mid_grad * matmul(low, weight[...]))
    branch_grad = (gate * mid_grad).astype(LOW)
    total[...] += matmul(low, branch_grad, 0, 0)
    mixed_grad[...] = matmul(branch_grad, weight[...], 1, 1).astype(LOW)

    @pl.when(i == pl.num_programs(0) - 1)
    def _():
        split_rows(me_ref[0], total[...], keep, send)


def unmerge(me, adapted_grad, middle, upstream, mixed, vectors, pieces):
    length, width = middle.shape
    step = 512
    rows = pl.BlockSpec((step, width), lambda i, _: (i, 0))
    part = (2, width // 4, width)
    return call(
        unmerge_kernel,
        "unmerge",
        (length // step,),
        [rows] * 4 + [whole(vectors.shape)] + portion(pieces, 3 * width // 8, width // 8),
        [rows, rows, kept((8, width)), kept(part), kept(part)],
        [
            jax.ShapeDtypeStruct((length, width), FULL),
            jax.ShapeDtypeStruct((length, width), LOW),
            jax.ShapeDtypeStruct((8, width), FULL),
            jax.ShapeDtypeStruct(part, LOW),
            jax.ShapeDtypeStruct(part, LOW),
        ],
        [pltpu.VMEM((width, width), LOW), pltpu.VMEM((width, width), FULL)],
        6 * length * width * width,
        (me, adapted_grad, middle, upstream, mixed, vectors, *pieces),
        2 * length * width * 12,
    )


def unattend_kernel(step, head, sums, me_ref, query, key, value, mixed, mixed_grad, logsum, cosine, sine, *refs):
    if sums:
        grads, mine, other = refs[2:5]
        mine[...] = plus(refs[0][0], refs[1][0])
        other[...] = plus(refs[0][1], refs[1][1])
    else:
        grads = refs[0]
    query_sum, key_sum, value_sum = refs[-3:]
    lane = lax.broadcasted_iota(jnp.int32, (1, LANES), 1)
    first = lane < head
    keys, values = key[...], value[...]
    zero = jnp.zeros_like(keys)
    keys_h = (jnp.where(first, keys, zero), jnp.where(first, zero, keys))
    values_h = (jnp.where(first, values, zero), jnp.where(first, zero, values))
    turned = keys.T
    scale = 1.0 / math.sqrt(head)
    for i in range(query.shape[0] // step):
        at = slice(i * step, (i + 1) * step)
        block, grad = query[at, :], mixed_grad[at, :]
        product = (grad.astype(FULL) * mixed[at, :].astype(FULL)).T
        queries, values_new, keys_new = [], [], []
        for h in range(2):
            center = jnp.sum(product[h * head : (h + 1) * head], axis=0, keepdims=True)
            probs = jnp.exp(matmul(keys_h[h], block, 1, 1) - logsum[0, h : h + 1, at])
            probs_grad = matmul(values_h[h], grad, 1, 1)
            scores_grad = (probs * (probs_grad - center)).astype(LOW)
            values_new.append(matmul(probs.astype(LOW), grad))
            keys_new.append(matmul(scores_grad, block))
            queries.append(matmul(turned[h * head : (h + 1) * head], scores_grad))
        query_sum[at, :] = jnp.concatenate(queries, axis=0).T * scale
        key_part = jnp.where(first, keys_new[0], keys_new[1])
        value_part = jnp.where(first, values_new[0], values_new[1])
        if i == 0:
            key_sum[...] = key_part
            value_sum[...] = value_part
        else:
            key_sum[...] += key_part
            value_sum[...] += value_part
    under = lower_half(head)
    cos, sin = cosine[...], sine[...]
    for which, total in enumerate((query_sum, key_sum)):
        rotated = total[...]
        swept = rotated * sin
        back = jnp.where(
            under, pltpu.roll(swept, LANES - head // 2, 1), -pltpu.roll(swept, head // 2, 1)
        )
        grads[which] = (rotated * cos + back).astype(LOW)
    grads[2] = value_sum[...].astype(LOW)


def unattend(
    me, query, key, value, mixed, mixed_grad, logsum, cosine, sine, head, start, pairs, sums=()
):
    length = mixed.shape[0]
    width = pairs * LANES
    more, outs, specs = [], [], []
    if sums:
        _, rows, columns = sums[0].shape
        part = rows // pairs
        more = [pl.BlockSpec((2, part, columns), lambda i, _: (0, i, 0))] * 2
        outs = [jax.ShapeDtypeStruct((rows, columns), LOW)] * 2
        specs = [pl.BlockSpec((part, columns), lambda i, _: (i, 0))] * 2
    block = pl.BlockSpec((length, LANES), lambda i, _: (0, i + start))
    own = pl.BlockSpec((length, LANES), lambda i, _: (0, i))
    return call(
        partial(unattend_kernel, 256, head, len(sums)),
        "unattend",
        (pairs,),
        [block] * 5
        + [pl.BlockSpec((1, 2, length), lambda i, _: (i + start, 0, 0))]
        + [whole((length, LANES))] * 2
        + more,
        [pl.BlockSpec((3, length, LANES), lambda i, _: (0, 0, i))] + specs,
        [jax.ShapeDtypeStruct((3, length, width), LOW)] + outs,
        [pltpu.VMEM((length, LANES), FULL)] * 3,
        40 * length * length * width,
        (me, query, key, value, mixed, mixed_grad, logsum, cosine, sine, *sums),
        2 * length * width * 8,
    )


def weigh_kernel(riders, sums, me_ref, turned, grads, *refs):
    ins, outs = refs[: riders + sums], refs[riders + sums :]
    keep, send = outs[:2]
    outs = outs[2:]
    if sums:
        mine, other = outs[:2]
        outs = outs[2:]
    found, sem = outs[:2]
    outs = outs[2:]
    me = me_ref[0]
    rows, wide = found.shape[1:]
    step = grads.shape[2]
    moves = []
    if riders:
        for k, (source, target) in enumerate(((ins[0], keep), (ins[1], send))):
            at = target.at[:, :, wide : wide + source.shape[2]]
            moves.append(pltpu.make_async_copy(source, at, sem.at[4 + k, 0]))
    if sums:
        for k in range(2):
            moves.append(pltpu.make_async_copy(ins[riders + k], outs[k], sem.at[4 + k, 1]))
    for move in moves:
        move.start()
    for which in range(3):
        cut = slice(which * step, (which + 1) * step)
        value = matmul(turned[...], grads[which]).astype(LOW)
        for j in range(4):
            found[j, :, cut] = value[j * rows : (j + 1) * rows]
            where = (j >> 1) ^ (me >> 1)
            for target, odd in ((keep, 0), (send, 1)):

                @pl.when(((me ^ j) & 1) == odd)
                def _(target=target, j=j, cut=cut, which=which, where=where):
                    pltpu.make_async_copy(
                        found.at[j, :, cut], target.at[where, :, cut], sem.at[j, which]
                    ).start()

    for move in moves:
        move.wait()
    if sums:
        mine[...] = plus(outs[0][0], outs[1][0])
        other[...] = plus(outs[0][1], outs[1][1])
    for j in range(4):
        for which in range(3):
            cut = slice(which * step, (which + 1) * step)
            pltpu.make_async_copy(
                found.at[j, :, cut], keep.at[0, :, cut], sem.at[j, which]
            ).wait()


def weigh(me, turned, grads, riders=(), sums=()):
    width, length = turned.shape
    step = grads.shape[2]
    more = riders[0].shape[2] if riders else 0
    shape = jax.ShapeDtypeStruct((2, width // 4, 3 * step + more), LOW)
    outs, scratch = [shape, shape], []
    away = pl.BlockSpec(memory_space=pl.ANY)
    specs = [away, away]
    if sums:
        out = jax.ShapeDtypeStruct(sums[0].shape[1:], LOW)
        outs += [out, out]
        specs += [whole(out.shape)] * 2
        scratch = [pltpu.VMEM(sums[0].shape, LOW)] * 2
    return call(
        partial(weigh_kernel, len(riders), len(sums)),
        "weigh",
        (1,),
        [whole(a.shape) for a in (turned, grads, *riders)] + [away] * len(sums),
        specs,
        outs,
        [pltpu.VMEM((4, width // 4, 3 * step), LOW), pltpu.SemaphoreType.DMA((6, 3))] + scratch,
        6 * length * width * step,
        (me, turned, grads, *riders, *sums),
        2 * length * width * 7,
    )


def unproject_kernel(me_ref, g0, g1, hidden, middle_grad, vectors, p0, p1, p2, p3, p4, p5, o0, o1, o2, o3, sums, weight):
    i = pl.program_id(0)

    @pl.when(i == 0)
    def _():
        assemble(me_ref, weight, (p0, p1, p2, p3, p4, p5), 0, 3)
        sums[...] = jnp.zeros_like(sums)

    gain, grow = vectors[0:1, :], vectors[1:2, :]
    width = hidden.shape[1]
    grad, at = None, 0
    for part in (g0, g1):
        size = part.shape[2]
        for which in range(3):
            low = which * width + at
            term = matmul(part[which], weight[:, low : low + size], 1, 1)
            grad = term if grad is None else grad + term
        at += size
    unit, inverse = normalize(hidden[...].astype(FULL))
    sums[0:1, :] += column_sum(grad)
    sums[1:2, :] += column_sum(grad * (unit * gain))
    normed_grad = grad * grow
    sums[2:3, :] += column_sum(normed_grad * unit)
    low = (middle_grad[...] + unnormalize(normed_grad * gain, unit, inverse)).astype(LOW)
    for d, target in enumerate((o0, o1, o2, o3)):

        @pl.when(i == me_ref[0] ^ d)
        def _(target=target):
            target[...] = low


def unproject(me, grads, hidden, middle_grad, vectors, pieces):
    length, width = hidden.shape
    step = length // 4
    rows = pl.BlockSpec((step, width), lambda i, _: (i, 0))
    return call(
        unproject_kernel,
        "unproject",
        (length // step,),
        [pl.BlockSpec((3, step, g.shape[2]), lambda i, _: (0, i, 0)) for g in grads]
        + [rows, rows, whole(vectors.shape)]
        + portion(pieces, 0, 3 * width // 8),
        [kept((step, width))] * 4 + [kept((8, width))],
        [jax.ShapeDtypeStruct((step, width), LOW)] * 4 + [jax.ShapeDtypeStruct((8, width), FULL)],
        [pltpu.VMEM((width, 3 * width), LOW)],
        6 * length * width * width,
        (me, *grads, hidden, middle_grad, vectors, *pieces),
        2 * length * width * 10,
    )


def lay_kernel(me_ref, *refs):
    for d, part in enumerate(refs[:-1]):
        refs[-1][pl.ds(me_ref[0] ^ d, 1)] = part[...][None]


def lay(me, parts):
    shape = (len(parts),) + parts[0].shape
    return call(
        lay_kernel, "lay", (1,), [whole(p.shape) for p in parts], [whole(shape)],
        [jax.ShapeDtypeStruct(shape, LOW)], [], 1024, (me, *parts), 1024,
    )[0]


def finish_kernel(
    seqs, columns, depth, me_ref, parts, others, heads, merges, modulate, modulate_bias, up, down, one, two, table
):
    half, rows = parts.shape[0], parts.shape[1] - 8
    size = 2 * half
    wide = parts.shape[2] // 2
    width = merges.shape[1]
    part = width // 2
    for p in range(size):
        at = slice(p * rows, (p + 1) * rows)
        value = jnp.where(
            me_ref[1] == p // half, parts[p % half, 8:, :], others[p % half, 8:, :]
        ).astype(FULL)
        for k in range(3):
            heads[at, k * width : k * width + part] = value[:, k * part : (k + 1) * part]
            heads[at, k * width + part : (k + 1) * width] = value[:, (5 + k) * part : (6 + k) * part]
        merges[at, :] = value[:, 3 * part : 5 * part]
    small = jnp.concatenate(
        [
            source[p, :8, :wide].astype(FULL) + source[p, :8, wide:].astype(FULL)
            for source in (parts, others)
            for p in range(half)
        ],
        axis=0,
    )
    row = lax.broadcasted_iota(jnp.int32, (8 * size, 1), 0) & 7
    mine = row < seqs
    zero = jnp.zeros((), FULL)
    grads = jnp.where(mine, small[:, :columns], zero)
    conds = jnp.where(mine, small[:, columns : columns + depth], zero)
    conds_grad = jnp.where(mine, small[:, columns + depth : columns + 2 * depth], zero)
    steps = small[:, columns + 2 * depth : columns + 2 * depth + 1].astype(jnp.int32)

    def exact(left, right):
        dims = (((0,), (0,)), ((), ()))
        return lax.dot_general(
            left, right, dims, precision=lax.Precision.HIGHEST, preferred_element_type=FULL
        )

    modulate[...] = exact(grads, conds)
    modulate_bias[...] = column_sum(grads)[0]
    ends = column_sum(jnp.where(row == seqs, small, zero))
    at = 0
    for target in (up, down, one, two):
        size = target.shape[0]
        target[...] = ends[0, at : at + size]
        at += size
    share = table.shape[0]
    own = me_ref[0] * share + lax.broadcasted_iota(jnp.int32, (1, share), 1)
    table[...] = exact(jnp.where(mine & (steps == own), 1.0, 0.0), conds_grad)


def finish(me, parts, others, width, columns, depth, sizes, share):
    shapes = [(width // 4, 3 * width), (width // 4, width), (columns, depth), (columns,)]
    shapes += [(size,) for size in sizes] + [(share, depth)]
    return call(
        partial(finish_kernel, 4, columns, depth), "finish", (1,), [whole(parts.shape)] * 2,
        [whole(s) for s in shapes], [jax.ShapeDtypeStruct(s, FULL) for s in shapes], [], 1024,
        (me, parts, others), 1024,
    )


def swap(array, axis, distance):
    size = lax.axis_size(axis)
    return lax.ppermute(array, axis, [(i, i ^ distance) for i in range(size)])


def fence(*trees):
    return lax.optimization_barrier(trees)


def bit(axis, distance):
    return (lax.axis_index(axis) // distance) % 2


def choose(parts, at):
    return lax.dynamic_index_in_dim(parts, at, 0, keepdims=False)


def choose_all(array, place):
    count = array.shape[0]
    return jnp.stack([choose(array, place ^ k) for k in range(count)])


def payload(parts):
    return jnp.concatenate([p.reshape(2, p.shape[0] // 2, p.shape[1]) for p in parts], axis=1)


def blocks_of(weight, width):
    return [weight[:, k : k + width] for k in range(0, weight.shape[1], width)]


def powers(size):
    return [1 << k for k in range(size.bit_length() - 1)]


def plus(*terms):
    total = terms[0].astype(FULL)
    for term in terms[1:]:
        total = total + term.astype(FULL)
    return total.astype(LOW)


def other_kernel(at_ref, kept_term, got, other):
    other[...] = plus(kept_term[0], got[0])


def sum_other(kept_term, got):
    _, rows, columns = kept_term.shape
    steps = 4 if rows % 256 == 0 else 2
    part = rows // steps
    two = pl.BlockSpec((1, part, columns), lambda i, _: (1, i, 0))
    return call(
        other_kernel, "other", (steps,), [two, two], [pl.BlockSpec((part, columns), lambda i, _: (i, 0))],
        [jax.ShapeDtypeStruct((rows, columns), LOW)], [], 1024,
        (jnp.zeros((1,), jnp.int32), kept_term, got), 1024,
    )[0]


def three_kernel(at_ref, kept_term, got, last, total):
    total[...] = plus(kept_term[0], got[0], last[...])


def sum_three(kept_term, got, last):
    _, rows, columns = kept_term.shape
    part = rows // 2
    two = pl.BlockSpec((1, part, columns), lambda i, _: (0, i, 0))
    one = pl.BlockSpec((part, columns), lambda i, _: (i, 0))
    return call(
        three_kernel, "two", (2,), [two, two, one], [one],
        [jax.ShapeDtypeStruct((rows, columns), LOW)], [], 1 << 33,
        (jnp.zeros((1,), jnp.int32), kept_term, got, last), 1 << 24,
    )[0]


def two_kernel(at_ref, first, second, total):
    total[...] = plus(first[...], second[...])


def sum_two(first, second):
    rows, columns = first.shape
    steps = 2 if rows % 32 == 0 else 1
    spec = pl.BlockSpec((rows // steps, columns), lambda i, _: (i, 0))
    return call(
        two_kernel, "two", (steps,), [spec] * 2, [spec],
        [jax.ShapeDtypeStruct((rows, columns), LOW)], [], 1 << 33,
        (jnp.zeros((1,), jnp.int32), first, second), 1 << 24,
    )[0]


def beside_kernel(at_ref, a, b, c, d, e, mine, other):
    cut = a.shape[2]
    for target, at in ((mine, at_ref[0]), (other, 1 - at_ref[0])):
        at = pl.ds(at, 1)
        target[:, :cut] = plus(a[at], b[at])[0]
        target[:, cut:] = plus(c[0, at], d[0, at], e[at])[0]


def split_beside(first, second):
    args = [a.reshape(a.shape[:-2] + (2, -1, a.shape[-1])) for a in (*first, *second)]
    rows = args[0].shape[1]
    out = (rows, args[0].shape[2] + args[4].shape[2])
    pair = pl.BlockSpec((1,) + args[2].shape[1:], lambda *_: (0, 0, 0, 0), pipeline_mode=pl.Buffered(1))
    return call(
        beside_kernel, "beside", (1,),
        [whole(args[0].shape), whole(args[1].shape), pair, pair, whole(args[4].shape)], [whole(out)] * 2,
        [jax.ShapeDtypeStruct(out, LOW)] * 2, [], 1024, (place_of(1), *args), 1024,
    )


def terms_kernel(at_ref, small, parts, total):
    value = plus(*[parts[k] for k in range(parts.shape[0])])
    for k in range(total.shape[0]):
        total[k, :8, :] = small[...]
        total[k, 8:, :] = value


def gather_terms(small, parts):
    shape = (parts.shape[0], 8 + parts.shape[1], small.shape[1])
    return call(
        terms_kernel, "terms", (1,), [whole(small.shape), whole(parts.shape)], [whole(shape)],
        [jax.ShapeDtypeStruct(shape, LOW)], [], 1024, (jnp.zeros((1,), jnp.int32), small, parts), 1024,
    )[0]


def exchange(parts):
    size = lax.axis_size("dp")
    groups = None
    if parts.shape[0] < size:
        groups = [list(range(b, size, 2)) for b in range(2)]
    return lax.all_to_all(parts, "dp", 0, 0, axis_index_groups=groups, tiled=True)


def deal(term, size=None):
    size = size or lax.axis_size("dp")
    rows, columns = term.shape
    return exchange(term.reshape(size, rows // size, columns))


def add_kernel(at_ref, parts, total):
    total[...] = plus(*[parts[k] for k in range(parts.shape[0])])


def add_up(parts):
    shape = parts.shape[1:]
    return call(
        add_kernel, "add", (1,), [whole(parts.shape)], [whole(shape)],
        [jax.ShapeDtypeStruct(shape, LOW)], [], 1 << 33, (jnp.zeros((1,), jnp.int32), parts), 1 << 24,
    )[0]


def place_of(distance):
    return bit("dp", distance).astype(jnp.int32).reshape(1)


def join_kernel(at_ref, first, second, both):
    b = at_ref[0]
    both[pl.ds(b, 1)] = first[...][None]
    both[pl.ds(1 - b, 1)] = second[...][None]


def join(first, second, distance):
    rows, columns = first.shape
    shape = (2, rows, columns)
    return call(
        join_kernel, "join", (1,), [whole(first.shape)] * 2, [whole(shape)],
        [jax.ShapeDtypeStruct(shape, LOW)], [], 1024, (place_of(distance), first, second), 1024,
    )[0].reshape(2 * rows, columns)


def settle_kernel(plan, size, at_ref, *refs):
    count = len(plan)
    outs = refs[2 * count :]
    depth = size.bit_length() - 1
    b = at_ref[0]
    for p, moves in enumerate(plan):
        rows = 2 * refs[2 * p].shape[0] // size
        for h in range(2):
            value = jnp.where(b == h, refs[2 * p][...], refs[2 * p + 1][...]).astype(FULL)
            for k in range(h, size, 2):
                at = sum(((k >> j) & 1) << (depth - 1 - j) for j in range(1, depth)) * rows
                for top, left, down, wide, out, to_row, to_column in moves:
                    low, high = max(top, k * rows), min(top + down, (k + 1) * rows)
                    if low < high:
                        start = to_row + low - top
                        source = at + low - k * rows
                        outs[out][start : start + high - low, to_column : to_column + wide] = value[
                            source : source + high - low, left : left + wide
                        ]


def settle(pairs, plan, shapes):
    args = [array for pair in pairs for array in pair]
    return call(
        partial(settle_kernel, plan, lax.axis_size("dp")),
        "settle",
        (1,),
        [whole(a.shape) for a in args],
        [whole(shape) for shape in shapes],
        [jax.ShapeDtypeStruct(shape, FULL) for shape in shapes],
        [],
        1024,
        (place_of(1), *args),
        1024,
    )


def shards(
    hidden_in,
    time_table,
    time_step,
    token_pos,
    heads_weight,
    merge_weight,
    lift_weight,
    lift_bias,
    drop_weight,
    drop_bias,
    modulate_weight,
    modulate_bias,
    first_gain,
    second_gain,
    out_grad,
):
    count = lax.axis_size("seq")
    place = lax.axis_index("seq")
    seqs, span, width = hidden_in.shape
    assert count == 4 and seqs == count
    length = span * count
    head = width // HEADS
    bits = powers(lax.axis_size("dp"))
    row_half = bit("dp", 1)
    me = jnp.stack([place, row_half]).astype(jnp.int32)

    units = drop_weight.shape[0]
    step = units // 2
    heads_pack = payload(blocks_of(heads_weight, width) + [merge_weight])
    heads_half = choose(heads_pack, row_half)
    heads_half, time_step = fence(heads_half, time_step)
    heads_across = swap(heads_half, "seq", 2)

    def feed_pack(h):
        columns = [lift_weight[:, j * units + h * step : j * units + (h + 1) * step] for j in range(4)]
        blocks = [jnp.concatenate(columns[k : k + 2], axis=1) for k in (0, 2)]
        return jnp.concatenate([drop_weight[h * step : (h + 1) * step]] + blocks, axis=0)

    table_rows, depth = time_table.shape
    chosen_rows = (time_step[:, None] == jnp.arange(table_rows, dtype=jnp.int32)[None, :]).astype(LOW)
    conds = jnp.dot(chosen_rows, time_table, preferred_element_type=FULL)
    modulation = matmul(conds.astype(LOW), modulate_weight, 1, 1) + modulate_bias.astype(FULL)
    columns = modulation.shape[1]
    vectors = [v.astype(FULL) for v in (lift_bias, drop_bias, first_gain, second_gain)]
    above = jnp.concatenate([modulation, token_pos.astype(FULL)], axis=1)
    below = jnp.concatenate(vectors)[None]
    below = jnp.pad(below, ((0, 0), (0, above.shape[1] - below.shape[1])))
    small = jnp.concatenate([above, below], axis=0)
    small_across = swap(small, "seq", 2)
    hidden_in, small = fence(hidden_in, small)
    heads_across, small, lift_weight, drop_weight = fence(
        heads_across, small, lift_weight, drop_weight
    )
    heads_handed = swap(heads_across, "dp", 1)
    heads_core = swap(heads_pack, "seq", 1), swap(heads_across, "seq", 1)
    hidden = lax.all_to_all(hidden_in, "seq", 0, 0, tiled=True).reshape(length, width)
    small = jnp.stack([small, small_across])
    small_core = swap(small, "seq", 1)
    small = jnp.stack([small[0], small_core[0], small[1], small_core[1]])
    small = choose_all(small, place)
    mine = lax.dynamic_index_in_dim(small, place, 1, keepdims=False)
    chosen = mine[:, :columns].reshape(6, width)
    positions = mine[:, columns:].reshape(length)
    rest = small[:, seqs]
    sizes = (lift_bias.shape[0], drop_bias.shape[0], first_gain.shape[0], second_gain.shape[0])
    vectors, at = [], 0
    for size in sizes:
        vectors.append(rest[:, at : at + size].reshape(1, -1))
        at += size
    up_bias, down_bias, gain_one, gain_two = vectors
    shift_a, scale_a, gate_a, shift_b, scale_b, gate_b = [chosen[k : k + 1] for k in range(6)]
    grow_a, grow_b = 1.0 + scale_a, 1.0 + scale_b

    def rows(*items):
        blank = jnp.zeros((8 - len(items), width), FULL)
        return jnp.concatenate(items + (blank,), axis=0)

    freqs = 10000.0 ** (-jnp.arange(0, head, 2, dtype=FULL) / head)
    freqs = jnp.tile(freqs, 2 * LANES // head)
    angles = positions[:, None] * freqs
    cosine, sine = jnp.cos(angles), jnp.sin(angles)

    pack_0, pack_1 = feed_pack(0), feed_pack(1)
    project_vectors = rows(gain_one, grow_a, shift_a)
    heads_handed, project_vectors, cosine, sine, pack_0, pack_1, me = fence(
        heads_handed, project_vectors, cosine, sine, pack_0, pack_1, me
    )
    heads = (
        heads_pack,
        heads_core[0],
        heads_across,
        heads_handed,
        heads_core[1],
        swap(heads_handed, "seq", 1),
    )
    hidden, heads, cosine, sine, pack_0, pack_1, out_grad = fence(
        hidden, heads, cosine, sine, pack_0, pack_1, out_grad
    )
    across_0 = swap(pack_0, "seq", 2)
    core_0, core_1 = swap(pack_0, "seq", 1), swap(pack_1, "seq", 1)
    adapted_a, query, key, value = project(
        me, hidden, project_vectors, heads, cosine, sine, head
    )
    merge_vectors, unmerge_vectors = rows(gate_a, gain_two, grow_b, shift_b), rows(gate_a, gain_two, grow_b)
    feed_vectors = rows(gate_b, down_bias)
    bias_0, bias_1 = [up_bias.reshape(4, 2, step)[:, h].reshape(1, 4 * step) for h in range(2)]
    query, merge_vectors, unmerge_vectors, feed_vectors, bias_0, bias_1 = fence(
        query, merge_vectors, unmerge_vectors, feed_vectors, bias_0, bias_1
    )
    query, out_grad = fence(query, out_grad)
    upstream = lax.all_to_all(out_grad, "seq", 0, 0, tiled=True).reshape(length, width)
    mixed, logsum = attend(me, query, key, value, head)
    mixed, logsum, across_0 = fence(mixed, logsum, across_0)
    mixed, pack_1 = fence(mixed, pack_1)
    other_0 = swap(across_0, "seq", 1)
    across_1 = swap(pack_1, "seq", 2)
    middle, adapted_b = merge(me, mixed, hidden, merge_vectors, heads)
    middle, adapted_b, core_0, other_0, upstream = fence(
        middle, adapted_b, core_0, other_0, upstream
    )
    pairs = width // LANES // 2
    adapted_b, upstream, core_1 = fence(adapted_b, upstream, core_1)
    lowered, grad, liftbias_0, keep_0, send_0 = feed(
        me, adapted_b, upstream, feed_vectors, bias_0, (pack_0, core_0, across_0, other_0)
    )
    lowered, grad, liftbias_0, keep_0, send_0, across_1 = fence(
        lowered, grad, liftbias_0, keep_0, send_0, across_1
    )
    other_1 = swap(across_1, "seq", 1)
    got_0 = swap(send_0, "seq", 1)
    *out_parts, adapted_b_grad, feed_sums, liftbias_1, keep_1, send_1 = feed(
        me, adapted_b, upstream, feed_vectors, bias_1, (pack_1, core_1, across_1, other_1),
        (lowered, grad, middle),
    )
    back = bits[::-1]
    last = len(back) - 1
    out_parts, adapted_b_grad, feed_sums, liftbias_1, keep_1, send_1, got_0 = fence(
        out_parts, adapted_b_grad, feed_sums, liftbias_1, keep_1, send_1, got_0
    )
    got_1 = swap(send_1, "seq", 1)
    core_0 = got_0
    adapted_b_grad, other_0 = fence(adapted_b_grad, sum_other(keep_0, core_0))
    got_0 = swap(other_0, "seq", 2)
    middle_grad, mixed_grad, merge_sums, merge_keep, merge_send = unmerge(
        me, adapted_b_grad, middle, upstream, mixed, unmerge_vectors, heads
    )
    middle_grad, mixed_grad, merge_sums, merge_keep, merge_send, got_1 = fence(
        middle_grad, mixed_grad, merge_sums, merge_keep, merge_send, got_1
    )
    heads_0, mine_1, other_1 = unattend(
        me, query, key, value, mixed, mixed_grad, logsum, cosine, sine, head, 0, pairs, (keep_1, got_1)
    )
    heads_0, mine_1, other_1, got_0 = fence(heads_0, mine_1, other_1, got_0)
    got_1 = swap(other_1, "seq", 2)
    heads_0, term_0 = fence(heads_0, sum_three(keep_0, core_0, got_0))
    parts_0 = deal(term_0)
    keep_2, send_2 = weigh(me, adapted_a, heads_0, (merge_keep, merge_send))
    mixed_grad, keep_2, send_2 = fence(mixed_grad, keep_2, send_2)
    got_2 = swap(send_2, "seq", 1)
    (heads_1,) = unattend(
        me, query, key, value, mixed, mixed_grad, logsum, cosine, sine, head, pairs, pairs
    )
    heads_1, got_1 = fence(heads_1, got_1)
    heads_1, term_1, parts_0 = fence(heads_1, sum_two(mine_1, got_1), parts_0)
    parts_1 = deal(term_1)
    heads_1, got_2 = fence(heads_1, got_2)
    keep_3, send_3, mine_2, other_2 = weigh(me, adapted_a, heads_1, (), (keep_2, got_2))
    keep_3, send_3, mine_2, other_2, parts_0 = fence(keep_3, send_3, mine_2, other_2, parts_0)
    got_3 = swap(send_3, "seq", 1)
    got_2 = swap(other_2, "seq", 2)
    term_0, core_3 = fence(add_up(parts_0), got_3)
    heads_1, term_0, other_3 = fence(heads_1, term_0, sum_other(keep_3, core_3))
    got_3 = swap(other_3, "seq", 2)
    got_0 = swap(term_0, "dp", back[0])
    *input_parts, project_sums = unproject(
        me, (heads_0, heads_1), hidden, middle_grad, rows(gain_one, grow_a), heads
    )
    input_parts, project_sums, got_0 = fence(input_parts, project_sums, got_0)
    input_parts, project_sums, term_0 = fence(
        input_parts, project_sums, join(term_0, got_0, back[0])
    )
    got_0 = swap(term_0, "dp", back[1])
    input_parts, project_sums, got_2, got_3, parts_1 = fence(
        input_parts, project_sums, got_2, got_3, parts_1
    )
    (mine_a, other_a), input_parts, project_sums, parts_1 = fence(
        split_beside((mine_2, got_2), (keep_3, core_3, got_3)), input_parts, project_sums, parts_1
    )
    got_a = swap(other_a, "dp", 1)
    liftbias_grad = jnp.stack([liftbias_0.reshape(4, step), liftbias_1.reshape(4, step)], axis=1)
    modulation_grad = jnp.concatenate(
        [project_sums[0:2], merge_sums[3:4], merge_sums[0:2], feed_sums[0:1]], axis=0
    ).reshape(count, columns)
    small = jnp.concatenate(
        [
            modulation_grad,
            liftbias_grad.reshape(count, -1),
            feed_sums[1].reshape(count, -1),
            project_sums[2].reshape(count, -1),
            merge_sums[2].reshape(count, -1),
        ],
        axis=1,
    )
    parts = [choose(small, place ^ d) for d in range(4)]
    term_1, parts = fence(add_up(parts_1), parts)
    got_1 = swap(term_1, "dp", back[0])
    parts = [swap(part, "seq", d) if d else part for d, part in enumerate(parts)]
    term_0, input_parts, parts = fence(join(term_0, got_0, back[1]), input_parts, parts)
    for k in range(2, last):
        term_0 = join(term_0, swap(term_0, "dp", back[k]), back[k])
    input_parts = [swap(part, "seq", d) if d else part for d, part in enumerate(input_parts)]
    mine_a, got_a = fence(mine_a, got_a)
    mine_a, got_a, got_1, parts, term_0 = fence(mine_a, got_a, got_1, parts, term_0)
    term_a, got_1, parts, out_parts, term_0 = fence(
        sum_two(mine_a, got_a), got_1, parts, out_parts, term_0
    )
    parts_a = deal(term_a, lax.axis_size("dp") // 2)
    got_0 = swap(term_0, "dp", back[-1])
    term_1 = join(term_1, got_1, back[0])
    got_1 = swap(term_1, "dp", back[1])
    out_parts = [swap(part, "seq", d) if d else part for d, part in enumerate(out_parts)]
    small = choose_all(jnp.stack(parts), place)
    exact = lax.Precision.HIGHEST
    conds_grad = jnp.einsum(
        "sm,mc->sc", small[:, :columns], modulate_weight.astype(FULL), precision=exact
    )
    conds_grad = sum([swap(conds_grad, "seq", d) for d in (1, 2, 3)], conds_grad)
    spare = term_a.shape[1] // 2 - columns - 2 * depth
    above = jnp.concatenate(
        [
            small[:, :columns],
            conds,
            conds_grad,
            jnp.broadcast_to(time_step.astype(FULL)[:, None], (seqs, spare)),
        ],
        axis=1,
    )
    below = jnp.sum(small[:, columns:], axis=0)[None]
    below = jnp.pad(below, ((0, 7 - seqs), (0, above.shape[1] - below.shape[1])))
    small = jnp.concatenate([above, below], axis=0)
    upper = lax.reduce_precision(small, 8, 7)
    small = jnp.concatenate([upper, small - upper], axis=1).astype(LOW)
    small, parts_a = fence(small, parts_a)
    small, parts_a, got_0 = fence(small, parts_a, got_0)
    small, parts_a, got_1, input_parts = fence(small, parts_a, got_1, input_parts)
    term_a, got_1, input_parts = fence(gather_terms(small, parts_a), got_1, input_parts)
    parts_a = exchange(term_a)
    term_1 = join(term_1, got_1, back[1])
    for k in range(2, last):
        term_1 = join(term_1, swap(term_1, "dp", back[k]), back[k])
    got_1 = swap(term_1, "dp", back[-1])
    input_grad = lay(me, input_parts)
    parts_a, got_1, input_grad = fence(parts_a, got_1, input_grad)
    got_a = swap(parts_a, "dp", 1)
    block_out = lay(me, out_parts)
    pair_0, pair_1 = (term_0, got_0), (term_1, got_1)
    deep = width // 4
    drop_grad, lift_grad = settle(
        [pair_0, pair_1],
        [
            [(0, 0, step, width, 0, h * step, 0)]
            + [
                (step + (j >> 1) * deep, (j & 1) * step, deep, step, 1, 0, j * units + h * step)
                for j in range(4)
            ]
            for h in range(2)
        ],
        [drop_weight.shape, lift_weight.shape],
    )
    block_out, input_grad, drop_grad, lift_grad, parts_a, got_a = fence(
        block_out, input_grad, drop_grad, lift_grad, parts_a, got_a
    )
    share = table_rows // count
    (
        heads_grad, merge_grad, modulate_grad, modulatebias_grad,
        liftbias_out, dropbias_out, firstgain_out, secondgain_out, table_grad,
    ) = finish(me, parts_a, got_a, width, columns, depth, sizes, share)
    return (
        block_out,
        input_grad,
        heads_grad,
        merge_grad,
        lift_grad,
        liftbias_out,
        drop_grad,
        dropbias_out,
        modulate_grad,
        modulatebias_grad,
        firstgain_out,
        secondgain_out,
        table_grad,
    )


def solution(mesh):
    return jax.shard_map(
        shards,
        mesh=mesh,
        in_specs=(
            P("dp", "seq", None),
            P(),
            P("dp"),
            P("dp", "seq"),
            P("seq", None),
            P("seq", None),
            P("seq", None),
            P("seq"),
            P("seq", None),
            P("seq"),
            P("seq", None),
            P("seq"),
            P("seq"),
            P("seq"),
            P("dp", "seq", None),
        ),
        out_specs=(
            P("dp", "seq", None),
            P("dp", "seq", None),
            P("seq", None),
            P("seq", None),
            P("seq", None),
            P("seq"),
            P("seq", None),
            P("seq"),
            P("seq", None),
            P("seq"),
            P("seq"),
            P("seq"),
            P("seq", None),
        ),
        check_vma=False,
    )
```
